32 devices in a mesh: facet: 16 (over z, x, core), chan: 2 (over y).
Axes of the slice: x: 2, y: 2, z: 4, core: 2. Of those that a mesh axis runs over, the one named last changes fastest.
Arguments:
- x_start: float32 [256, 256, 128], P('chan', 'facet'), may hold values from 0 to 2
- dirty: float32 [256, 256, 128], P('chan', 'facet'), may hold values from -6 to 6
- weights: float32 [8, 256, 128], P(None, 'facet'), may hold values from 1 to 16
- filters: float32 [8, 16], replicated, may hold values from -1.5 to 1.5
- basis: float32 [16, 256, 32], P('facet', 'chan'), may hold values from -1 to 1
- bounds: float32 [32], replicated, may hold values from 0.1 to 3
- margin_rows: int32 [16], replicated, may hold values from 1 to 15, as said below
Outputs:
- image: float32 [256, 256, 128], P('chan', 'facet')
- wavelet_dual: float32 [8, 256, 256, 128], P(None, 'chan', 'facet')
- spectral_dual: float32 [256, 256, 128], P('chan', 'facet')
The draws below stay inside these ranges and needn't reach their ends.
Inputs may be any that keep to these rules, and one draw needn't show every extreme that they name: `margin_rows`: each facet borrows 1 to 15 rows; some facet after the first borrows 15.
All inputs are finite; a program needn't handle non-finite values.
Results may differ from the reference program's by a relative error of at most 0.0001.
Values sent between devices are 32-bit elements; how exact they have to be, the bound alone decides.
No kernel may reach another device: no remote copies, remote signals or barrier semaphores. Data moves between devices by JAX's collectives and lax.ppermute only.
A program may use at most 128 MiB of HBM per device.

```python
import math
import jax
import jax.numpy as jnp
from jax import lax

NB = 8
CH = 256
RANK = 32
FR = 16
FC = 128
ITERS = 2
MAXB = 15
FACETS = 16
ROWS = 256


def draw_margin_rows(key, part):
    first_key, second_key = jax.random.split(jax.random.fold_in(key, 17))
    values = jax.random.randint(first_key, (FACETS,), 1, MAXB + 1)
    chosen = jax.random.randint(second_key, (), 1, FACETS)
    return jnp.where(jnp.arange(FACETS) == chosen, MAXB, values).astype(jnp.int32)


def level_of(stream_key, shape, cuts, low, high):
    factor_of, own = 1.0, jax.random.fold_in(stream_key, 6)
    for position, shards_of in cuts:
        draws = jnp.exp(jax.random.uniform(jax.random.fold_in(own, position), (shards_of,), jnp.float32, low / len(cuts), high / len(cuts)))
        factor_of = factor_of * jnp.repeat(draws, shape[position] // shards_of).reshape([-1 if axis == position else 1 for axis in range(len(shape))])
    return factor_of


def centred(key, extent, deviation, limit, cuts=(), kind=jnp.bfloat16):
    loudness = level_of(key, extent, cuts, -0.22, 0.18) if cuts else 1.0
    result = jax.random.normal(key, extent, jnp.float32) * deviation * loudness
    return jnp.minimum(jnp.maximum(result, -limit), limit).astype(kind)


def setup_inputs(seed: int = 0) -> dict:
    keys = jax.random.split(jax.random.key(seed), 8)
    return {
        "x_start": jnp.clip(2.0 * jax.random.uniform(keys[0], (CH, ROWS, FC), jnp.float32) ** level_of(keys[0], (CH, ROWS, FC), ((0, 2), (1, 16)), -0.2, 0.2), 0.0, 2.0),
        "dirty": centred(keys[1], (CH, ROWS, FC), 1.0, 6.0, ((0, 2), (1, 16)), jnp.float32),
        "weights": jnp.clip(jnp.exp(math.log(16.0) - 2.7725887 * jax.random.uniform(keys[2], (NB, ROWS, FC), jnp.float32) ** level_of(keys[2], (NB, ROWS, FC), ((1, 16),), -0.2, 0.2)), 1.0, 16.0),
        "filters": centred(keys[3], (NB, 2 * NB), (2 * NB) ** -0.5, 1.5, (), jnp.float32),
        "basis": centred(keys[4], (FACETS, CH, RANK), RANK ** -0.5, 1.0, ((0, 16), (1, 2)), jnp.float32),
        "bounds": jnp.clip(jnp.exp(jax.random.uniform(keys[5], (RANK,), jnp.float32, math.log(0.1), math.log(3.0))), 0.1, 3.0),
        "margin_rows": draw_margin_rows(jax.random.fold_in(keys[7], 71), 0),
    }


primal_step = 0.5
dual_step = 0.5

def build_toeplitz(filters, height):
    bases, tap_count = filters.shape
    reach_rows = tap_count - 1
    tap_mask = jnp.arange(tap_count)[None, :] < 2 * (jnp.arange(bases)[:, None] + 1)
    tap_values = jnp.where(tap_mask, filters, jnp.zeros_like(filters))
    tap_index = jnp.arange(height)[:, None] - jnp.arange(height + reach_rows)[None, :] + reach_rows
    one_hot = (tap_index[None, :, :] == jnp.arange(tap_count)[:, None, None]).astype(filters.dtype)
    return jnp.einsum('bk,krs->brs', tap_values, one_hot, precision=lax.Precision.HIGHEST)

def reference(x_start, dirty, weights, filters, basis, bounds, margin_rows):
    reach_rows = MAXB
    toeplitz = build_toeplitz(filters, FR)
    offsets = jnp.arange(reach_rows)
    edge_mask = ((reach_rows - offsets)[None, :] <= margin_rows[:, None]).astype(x_start.dtype)

    def analysis(cube_in):
        blocks = cube_in.reshape(CH, FACETS, FR, FC)
        previous = jnp.concatenate([jnp.zeros((CH, 1, reach_rows, FC), cube_in.dtype), blocks[:, :-1, FR - reach_rows:, :]], axis=1)
        extended = jnp.concatenate([previous * edge_mask[None, :, :, None], blocks], axis=2)

        def per_basis(matrix):
            return jnp.einsum('rs,cfsn->cfrn', matrix, extended, precision=lax.Precision.HIGHEST).reshape(CH, ROWS, FC)
        return lax.map(per_basis, toeplitz)

    def adjoint(dual_state):
        blocks = dual_state.reshape(NB, CH, FACETS, FR, FC)

        def accumulate(total, basis_pair):
            matrix, dual_piece = basis_pair
            return (total + jnp.einsum('rs,cfrn->cfsn', matrix, dual_piece, precision=lax.Precision.HIGHEST), None)
        spread, _ = lax.scan(accumulate, jnp.zeros((CH, FACETS, FR + reach_rows, FC), dual_state.dtype), (toeplitz, blocks))
        border_sum = spread[:, :, :reach_rows, :] * edge_mask[None, :, :, None]
        shifted = jnp.concatenate([border_sum[:, 1:], jnp.zeros((CH, 1, reach_rows, FC), dual_state.dtype)], axis=1)
        interior = spread[:, :, reach_rows:, :] + jnp.pad(shifted, ((0, 0), (0, 0), (FR - reach_rows, 0), (0, 0)))
        return interior.reshape(CH, ROWS, FC)
    image = x_start
    wavelet = jnp.zeros((NB, CH, ROWS, FC), x_start.dtype)
    spectral = jnp.zeros_like(x_start)
    for iteration in range(ITERS):
        gradient = image - dirty + spectral
        if iteration > 0:
            gradient = gradient + adjoint(wavelet)
        updated = jnp.maximum(image - primal_step * gradient, 0.0)
        reflected = 2.0 * updated - image
        lifted = wavelet + dual_step * analysis(reflected)
        magnitudes = jnp.sqrt(lax.optimization_barrier(jnp.sum(lifted * lifted, axis=1)))
        wavelet = lifted * (weights / jnp.maximum(magnitudes, weights))[:, None]
        spectral_lift = (spectral + dual_step * reflected).reshape(CH, FACETS, FR, FC)
        coefficients = jnp.einsum('fcq,cfpn->qfpn', basis, spectral_lift, precision=lax.Precision.HIGHEST)
        limits = bounds[:, None, None, None]
        clipped = jnp.clip(coefficients, -limits, limits)
        spectral = jnp.einsum('fcq,qfpn->cfpn', basis, clipped, precision=lax.Precision.HIGHEST).reshape(CH, ROWS, FC)
        image = updated
    return (image, wavelet, spectral)
```

```python
import functools

import jax
import jax.numpy as jnp
from jax import lax
from jax.experimental import pallas as pl
from jax.experimental.pallas import tpu as pltpu
from jax.sharding import PartitionSpec as P

PRIMAL = 0.5
DUAL = 0.5
F32 = jnp.float32
BF16 = jnp.bfloat16
CHUNKS = 2
GROUP = 4
VMEM_LIMIT = 24 << 20


def shift(value, axis, steps):
    count = lax.axis_size(axis)
    initial, last = (max(0, -steps), min(count, count - steps))
    return lax.ppermute(value, axis, [(source, source + steps) for source in range(initial, last)])


def chan_pairs(value, stride):
    count = lax.axis_size("chan")
    return lax.ppermute(value, "chan", [(source, source ^ stride) for source in range(count)])


def chan_terms(value):
    count = lax.axis_size("chan")
    if count & (count - 1):
        return lax.psum(value, "chan"), jnp.zeros_like(value)
    stride = 1
    other = jnp.zeros_like(value)
    while stride < count:
        if stride > 1:
            value = value + other
        other = chan_pairs(value, stride)
        stride *= 2
    return value, other


def high_low(value):
    high = lax.reduce_precision(value, 8, 7)
    low = value - high
    return high.astype(BF16), low.astype(BF16)


def split(value):
    high = value.astype(BF16)
    low = (value - high.astype(F32)).astype(BF16)
    return high, low


def three_lhs(matrix):
    high, low = high_low(matrix)
    return jnp.concatenate([high, high, low], axis=1)


def three_rhs(value):
    high, low = split(value)
    return jnp.concatenate([high, low, high], axis=0)


def two_lhs(matrix):
    high, low = high_low(matrix)
    top = jnp.concatenate([high, high], axis=1)
    bottom = jnp.concatenate([low, jnp.zeros_like(low)], axis=1)
    return jnp.concatenate([top, bottom], axis=0)


def two_rhs(value):
    high, low = split(value)
    return jnp.concatenate([high, low], axis=0)


def dot(lhs, rhs):
    return jnp.dot(lhs, rhs, preferred_element_type=F32)


def edge_toeplitz(filters, height, margin):
    bases, taps = filters.shape
    tap_mask = jnp.arange(taps)[None, :] < 2 * (jnp.arange(bases)[:, None] + 1)
    taps_of = jnp.where(tap_mask, filters, jnp.zeros_like(filters))
    rows = jnp.arange(height)[:, None]
    columns = jnp.arange(2 * height)[None, :]
    index = rows - columns + height
    allowed = (columns >= height) | (height - columns <= margin)
    result = jnp.zeros((bases, height, 2 * height), F32)
    for tap in range(taps):
        hit = (index == tap) & allowed
        result = jnp.where(hit[None], taps_of[:, tap][:, None, None], result)
    return result.reshape(bases * height, 2 * height)


def reflect_kernel(x_ref, d_ref, *r_refs):
    block = r_refs[0].shape[0]
    for index, r_ref in enumerate(r_refs):
        rows = pl.ds(index * block, block)
        x = x_ref[rows, :]
        updated = jnp.maximum(x - PRIMAL * (x - d_ref[rows, :]), 0.0)
        r_ref[...] = 2.0 * updated - x


def coef_kernel(height, spectral, lhs_ref, *refs):
    out_ref = refs[-1]
    s_ref = refs[0] if spectral else None
    r_refs = refs[1 if spectral else 0 : -1]
    rank = out_ref.shape[0]

    def pixels(row):
        parts = [r[pl.ds(row, r.shape[0] // height, stride=height), :] for r in r_refs]
        value = DUAL * jnp.concatenate(parts, axis=0)
        if spectral:
            value = value + s_ref[pl.ds(row, s_ref.shape[0] // height, stride=height), :]
        return value

    lhs = lhs_ref[...]
    lanes = out_ref.shape[1] // height
    for row in range(0, height, 2):
        value = jnp.concatenate([pixels(row), pixels(row + 1)], axis=1)
        both = dot(lhs, two_rhs(value))
        out_ref[:, row * lanes : (row + 2) * lanes] = both[:rank] + both[rank:]


def spectral_kernel(height, lhs_ref, own_ref, other_ref, bounds_ref, out_ref):
    lanes = out_ref.shape[1]
    channels = out_ref.shape[0] // height
    limit = bounds_ref[...]
    lhs = lhs_ref[...]
    for row in range(0, height, 2):
        span = slice(row * lanes, (row + 2) * lanes)
        total = own_ref[:, span] + other_ref[:, span]
        clipped = jnp.minimum(jnp.maximum(total, -limit), limit)
        both = dot(lhs, three_rhs(clipped))
        out_ref[pl.ds(row, channels, stride=height), :] = both[:, :lanes]
        out_ref[pl.ds(row + 1, channels, stride=height), :] = both[:, lanes:]


def scale_of(weights_ref, own_ref, other_ref):
    weights = weights_ref[...]
    return weights / jnp.maximum(jnp.sqrt(own_ref[...] + other_ref[...]), weights)


def extended(halo_ref, own_ref, height, channel):
    rows = pl.ds(pl.multiple_of(channel * height, height), height)
    return jnp.concatenate([halo_ref[rows, :], own_ref[rows, :]], axis=0)


def lift_kernel(height, first, *refs):
    if first:
        halo_ref, own_ref, lhs_ref, before_ref, out_ref, squares_ref = refs
    else:
        (halo_ref, own_ref, lhs_ref, before_ref, dual_ref, weights_ref, mine_ref, other_ref, out_ref, squares_ref) = refs
        scale = scale_of(weights_ref, mine_ref, other_ref)
    size = squares_ref.shape[0]
    lanes = own_ref.shape[1]
    channels = own_ref.shape[0] // height
    lhs = lhs_ref[...]

    def step(group, total):
        for pair in range(0, GROUP, 2):
            channel = group * GROUP + pair
            value = jnp.concatenate(
                [extended(halo_ref, own_ref, height, channel), extended(halo_ref, own_ref, height, channel + 1)], axis=1
            )
            both = dot(lhs, three_rhs(value))
            for half in range(2):
                rows = pl.ds(pl.multiple_of((channel + half) * size, size), size)
                lifted = both[:, half * lanes : (half + 1) * lanes]
                if not first:
                    lifted = lifted + dual_ref[rows, :] * scale
                out_ref[rows, :] = lifted
                total = total + lifted * lifted
        return total

    squares_ref[...] = lax.fori_loop(0, channels // GROUP, step, before_ref[...])


def adjoint_kernel(height, start, dual_ref, lhs_ref, weights_ref, mine_ref, other_ref, x_ref, d_ref, s_ref, border_ref, partial_ref):
    size, lanes = weights_ref.shape
    channels = border_ref.shape[0] // height
    scale = scale_of(weights_ref, mine_ref, other_ref)
    lhs = lhs_ref[...]

    def step(group, carry):
        for pair in range(0, GROUP, 2):
            channel = group * GROUP + pair
            duals = [
                dual_ref[pl.ds(pl.multiple_of((channel + half) * size, size), size), :] * scale for half in range(2)
            ]
            both = dot(lhs, two_rhs(jnp.concatenate(duals, axis=1)))
            spread = both[: 2 * height] + both[2 * height :]
            for half in range(2):
                rows = pl.ds(pl.multiple_of((channel + half) * height, height), height)
                mine = spread[:, half * lanes : (half + 1) * lanes]
                border_ref[rows, :] = mine[:height]
                cube = pl.ds(pl.multiple_of(start + (channel + half) * height, height), height)
                x, d = x_ref[cube, :], d_ref[cube, :]
                updated = jnp.maximum(x - PRIMAL * (x - d), 0.0)
                gradient = (updated - d) + s_ref[cube, :] + mine[height:]
                partial_ref[rows, :] = updated - PRIMAL * gradient
        return carry

    lax.fori_loop(0, channels // GROUP, step, 0)


def update_kernel(start, partial_ref, border_ref, x_ref, d_ref, u_ref, r_ref):
    cube = pl.ds(start, u_ref.shape[0])
    x = x_ref[cube, :]
    before = jnp.maximum(x - PRIMAL * (x - d_ref[cube, :]), 0.0)
    updated = jnp.maximum(partial_ref[...] - PRIMAL * border_ref[...], 0.0)
    u_ref[...] = updated
    r_ref[...] = 2.0 * updated - before


def wavelet_kernel(chunks, height, *refs):
    dual_refs = refs[:chunks]
    weights_ref, mine_ref, other_ref, out_ref, buffer, sems = refs[chunks:]
    size = weights_ref.shape[0]
    bases = size // height
    scale = scale_of(weights_ref, mine_ref, other_ref)
    block = buffer.shape[2]
    slots = buffer.shape[0]
    pending = [None] * slots
    turn = 0
    for index, dual_ref in enumerate(dual_refs):
        channels = dual_ref.shape[0] // size
        for start in range(0, channels, block):
            slot = turn % slots
            if pending[slot] is not None:
                pending[slot].wait()

            def step(channel, carry):
                rows = pl.ds(pl.multiple_of((start + channel) * size, size), size)
                value = dual_ref[rows, :] * scale
                for basis in range(bases):
                    buffer[slot, basis, channel] = value[basis * height : (basis + 1) * height]
                return carry

            lax.fori_loop(0, block, step, 0, unroll=2)
            copy = pltpu.make_async_copy(
                buffer.at[slot], out_ref.at[:, pl.ds(index * channels + start, block)], sems.at[slot]
            )
            copy.start()
            pending[slot] = copy
            turn += 1
    for copy in pending:
        if copy is not None:
            copy.wait()


def whole():
    return pl.BlockSpec(memory_space=pltpu.VMEM)


def call(kernel, outs, ins, operands, flops, nbytes, scratch=(), out_specs=None):
    return pl.pallas_call(
        kernel,
        out_shape=outs,
        in_specs=ins,
        out_specs=out_specs if out_specs is not None else jax.tree.map(lambda _: whole(), outs),
        scratch_shapes=scratch,
        compiler_params=pltpu.CompilerParams(vmem_limit_bytes=VMEM_LIMIT),
        cost_estimate=pl.CostEstimate(flops=flops, bytes_accessed=nbytes, transcendentals=0),
    )(*operands)


def body(x_start, dirty, weights, filters, basis, bounds, margin_rows):
    channels, height, lanes = x_start.shape
    bases, taps = filters.shape
    rank = bounds.shape[0]
    assert taps == height
    size = bases * height
    chunks = CHUNKS if channels >= 8 * CHUNKS else 1
    per = channels // chunks
    block = per * height
    rows = channels * height

    def flat(extent):
        return jax.ShapeDtypeStruct((extent, lanes), F32)

    x = x_start.reshape(rows, lanes)
    d = dirty.reshape(rows, lanes)
    w = weights.reshape(size, lanes)
    margin = lax.dynamic_index_in_dim(margin_rows, lax.axis_index("facet"), 0, keepdims=False)
    matrix = edge_toeplitz(filters, height, margin)
    lift_lhs = three_lhs(DUAL * matrix)
    adjoint_lhs = two_lhs(matrix.T)
    loading = basis[0]
    coef_lhs = two_lhs(loading.T)
    spectral_lhs = three_lhs(loading)
    limits = bounds[:, None]
    cubes = rows * lanes * 4
    duals = per * size * lanes * 4

    reflected = call(
        reflect_kernel, [flat(block)] * chunks, [whole()] * 2, (x, d), 4 * rows * lanes, 3 * cubes
    )
    halos = [shift(r, "facet", 1) for r in reflected]

    def coefficients(parts, spectral):
        operands = (coef_lhs,) + ((spectral,) if spectral is not None else ()) + tuple(parts)
        return call(
            functools.partial(coef_kernel, height, spectral is not None),
            jax.ShapeDtypeStruct((rank, height * lanes), F32),
            [whole()] * len(operands), operands, 6 * rank * rows * lanes, 2 * cubes,
        )

    def synthesis(own, other):
        return call(
            functools.partial(spectral_kernel, height), flat(rows), [whole()] * 4,
            (spectral_lhs, own, other, limits), 6 * rank * rows * lanes, 2 * cubes,
        )

    spectral = synthesis(*chan_terms(coefficients(reflected, None)))

    squares = jnp.zeros((size, lanes), F32)
    lifted = []
    for index in range(chunks):
        out, squares = call(
            functools.partial(lift_kernel, height, True), [flat(per * size), flat(size)], [whole()] * 4,
            (halos[index], reflected[index], lift_lhs, squares), 6 * 32 * per * size * lanes, duals,
        )
        lifted.append(out)
    own, other = chan_terms(squares)

    image, reflected, halos = [], [], []
    for index in range(chunks):
        borders, partial = call(
            functools.partial(adjoint_kernel, height, index * block), [flat(block)] * 2,
            [whole()] * 8,
            (lifted[index], adjoint_lhs, w, own, other, x, d, spectral), 6 * 32 * per * size * lanes, duals,
        )
        received = shift(borders, "facet", -1)
        updated, r = call(
            functools.partial(update_kernel, index * block), [flat(block)] * 2, [whole()] * 4,
            (partial, received, x, d), 5 * block * lanes, 6 * block * lanes * 4,
        )
        image.append(updated)
        reflected.append(r)
        halos.append(shift(r, "facet", 1))

    terms = chan_terms(coefficients(reflected, spectral))

    squares = jnp.zeros((size, lanes), F32)
    final = []
    for index in range(chunks):
        out, squares = call(
            functools.partial(lift_kernel, height, False), [flat(per * size), flat(size)], [whole()] * 8,
            (halos[index], reflected[index], lift_lhs, squares, lifted[index], w, own, other),
            6 * 32 * per * size * lanes, 2 * duals,
        )
        final.append(out)
    own, other = chan_terms(squares)
    spectral = synthesis(*terms)

    slab = min(per, 16)
    wavelet = call(
        functools.partial(wavelet_kernel, chunks, height),
        jax.ShapeDtypeStruct((bases, channels, height, lanes), F32),
        [whole()] * (chunks + 3), (*final, w, own, other), rows * lanes * bases, 2 * cubes * bases,
        scratch=[pltpu.VMEM((3, bases, slab, height, lanes), F32), pltpu.SemaphoreType.DMA((3,))],
        out_specs=pl.BlockSpec(memory_space=pl.ANY),
    )
    return (
        jnp.concatenate(image, axis=0).reshape(channels, height, lanes),
        wavelet,
        spectral.reshape(channels, height, lanes),
    )


def solution(mesh):
    in_specs = (
        P("chan", "facet", None),
        P("chan", "facet", None),
        P(None, "facet", None),
        P(),
        P("facet", "chan", None),
        P(),
        P(),
    )
    out_specs = (P("chan", "facet", None), P(None, "chan", "facet", None), P("chan", "facet", None))
    return jax.shard_map(body, mesh=mesh, in_specs=in_specs, out_specs=out_specs, check_vma=False)
```

```python
import functools

import jax
import jax.numpy as jnp
from jax import lax
from jax.experimental import pallas as pl
from jax.experimental.pallas import tpu as pltpu
from jax.sharding import PartitionSpec as P

PRIMAL = 0.5
DUAL = 0.5
F32 = jnp.float32
BF16 = jnp.bfloat16
CHUNKS = 2
GROUP = 32
VMEM_LIMIT = 24 << 20


def shift(value, axis, steps):
    count = lax.axis_size(axis)
    initial, last = (max(0, -steps), min(count, count - steps))
    return lax.ppermute(value, axis, [(source, source + steps) for source in range(initial, last)])


def chan_pairs(value, stride):
    count = lax.axis_size("chan")
    return lax.ppermute(value, "chan", [(source, source ^ stride) for source in range(count)])


def chan_terms(value):
    count = lax.axis_size("chan")
    if count & (count - 1):
        return lax.psum(value, "chan"), jnp.zeros_like(value)
    stride = 1
    other = jnp.zeros_like(value)
    while stride < count:
        if stride > 1:
            value = value + other
        other = chan_pairs(value, stride)
        stride *= 2
    return value, other


def split(value):
    high = value.astype(BF16)
    low = (value - high.astype(F32)).astype(BF16)
    return high, low


def three_lhs(matrix):
    high, low = split(matrix)
    return jnp.concatenate([high, high, low], axis=1)


def three_rhs(value):
    high, low = split(value)
    return jnp.concatenate([high, low, high], axis=0)


def two_lhs(matrix):
    high, low = split(matrix)
    top = jnp.concatenate([high, high], axis=1)
    bottom = jnp.concatenate([low, jnp.zeros_like(low)], axis=1)
    return jnp.concatenate([top, bottom], axis=0)


def two_rhs(value):
    high, low = split(value)
    return jnp.concatenate([high, low], axis=0)


def dot(lhs, rhs):
    return jnp.dot(lhs, rhs, preferred_element_type=F32)


def setup_kernel(
    filters_ref, bounds_ref, margin_ref, loading_ref, lift_ref, adjoint_ref, coef_ref, spectral_ref, limits_ref
):
    bases, taps = filters_ref.shape
    height = taps
    size = bases * height
    margin = margin_ref[lax.axis_index("facet")]
    source = lax.broadcasted_iota(jnp.int32, (2 * height, size), 0)
    target = lax.broadcasted_iota(jnp.int32, (2 * height, size), 1)
    tap_of = lax.rem(target, height) - source + height
    tap_of = jnp.where((source >= height) | (height - source <= margin), tap_of, -1)
    basis_of = lax.div(target, height)
    matrix = jnp.zeros((2 * height, size), F32)
    for tap in range(taps):
        values = jnp.zeros((2 * height, size), F32)
        for basis in range(bases):
            if tap < 2 * (basis + 1):
                values = jnp.where(basis_of == basis, filters_ref[basis, tap], values)
        matrix = jnp.where(tap_of == tap, values, matrix)
    adjoint_ref[...] = two_lhs(matrix)
    lift_ref[...] = three_lhs(DUAL * matrix.T)
    loading = loading_ref[...]
    coef_ref[...] = two_lhs(loading)
    spectral_ref[...] = three_lhs(loading.T)
    row = lax.broadcasted_iota(jnp.int32, limits_ref.shape, 0)
    limits = jnp.zeros(limits_ref.shape, F32)
    for index in range(bounds_ref.shape[0]):
        limits = jnp.where(row == index, bounds_ref[index], limits)
    limits_ref[...] = limits


def reflect_kernel(x_ref, d_ref, *refs):
    r_refs, (x_buffer, d_buffer, sems) = refs[:-3], refs[-3:]
    block = r_refs[0].shape[0]
    copies = []
    for index in range(len(r_refs)):
        rows = pl.ds(index * block, block)
        for turn, (source, target) in enumerate(((x_ref, x_buffer), (d_ref, d_buffer))):
            copy = pltpu.make_async_copy(source.at[rows], target.at[rows], sems.at[2 * index + turn])
            copy.start()
            copies.append(copy)
    for index, r_ref in enumerate(r_refs):
        copies[2 * index].wait()
        copies[2 * index + 1].wait()
        rows = pl.ds(index * block, block)
        x = x_buffer[rows, :]
        updated = jnp.maximum(x - PRIMAL * (x - d_buffer[rows, :]), 0.0)
        r_ref[...] = 2.0 * updated - x


def coef_kernel(height, spectral, lhs_ref, *refs):
    out_ref = refs[-1]
    s_ref = refs[0] if spectral else None
    r_refs = refs[1 if spectral else 0 : -1]
    rank = out_ref.shape[0]

    def pixels(row):
        parts = [r[pl.ds(row, r.shape[0] // height, stride=height), :] for r in r_refs]
        value = DUAL * jnp.concatenate(parts, axis=0)
        if spectral:
            value = value + s_ref[pl.ds(row, s_ref.shape[0] // height, stride=height), :]
        return value

    lhs = lhs_ref[...]
    lanes = out_ref.shape[1] // height
    for row in range(0, height, 2):
        value = jnp.concatenate([pixels(row), pixels(row + 1)], axis=1)
        both = dot(lhs, two_rhs(value))
        out_ref[:, row * lanes : (row + 2) * lanes] = both[:rank] + both[rank:]


def spectral_kernel(height, lhs_ref, own_ref, other_ref, bounds_ref, out_ref):
    lanes = out_ref.shape[1]
    channels = out_ref.shape[0] // height
    limit = jnp.concatenate([bounds_ref[...]] * 2, axis=1)
    lhs = lhs_ref[...]
    for row in range(0, height, 2):
        span = slice(row * lanes, (row + 2) * lanes)
        total = own_ref[:, span] + other_ref[:, span]
        clipped = jnp.minimum(jnp.maximum(total, -limit), limit)
        both = dot(lhs, three_rhs(clipped))
        out_ref[pl.ds(row, channels, stride=height), :] = both[:, :lanes]
        out_ref[pl.ds(row + 1, channels, stride=height), :] = both[:, lanes:]


def scale_of(weights_ref, own_ref, other_ref):
    weights = weights_ref[...]
    return weights / jnp.maximum(jnp.sqrt(own_ref[...] + other_ref[...]), weights)


def extended(halo_ref, own_ref, height, channel):
    rows = pl.ds(pl.multiple_of(channel * height, height), height)
    return jnp.concatenate([halo_ref[rows, :], own_ref[rows, :]], axis=0)


def lift_kernel(height, first, *refs):
    if first:
        halo_ref, own_ref, lhs_ref, before_ref, out_ref, squares_ref = refs
    else:
        (halo_ref, own_ref, lhs_ref, before_ref, dual_ref, weights_ref, mine_ref, other_ref, out_ref, squares_ref) = refs
        scale = scale_of(weights_ref, mine_ref, other_ref)
    size = squares_ref.shape[0]
    lanes = own_ref.shape[1]
    channels = own_ref.shape[0] // height
    lhs = lhs_ref[...]
    many = min(GROUP, channels)

    def step(group, total):
        for pair in range(0, many, 2):
            channel = group * many + pair
            value = jnp.concatenate(
                [extended(halo_ref, own_ref, height, channel), extended(halo_ref, own_ref, height, channel + 1)], axis=1
            )
            both = dot(lhs, three_rhs(value))
            for half in range(2):
                rows = pl.ds(pl.multiple_of((channel + half) * size, size), size)
                lifted = both[:, half * lanes : (half + 1) * lanes]
                if not first:
                    lifted = lifted + dual_ref[rows, :] * scale
                out_ref[rows, :] = lifted
                total = total + lifted * lifted
        return total

    squares_ref[...] = lax.fori_loop(0, channels // many, step, before_ref[...])


def adjoint_kernel(height, start, dual_ref, lhs_ref, weights_ref, mine_ref, other_ref, x_ref, d_ref, s_ref, border_ref, partial_ref):
    size, lanes = weights_ref.shape
    channels = border_ref.shape[0] // height
    scale = scale_of(weights_ref, mine_ref, other_ref)
    lhs = lhs_ref[...]
    many = min(GROUP, channels)

    def step(group, carry):
        for pair in range(0, many, 2):
            channel = group * many + pair
            duals = [
                dual_ref[pl.ds(pl.multiple_of((channel + half) * size, size), size), :] * scale for half in range(2)
            ]
            both = dot(lhs, two_rhs(jnp.concatenate(duals, axis=1)))
            spread = both[: 2 * height] + both[2 * height :]
            for half in range(2):
                rows = pl.ds(pl.multiple_of((channel + half) * height, height), height)
                mine = spread[:, half * lanes : (half + 1) * lanes]
                border_ref[rows, :] = mine[:height]
                cube = pl.ds(pl.multiple_of(start + (channel + half) * height, height), height)
                x, d = x_ref[cube, :], d_ref[cube, :]
                updated = jnp.maximum(x - PRIMAL * (x - d), 0.0)
                gradient = (updated - d) + s_ref[cube, :] + mine[height:]
                partial_ref[rows, :] = updated - PRIMAL * gradient
        return carry

    lax.fori_loop(0, channels // many, step, 0)


def update_kernel(chunks, *refs):
    partial_refs, border_refs = refs[:chunks], refs[chunks : 2 * chunks]
    x_ref, d_ref, u_ref = refs[2 * chunks : 2 * chunks + 3]
    for index, r_ref in enumerate(refs[2 * chunks + 3 :]):
        rows = pl.ds(index * r_ref.shape[0], r_ref.shape[0])
        x = x_ref[rows, :]
        before = jnp.maximum(x - PRIMAL * (x - d_ref[rows, :]), 0.0)
        updated = jnp.maximum(partial_refs[index][...] - PRIMAL * border_refs[index][...], 0.0)
        u_ref[rows, :] = updated
        r_ref[...] = 2.0 * updated - before


def wavelet_kernel(chunks, height, *refs):
    dual_refs = refs[:chunks]
    weights_ref, mine_ref, other_ref, out_ref, buffer, sems = refs[chunks:]
    size = weights_ref.shape[0]
    bases = size // height
    scale = scale_of(weights_ref, mine_ref, other_ref)
    block = buffer.shape[2]
    slots = buffer.shape[0]
    pending = [None] * slots
    turn = 0
    for index, dual_ref in enumerate(dual_refs):
        channels = dual_ref.shape[0] // size
        for start in range(0, channels, block):
            slot = turn % slots
            if pending[slot] is not None:
                pending[slot].wait()

            def step(channel, carry):
                rows = pl.ds(pl.multiple_of((start + channel) * size, size), size)
                value = dual_ref[rows, :] * scale
                for basis in range(bases):
                    buffer[slot, basis, channel] = value[basis * height : (basis + 1) * height]
                return carry

            lax.fori_loop(0, block, step, 0, unroll=2)
            copy = pltpu.make_async_copy(
                buffer.at[slot], out_ref.at[:, pl.ds(index * channels + start, block)], sems.at[slot]
            )
            copy.start()
            pending[slot] = copy
            turn += 1
    for copy in pending:
        if copy is not None:
            copy.wait()


def whole():
    return pl.BlockSpec(memory_space=pltpu.VMEM)


def call(kernel, outs, ins, operands, flops, nbytes, scratch=(), out_specs=None, limit=VMEM_LIMIT):
    return pl.pallas_call(
        kernel,
        out_shape=outs,
        in_specs=ins,
        out_specs=out_specs if out_specs is not None else jax.tree.map(lambda _: whole(), outs),
        scratch_shapes=scratch,
        compiler_params=pltpu.CompilerParams(vmem_limit_bytes=limit),
        cost_estimate=pl.CostEstimate(flops=flops, bytes_accessed=nbytes, transcendentals=0),
    )(*operands)


def body(x_start, dirty, weights, filters, basis, bounds, margin_rows):
    channels, height, lanes = x_start.shape
    bases, taps = filters.shape
    rank = bounds.shape[0]
    assert taps == height
    size = bases * height
    chunks = CHUNKS if channels >= 8 * CHUNKS else 1
    per = channels // chunks
    block = per * height
    rows = channels * height

    def flat(extent):
        return jax.ShapeDtypeStruct((extent, lanes), F32)

    x = x_start.reshape(rows, lanes)
    d = dirty.reshape(rows, lanes)
    w = weights.reshape(size, lanes)
    loading = basis[0].T
    cubes = rows * lanes * 4
    duals = per * size * lanes * 4

    distant = pl.BlockSpec(memory_space=pltpu.HBM)
    reflected = call(
        reflect_kernel, [flat(block)] * chunks, [distant] * 2, (x, d), 4 * rows * lanes, 3 * cubes,
        scratch=[pltpu.VMEM((rows, lanes), F32)] * 2 + [pltpu.SemaphoreType.DMA((2 * chunks,))], limit=None,
    )
    halos = [shift(r, "facet", 1) for r in reflected]

    scalars = pl.BlockSpec(memory_space=pltpu.SMEM)
    lift_lhs, adjoint_lhs, coef_lhs, spectral_lhs, limits = call(
        setup_kernel,
        [
            jax.ShapeDtypeStruct((size, 6 * height), BF16),
            jax.ShapeDtypeStruct((4 * height, 2 * size), BF16),
            jax.ShapeDtypeStruct((2 * rank, 2 * channels), BF16),
            jax.ShapeDtypeStruct((channels, 3 * rank), BF16),
            flat(rank),
        ],
        [scalars] * 3 + [whole()], (filters, bounds, margin_rows, loading), 100000, 100000,
    )

    def coefficients(parts, spectral):
        operands = (coef_lhs,) + ((spectral,) if spectral is not None else ()) + tuple(parts)
        return call(
            functools.partial(coef_kernel, height, spectral is not None),
            jax.ShapeDtypeStruct((rank, height * lanes), F32),
            [whole()] * len(operands), operands, 6 * rank * rows * lanes, 2 * cubes,
        )

    def synthesis(own, other):
        return call(
            functools.partial(spectral_kernel, height), flat(rows), [whole()] * 4,
            (spectral_lhs, own, other, limits), 6 * rank * rows * lanes, 2 * cubes,
        )

    spectral = synthesis(*chan_terms(coefficients(reflected, None)))

    squares = jnp.zeros((size, lanes), F32)
    lifted = []
    for index in range(chunks):
        out, squares = call(
            functools.partial(lift_kernel, height, True), [flat(per * size), flat(size)], [whole()] * 4,
            (halos[index], reflected[index], lift_lhs, squares), 6 * 32 * per * size * lanes, duals,
        )
        lifted.append(out)
    own, other = chan_terms(squares)

    borders, partials = [], []
    for index in range(chunks):
        border, partial = call(
            functools.partial(adjoint_kernel, height, index * block), [flat(block)] * 2, [whole()] * 8,
            (lifted[index], adjoint_lhs, w, own, other, x, d, spectral), 6 * 32 * per * size * lanes, duals,
        )
        borders.append(shift(border, "facet", -1))
        partials.append(partial)
    updates = call(
        functools.partial(update_kernel, chunks), [flat(rows)] + [flat(block)] * chunks, [whole()] * (2 * chunks + 2),
        (*partials, *borders, x, d), 5 * rows * lanes, 6 * cubes,
    )
    image, reflected = updates[0], updates[1:]
    halos = [shift(r, "facet", 1) for r in reflected]

    terms = chan_terms(coefficients(reflected, spectral))

    squares = jnp.zeros((size, lanes), F32)
    final = []
    for index in range(chunks):
        out, squares = call(
            functools.partial(lift_kernel, height, False), [flat(per * size), flat(size)], [whole()] * 8,
            (halos[index], reflected[index], lift_lhs, squares, lifted[index], w, own, other),
            6 * 32 * per * size * lanes, 2 * duals,
        )
        final.append(out)
    own, other = chan_terms(squares)
    spectral = synthesis(*terms)

    slab = min(per, 16)
    wavelet = call(
        functools.partial(wavelet_kernel, chunks, height),
        jax.ShapeDtypeStruct((bases, channels, height, lanes), F32),
        [whole()] * (chunks + 3), (*final, w, own, other), rows * lanes * bases, 2 * cubes * bases,
        scratch=[pltpu.VMEM((3, bases, slab, height, lanes), F32), pltpu.SemaphoreType.DMA((3,))],
        out_specs=distant,
    )
    return (
        image.reshape(channels, height, lanes),
        wavelet,
        spectral.reshape(channels, height, lanes),
    )


def solution(mesh):
    in_specs = (
        P("chan", "facet", None),
        P("chan", "facet", None),
        P(None, "facet", None),
        P(),
        P("facet", "chan", None),
        P(),
        P(),
    )
    out_specs = (P("chan", "facet", None), P(None, "chan", "facet", None), P("chan", "facet", None))
    return jax.shard_map(body, mesh=mesh, in_specs=in_specs, out_specs=out_specs, check_vma=False)
```

```python
import functools

import jax
import jax.numpy as jnp
from jax import lax
from jax.experimental import pallas as pl
from jax.experimental.pallas import tpu as pltpu
from jax.sharding import PartitionSpec as P

PRIMAL = 0.5
DUAL = 0.5
F32 = jnp.float32
BF16 = jnp.bfloat16
CHUNKS = 2
GROUP = 32
VMEM_LIMIT = 24 << 20


def shift(value, axis, steps):
    count = lax.axis_size(axis)
    initial, last = (max(0, -steps), min(count, count - steps))
    return lax.ppermute(value, axis, [(source, source + steps) for source in range(initial, last)])


def chan_pairs(value, stride):
    count = lax.axis_size("chan")
    return lax.ppermute(value, "chan", [(source, source ^ stride) for source in range(count)])


def chan_terms(value):
    count = lax.axis_size("chan")
    if count & (count - 1):
        return lax.psum(value, "chan"), jnp.zeros_like(value)
    stride = 1
    other = jnp.zeros_like(value)
    while stride < count:
        if stride > 1:
            value = value + other
        other = chan_pairs(value, stride)
        stride *= 2
    return value, other


def split(value):
    high = value.astype(BF16)
    low = (value - high.astype(F32)).astype(BF16)
    return high, low


def three_lhs(matrix):
    high, low = split(matrix)
    return jnp.concatenate([high, high, low], axis=1)


def three_rhs(value):
    high, low = split(value)
    return jnp.concatenate([high, low, high], axis=0)


def two_lhs(matrix):
    high, low = split(matrix)
    top = jnp.concatenate([high, high], axis=1)
    bottom = jnp.concatenate([low, jnp.zeros_like(low)], axis=1)
    return jnp.concatenate([top, bottom], axis=0)


def two_rhs(value):
    high, low = split(value)
    return jnp.concatenate([high, low], axis=0)


def dot(lhs, rhs):
    return jnp.dot(lhs, rhs, preferred_element_type=F32)


def setup_kernel(
    filters_ref, bounds_ref, margin_ref, loading_ref,
    lift_ref, next_ref, interior_ref, border_ref, coef_ref, spectral_ref, limits_ref,
):
    bases, taps = filters_ref.shape
    height = taps
    size = bases * height
    facet = lax.axis_index("facet")
    last = margin_ref.shape[0] - 1
    own_margin = margin_ref[facet]
    next_margin = jnp.where(facet < last, margin_ref[jnp.minimum(facet + 1, last)], 0)
    source = lax.broadcasted_iota(jnp.int32, (2 * height, size), 0)
    target = lax.broadcasted_iota(jnp.int32, (2 * height, size), 1)
    tap_of = lax.rem(target, height) - source + height
    basis_of = lax.div(target, height)
    matrix = jnp.zeros((2 * height, size), F32)
    for tap in range(taps):
        values = jnp.zeros((2 * height, size), F32)
        for basis in range(bases):
            if tap < 2 * (basis + 1):
                values = jnp.where(basis_of == basis, filters_ref[basis, tap], values)
        matrix = jnp.where(tap_of == tap, values, matrix)

    def masked(margin):
        return jnp.where((source >= height) | (height - source <= margin), matrix, 0.0)

    below = masked(next_margin)
    lift_ref[...] = three_lhs(DUAL * masked(own_margin).T)
    next_ref[...] = three_lhs(DUAL * below.T)
    interior_ref[...] = two_lhs(matrix[height:])
    border_ref[...] = two_lhs(below[:height])
    loading = loading_ref[...]
    coef_ref[...] = two_lhs(loading)
    spectral_ref[...] = three_lhs(loading.T)
    row = lax.broadcasted_iota(jnp.int32, limits_ref.shape, 0)
    limits = jnp.zeros(limits_ref.shape, F32)
    for index in range(bounds_ref.shape[0]):
        limits = jnp.where(row == index, bounds_ref[index], limits)
    limits_ref[...] = limits


def coef_kernel(height, spectral, lhs_ref, *refs):
    out_ref = refs[-1]
    s_ref = refs[0] if spectral else None
    r_refs = refs[1 if spectral else 0 : -1]
    rank = out_ref.shape[0]

    def pixels(row):
        parts = [r[pl.ds(row, r.shape[0] // height, stride=height), :] for r in r_refs]
        value = DUAL * jnp.concatenate(parts, axis=0)
        if spectral:
            value = value + s_ref[pl.ds(row, s_ref.shape[0] // height, stride=height), :]
        return value

    lhs = lhs_ref[...]
    lanes = out_ref.shape[1] // height
    for row in range(0, height, 2):
        value = jnp.concatenate([pixels(row), pixels(row + 1)], axis=1)
        both = dot(lhs, two_rhs(value))
        out_ref[:, row * lanes : (row + 2) * lanes] = both[:rank] + both[rank:]


def spectral_kernel(height, lhs_ref, own_ref, other_ref, bounds_ref, *refs):
    image_refs, out_ref = refs[:-1], refs[-1]
    if image_refs:
        image_ref, image_refs = refs[-2], refs[:-2]
        for index, part_ref in enumerate(image_refs):
            image_ref[pl.ds(index * part_ref.shape[0], part_ref.shape[0]), :] = part_ref[...]
    lanes = out_ref.shape[1]
    channels = out_ref.shape[0] // height
    limit = jnp.concatenate([bounds_ref[...]] * 2, axis=1)
    lhs = lhs_ref[...]
    for row in range(0, height, 2):
        span = slice(row * lanes, (row + 2) * lanes)
        total = own_ref[:, span] + other_ref[:, span]
        clipped = jnp.minimum(jnp.maximum(total, -limit), limit)
        both = dot(lhs, three_rhs(clipped))
        out_ref[pl.ds(row, channels, stride=height), :] = both[:, :lanes]
        out_ref[pl.ds(row + 1, channels, stride=height), :] = both[:, lanes:]


def scale_kernel(weights_ref, own_ref, other_ref, scale_ref):
    weights = weights_ref[...]
    scale_ref[...] = weights / jnp.maximum(jnp.sqrt(own_ref[...] + other_ref[...]), weights)


def extended(halo_ref, own_ref, height, channel):
    rows = pl.ds(pl.multiple_of(channel * height, height), height)
    return jnp.concatenate([halo_ref[rows, :], own_ref[rows, :]], axis=0)


def lift_kernel(height, kind, *refs):
    if kind == "next":
        halo_ref, own_ref, lhs_ref, out_ref = refs
    elif kind == "first":
        halo_ref, own_ref, lhs_ref, before_ref, out_ref, squares_ref = refs
    else:
        halo_ref, own_ref, lhs_ref, before_ref, dual_ref, scale_ref, out_ref, squares_ref = refs
        scale = scale_ref[...]
    lhs = lhs_ref[...]
    size = lhs.shape[0]
    lanes = own_ref.shape[1]
    channels = own_ref.shape[0] // height
    many = min(GROUP, channels)

    def step(group, total):
        for pair in range(0, many, 2):
            channel = group * many + pair
            value = jnp.concatenate(
                [extended(halo_ref, own_ref, height, channel), extended(halo_ref, own_ref, height, channel + 1)], axis=1
            )
            both = dot(lhs, three_rhs(value))
            for half in range(2):
                rows = pl.ds(pl.multiple_of((channel + half) * size, size), size)
                lifted = both[:, half * lanes : (half + 1) * lanes]
                if kind == "second":
                    lifted = lifted + dual_ref[rows, :] * scale
                out_ref[rows, :] = lifted
                if kind != "next":
                    total = total + lifted * lifted
        return total

    if kind == "next":
        lax.fori_loop(0, channels // many, step, 0)
    else:
        squares_ref[...] = lax.fori_loop(0, channels // many, step, before_ref[...])


def adjoint_kernel(height, start, border, dual_ref, lhs_ref, scale_ref, *refs):
    if border:
        partial_ref, x_ref, d_ref, updated_ref, reflected_ref = refs
    else:
        s_ref, x_ref, d_ref, partial_ref = refs
    size, lanes = scale_ref.shape
    channels = partial_ref.shape[0] // height
    scale = scale_ref[...]
    lhs = lhs_ref[...]
    many = min(GROUP, channels)

    def step(group, carry):
        for pair in range(0, many, 2):
            channel = group * many + pair
            duals = [
                dual_ref[pl.ds(pl.multiple_of((channel + half) * size, size), size), :] * scale for half in range(2)
            ]
            both = dot(lhs, two_rhs(jnp.concatenate(duals, axis=1)))
            spread = both[:height] + both[height:]
            for half in range(2):
                rows = pl.ds(pl.multiple_of((channel + half) * height, height), height)
                cube = pl.ds(pl.multiple_of(start + (channel + half) * height, height), height)
                mine = spread[:, half * lanes : (half + 1) * lanes]
                x, d = x_ref[cube, :], d_ref[cube, :]
                before = jnp.maximum(x - PRIMAL * (x - d), 0.0)
                if border:
                    updated = jnp.maximum(partial_ref[rows, :] - PRIMAL * mine, 0.0)
                    updated_ref[rows, :] = updated
                    reflected_ref[rows, :] = 2.0 * updated - before
                else:
                    partial_ref[rows, :] = before - PRIMAL * ((before - d) + s_ref[cube, :] + mine)
        return carry

    lax.fori_loop(0, channels // many, step, 0)


def wavelet_kernel(chunks, height, *refs):
    dual_refs = refs[:chunks]
    weights_ref, mine_ref, other_ref, out_ref, buffer, sems = refs[chunks:]
    size = weights_ref.shape[0]
    bases = size // height
    weights = weights_ref[...]
    scale = weights / jnp.maximum(jnp.sqrt(mine_ref[...] + other_ref[...]), weights)
    block = buffer.shape[2]
    slots = buffer.shape[0]
    pending = [None] * slots
    turn = 0
    for index, dual_ref in enumerate(dual_refs):
        channels = dual_ref.shape[0] // size
        for start in range(0, channels, block):
            slot = turn % slots
            if pending[slot] is not None:
                pending[slot].wait()

            def step(channel, carry):
                rows = pl.ds(pl.multiple_of((start + channel) * size, size), size)
                value = dual_ref[rows, :] * scale
                for basis in range(bases):
                    buffer[slot, basis, channel] = value[basis * height : (basis + 1) * height]
                return carry

            lax.fori_loop(0, block, step, 0, unroll=2)
            copy = pltpu.make_async_copy(
                buffer.at[slot], out_ref.at[:, pl.ds(index * channels + start, block)], sems.at[slot]
            )
            copy.start()
            pending[slot] = copy
            turn += 1
    for copy in pending:
        if copy is not None:
            copy.wait()


def whole():
    return pl.BlockSpec(memory_space=pltpu.VMEM)


def call(kernel, outs, ins, operands, flops, nbytes, scratch=(), out_specs=None, limit=VMEM_LIMIT):
    return pl.pallas_call(
        kernel,
        out_shape=outs,
        in_specs=ins,
        out_specs=out_specs if out_specs is not None else jax.tree.map(lambda _: whole(), outs),
        scratch_shapes=scratch,
        compiler_params=pltpu.CompilerParams(vmem_limit_bytes=limit),
        cost_estimate=pl.CostEstimate(flops=flops, bytes_accessed=nbytes, transcendentals=0),
    )(*operands)


def body(x_start, dirty, weights, filters, basis, bounds, margin_rows):
    channels, height, lanes = x_start.shape
    bases, taps = filters.shape
    rank = bounds.shape[0]
    assert taps == height
    size = bases * height
    chunks = CHUNKS if channels >= 8 * CHUNKS else 1
    per = channels // chunks
    block = per * height
    rows = channels * height

    def flat(extent):
        return jax.ShapeDtypeStruct((extent, lanes), F32)

    x = x_start.reshape(rows, lanes)
    d = dirty.reshape(rows, lanes)
    w = weights.reshape(size, lanes)
    loading = basis[0].T
    cubes = rows * lanes * 4
    duals = per * size * lanes * 4

    distant = pl.BlockSpec(memory_space=pltpu.HBM)
    scalars = pl.BlockSpec(memory_space=pltpu.SMEM)
    work = 6 * 2 * height * per * size * lanes

    reflected = []
    for index in range(chunks):
        some = slice(index * block, (index + 1) * block)
        updated = jnp.maximum(x[some] - PRIMAL * (x[some] - d[some]), 0.0)
        reflected.append(2.0 * updated - x[some])
    halos = [shift(r, "facet", 1) for r in reflected]

    lift_lhs, next_lhs, interior_lhs, border_lhs, coef_lhs, spectral_lhs, limits = call(
        setup_kernel,
        [
            jax.ShapeDtypeStruct((size, 6 * height), BF16),
            jax.ShapeDtypeStruct((size, 6 * height), BF16),
            jax.ShapeDtypeStruct((2 * height, 2 * size), BF16),
            jax.ShapeDtypeStruct((2 * height, 2 * size), BF16),
            jax.ShapeDtypeStruct((2 * rank, 2 * channels), BF16),
            jax.ShapeDtypeStruct((channels, 3 * rank), BF16),
            flat(rank),
        ],
        [scalars] * 3 + [whole()], (filters, bounds, margin_rows, loading), 100000, 100000,
    )

    def coefficients(parts, spectral):
        operands = (coef_lhs,) + ((spectral,) if spectral is not None else ()) + tuple(parts)
        return call(
            functools.partial(coef_kernel, height, spectral is not None),
            jax.ShapeDtypeStruct((rank, height * lanes), F32),
            [whole()] * len(operands), operands, 6 * rank * rows * lanes, 2 * cubes,
        )

    def synthesis(own, other, image=()):
        outs = [flat(rows)] * (2 if image else 1)
        return call(
            functools.partial(spectral_kernel, height), outs, [whole()] * (4 + len(image)),
            (spectral_lhs, own, other, limits, *image), 6 * rank * rows * lanes, 2 * cubes,
        )

    coefs = coefficients(reflected, None)
    tied = lax.optimization_barrier((coefs, *reflected))
    terms = chan_terms(tied[0])
    below = [shift(r, "facet", -1) for r in tied[1:]]
    (spectral,) = synthesis(*terms)

    squares = jnp.zeros((size, lanes), F32)
    lifted = []
    for index in range(chunks):
        out, squares = call(
            functools.partial(lift_kernel, height, "first"), [flat(per * size), flat(size)], [whole()] * 4,
            (halos[index], reflected[index], lift_lhs, squares), work, duals,
        )
        lifted.append(out)
    scale = call(scale_kernel, flat(size), [whole()] * 3, (w, *chan_terms(squares)), 10 * size * lanes, 16 * size * lanes)
    scale_below = shift(scale, "facet", -1)

    image, halos, again = [], [], []
    for index in range(chunks):
        dual_below = call(
            functools.partial(lift_kernel, height, "next"), flat(per * size), [whole()] * 3,
            (reflected[index], below[index], next_lhs), work, duals,
        )
        partial = call(
            functools.partial(adjoint_kernel, height, index * block, False), flat(block), [whole()] * 6,
            (lifted[index], interior_lhs, scale, spectral, x, d), work, duals,
        )
        updated, r = call(
            functools.partial(adjoint_kernel, height, index * block, True), [flat(block)] * 2, [whole()] * 6,
            (dual_below, border_lhs, scale_below, partial, x, d), work, duals,
        )
        image.append(updated)
        again.append(r)
        halos.append(shift(r, "facet", 1))
    terms = chan_terms(coefficients(again, spectral))

    squares = jnp.zeros((size, lanes), F32)
    final = []
    for index in range(chunks):
        out, squares = call(
            functools.partial(lift_kernel, height, "second"), [flat(per * size), flat(size)], [whole()] * 6,
            (halos[index], again[index], lift_lhs, squares, lifted[index], scale), work, 2 * duals,
        )
        final.append(out)
    own, other = chan_terms(squares)
    image, spectral = synthesis(*terms, image)

    slab = min(per, 16)
    wavelet = call(
        functools.partial(wavelet_kernel, chunks, height),
        jax.ShapeDtypeStruct((bases, channels, height, lanes), F32),
        [whole()] * (chunks + 3), (*final, w, own, other), rows * lanes * bases, 2 * cubes * bases,
        scratch=[pltpu.VMEM((3, bases, slab, height, lanes), F32), pltpu.SemaphoreType.DMA((3,))],
        out_specs=distant,
    )
    return (
        image.reshape(channels, height, lanes),
        wavelet,
        spectral.reshape(channels, height, lanes),
    )


def solution(mesh):
    in_specs = (
        P("chan", "facet", None),
        P("chan", "facet", None),
        P(None, "facet", None),
        P(),
        P("facet", "chan", None),
        P(),
        P(),
    )
    out_specs = (P("chan", "facet", None), P(None, "chan", "facet", None), P("chan", "facet", None))
    return jax.shard_map(body, mesh=mesh, in_specs=in_specs, out_specs=out_specs, check_vma=False)
```

```python
import functools

import jax
import jax.numpy as jnp
from jax import lax
from jax.experimental import pallas as pl
from jax.experimental.pallas import tpu as pltpu
from jax.sharding import PartitionSpec as P

PRIMAL = 0.5
DUAL = 0.5
F32 = jnp.float32
BF16 = jnp.bfloat16
CHUNKS = 2
GROUP = 32
VMEM_LIMIT = 24 << 20
REFLECT_LIMIT = 56000000


def shift(value, axis, steps):
    count = lax.axis_size(axis)
    initial, last = (max(0, -steps), min(count, count - steps))
    return lax.ppermute(value, axis, [(source, source + steps) for source in range(initial, last)])


def chan_pairs(value, stride):
    count = lax.axis_size("chan")
    return lax.ppermute(value, "chan", [(source, source ^ stride) for source in range(count)])


def chan_terms(value):
    count = lax.axis_size("chan")
    if count & (count - 1):
        return lax.psum(value, "chan"), jnp.zeros_like(value)
    stride = 1
    other = jnp.zeros_like(value)
    while stride < count:
        if stride > 1:
            value = value + other
        other = chan_pairs(value, stride)
        stride *= 2
    return value, other


def split(value):
    high = value.astype(BF16)
    low = (value - high.astype(F32)).astype(BF16)
    return high, low


def three_lhs(matrix):
    high, low = split(matrix)
    return jnp.concatenate([high, high, low], axis=1)


def three_rhs(value):
    high, low = split(value)
    return jnp.concatenate([high, low, high], axis=0)


def two_lhs(matrix):
    high, low = split(matrix)
    top = jnp.concatenate([high, high], axis=1)
    bottom = jnp.concatenate([low, jnp.zeros_like(low)], axis=1)
    return jnp.concatenate([top, bottom], axis=0)


def two_rhs(value):
    high, low = split(value)
    return jnp.concatenate([high, low], axis=0)


def dot(lhs, rhs):
    return jnp.dot(lhs, rhs, preferred_element_type=F32)


def setup_kernel(
    filters_ref, bounds_ref, margin_ref, loading_ref,
    lift_ref, next_ref, interior_ref, border_ref, coef_ref, spectral_ref, limits_ref,
):
    bases, taps = filters_ref.shape
    height = taps
    size = bases * height
    facet = lax.axis_index("facet")
    last = margin_ref.shape[0] - 1
    own_margin = margin_ref[facet]
    next_margin = jnp.where(facet < last, margin_ref[jnp.minimum(facet + 1, last)], 0)
    source = lax.broadcasted_iota(jnp.int32, (2 * height, size), 0)
    target = lax.broadcasted_iota(jnp.int32, (2 * height, size), 1)
    tap_of = lax.rem(target, height) - source + height
    basis_of = lax.div(target, height)
    matrix = jnp.zeros((2 * height, size), F32)
    for tap in range(taps):
        values = jnp.zeros((2 * height, size), F32)
        for basis in range(bases):
            if tap < 2 * (basis + 1):
                values = jnp.where(basis_of == basis, filters_ref[basis, tap], values)
        matrix = jnp.where(tap_of == tap, values, matrix)

    def masked(margin):
        return jnp.where((source >= height) | (height - source <= margin), matrix, 0.0)

    below = masked(next_margin)
    lift_ref[...] = three_lhs(DUAL * masked(own_margin).T)
    next_ref[...] = three_lhs(DUAL * below.T)
    interior_ref[...] = two_lhs(matrix[height:])
    border_ref[...] = two_lhs(below[:height])
    loading = loading_ref[...]
    coef_ref[...] = two_lhs(loading)
    spectral_ref[...] = three_lhs(loading.T)
    row = lax.broadcasted_iota(jnp.int32, limits_ref.shape, 0)
    limits = jnp.zeros(limits_ref.shape, F32)
    for index in range(bounds_ref.shape[0]):
        limits = jnp.where(row == index, bounds_ref[index], limits)
    limits_ref[...] = limits


def reflect_kernel(start, x_ref, d_ref, r_ref, x_buffer, d_buffer, sems):
    rows = pl.ds(start, r_ref.shape[0])
    copies = [
        pltpu.make_async_copy(source.at[rows], target, sems.at[turn])
        for turn, (source, target) in enumerate(((x_ref, x_buffer), (d_ref, d_buffer)))
    ]
    for copy in copies:
        copy.start()
    for copy in copies:
        copy.wait()
    x = x_buffer[...]
    updated = jnp.maximum(x - PRIMAL * (x - d_buffer[...]), 0.0)
    r_ref[...] = 2.0 * updated - x


def coef_kernel(height, spectral, lhs_ref, *refs):
    *r_refs, out_ref = refs
    if spectral:
        s_ref, *r_refs = r_refs
    rank = out_ref.shape[0]

    def pixels(row):
        parts = [r[pl.ds(row, r.shape[0] // height, stride=height), :] for r in r_refs]
        value = DUAL * jnp.concatenate(parts, axis=0)
        if spectral:
            value = value + s_ref[pl.ds(row, s_ref.shape[0] // height, stride=height), :]
        return value

    lhs = lhs_ref[...]
    lanes = out_ref.shape[1] // height
    for row in range(0, height, 2):
        value = jnp.concatenate([pixels(row), pixels(row + 1)], axis=1)
        both = dot(lhs, two_rhs(value))
        out_ref[:, row * lanes : (row + 2) * lanes] = both[:rank] + both[rank:]


def spectral_kernel(height, lhs_ref, own_ref, other_ref, bounds_ref, *refs):
    image_refs, out_ref = refs[:-1], refs[-1]
    if image_refs:
        image_ref, image_refs = refs[-2], refs[:-2]
        for index, part_ref in enumerate(image_refs):
            image_ref[pl.ds(index * part_ref.shape[0], part_ref.shape[0]), :] = part_ref[...]
    lanes = out_ref.shape[1]
    channels = out_ref.shape[0] // height
    limit = jnp.concatenate([bounds_ref[...]] * 2, axis=1)
    lhs = lhs_ref[...]
    for row in range(0, height, 2):
        span = slice(row * lanes, (row + 2) * lanes)
        total = own_ref[:, span] + other_ref[:, span]
        clipped = jnp.minimum(jnp.maximum(total, -limit), limit)
        both = dot(lhs, three_rhs(clipped))
        out_ref[pl.ds(row, channels, stride=height), :] = both[:, :lanes]
        out_ref[pl.ds(row + 1, channels, stride=height), :] = both[:, lanes:]


def scale_kernel(weights_ref, own_ref, other_ref, scale_ref):
    weights = weights_ref[...]
    scale_ref[...] = weights / jnp.maximum(jnp.sqrt(own_ref[...] + other_ref[...]), weights)


def extended(halo_ref, own_ref, height, channel):
    rows = pl.ds(pl.multiple_of(channel * height, height), height)
    return jnp.concatenate([halo_ref[rows, :], own_ref[rows, :]], axis=0)


def lift_kernel(height, kind, *refs):
    if kind == "first":
        halo_ref, own_ref, lhs_ref, before_ref, out_ref, squares_ref = refs
    else:
        halo_ref, own_ref, lhs_ref, before_ref, dual_ref, scale_ref, out_ref, squares_ref = refs
        scale = scale_ref[...]
    lhs = lhs_ref[...]
    size = lhs.shape[0]
    lanes = own_ref.shape[1]
    channels = own_ref.shape[0] // height
    many = min(GROUP, channels)

    def step(group, total):
        for pair in range(0, many, 2):
            channel = group * many + pair
            value = jnp.concatenate(
                [extended(halo_ref, own_ref, height, channel), extended(halo_ref, own_ref, height, channel + 1)], axis=1
            )
            both = dot(lhs, three_rhs(value))
            for half in range(2):
                rows = pl.ds(pl.multiple_of((channel + half) * size, size), size)
                lifted = both[:, half * lanes : (half + 1) * lanes]
                if kind == "second":
                    lifted = lifted + dual_ref[rows, :] * scale
                out_ref[rows, :] = lifted
                total = total + lifted * lifted
        return total

    squares_ref[...] = lax.fori_loop(0, channels // many, step, before_ref[...])


def adjoint_kernel(height, start, dual_ref, lhs_ref, scale_ref, s_ref, x_ref, d_ref, partial_ref):
    size, lanes = scale_ref.shape
    channels = partial_ref.shape[0] // height
    scale = scale_ref[...]
    lhs = lhs_ref[...]
    many = min(GROUP, channels)

    def step(group, carry):
        for pair in range(0, many, 2):
            channel = group * many + pair
            duals = [
                dual_ref[pl.ds(pl.multiple_of((channel + half) * size, size), size), :] * scale for half in range(2)
            ]
            both = dot(lhs, two_rhs(jnp.concatenate(duals, axis=1)))
            spread = both[:height] + both[height:]
            for half in range(2):
                rows = pl.ds(pl.multiple_of((channel + half) * height, height), height)
                cube = pl.ds(pl.multiple_of(start + (channel + half) * height, height), height)
                x, d = x_ref[cube, :], d_ref[cube, :]
                before = jnp.maximum(x - PRIMAL * (x - d), 0.0)
                mine = spread[:, half * lanes : (half + 1) * lanes]
                partial_ref[rows, :] = before - PRIMAL * ((before - d) + s_ref[cube, :] + mine)
        return carry

    lax.fori_loop(0, channels // many, step, 0)


def border_kernel(
    height, start, own_ref, below_ref, next_ref, border_ref, scale_ref, partial_ref, x_ref, d_ref, updated_ref, reflected_ref
):
    size, lanes = scale_ref.shape
    channels = partial_ref.shape[0] // height
    scale = jnp.concatenate([scale_ref[...]] * 2, axis=1)
    lift_lhs = next_ref[...]
    border_lhs = border_ref[...]
    many = min(GROUP, channels)

    def step(group, carry):
        for pair in range(0, many, 2):
            channel = group * many + pair
            spans = [
                (
                    pl.ds(pl.multiple_of((channel + half) * height, height), height),
                    pl.ds(pl.multiple_of(start + (channel + half) * height, height), height),
                )
                for half in range(2)
            ]
            value = jnp.concatenate(
                [jnp.concatenate([own_ref[rows, :], below_ref[rows, :]], axis=0) for rows, cube in spans], axis=1
            )
            duals = dot(lift_lhs, three_rhs(value)) * scale
            both = dot(border_lhs, two_rhs(duals))
            spread = both[:height] + both[height:]
            for half, (rows, cube) in enumerate(spans):
                x, d = x_ref[cube, :], d_ref[cube, :]
                before = jnp.maximum(x - PRIMAL * (x - d), 0.0)
                mine = spread[:, half * lanes : (half + 1) * lanes]
                updated = jnp.maximum(partial_ref[rows, :] - PRIMAL * mine, 0.0)
                updated_ref[rows, :] = updated
                reflected_ref[rows, :] = 2.0 * updated - before
        return carry

    lax.fori_loop(0, channels // many, step, 0)


def wavelet_kernel(chunks, height, *refs):
    dual_refs = refs[:chunks]
    weights_ref, mine_ref, other_ref, out_ref, buffer, sems = refs[chunks:]
    size = weights_ref.shape[0]
    bases = size // height
    weights = weights_ref[...]
    scale = weights / jnp.maximum(jnp.sqrt(mine_ref[...] + other_ref[...]), weights)
    block = buffer.shape[2]
    slots = buffer.shape[0]
    pending = [None] * slots
    turn = 0
    for index, dual_ref in enumerate(dual_refs):
        channels = dual_ref.shape[0] // size
        for start in range(0, channels, block):
            slot = turn % slots
            if pending[slot] is not None:
                pending[slot].wait()

            def step(channel, carry):
                rows = pl.ds(pl.multiple_of((start + channel) * size, size), size)
                value = dual_ref[rows, :] * scale
                for basis in range(bases):
                    buffer[slot, basis, channel] = value[basis * height : (basis + 1) * height]
                return carry

            lax.fori_loop(0, block, step, 0, unroll=2)
            copy = pltpu.make_async_copy(
                buffer.at[slot], out_ref.at[:, pl.ds(index * channels + start, block)], sems.at[slot]
            )
            copy.start()
            pending[slot] = copy
            turn += 1
    for copy in pending:
        if copy is not None:
            copy.wait()


def whole():
    return pl.BlockSpec(memory_space=pltpu.VMEM)


def call(kernel, outs, ins, operands, flops, nbytes, scratch=(), out_specs=None, limit=VMEM_LIMIT):
    return pl.pallas_call(
        kernel,
        out_shape=outs,
        in_specs=ins,
        out_specs=out_specs if out_specs is not None else jax.tree.map(lambda _: whole(), outs),
        scratch_shapes=scratch,
        compiler_params=pltpu.CompilerParams(vmem_limit_bytes=limit),
        cost_estimate=pl.CostEstimate(flops=flops, bytes_accessed=nbytes, transcendentals=0),
    )(*operands)


def body(x_start, dirty, weights, filters, basis, bounds, margin_rows):
    channels, height, lanes = x_start.shape
    bases, taps = filters.shape
    rank = bounds.shape[0]
    assert taps == height
    size = bases * height
    chunks = CHUNKS if channels >= 8 * CHUNKS else 1
    per = channels // chunks
    block = per * height
    rows = channels * height

    def flat(extent):
        return jax.ShapeDtypeStruct((extent, lanes), F32)

    x = x_start.reshape(rows, lanes)
    d = dirty.reshape(rows, lanes)
    w = weights.reshape(size, lanes)
    loading = basis[0].T
    cubes = rows * lanes * 4
    duals = per * size * lanes * 4

    distant = pl.BlockSpec(memory_space=pltpu.HBM)
    scalars = pl.BlockSpec(memory_space=pltpu.SMEM)
    work = 6 * 2 * height * per * size * lanes

    reflected = []
    for index in range(chunks):
        reflected.append(call(
            functools.partial(reflect_kernel, index * block), flat(block), [distant] * 2, (x, d),
            4 * block * lanes, 12 * block * lanes,
            scratch=[pltpu.VMEM((block, lanes), F32)] * 2 + [pltpu.SemaphoreType.DMA((2,))], limit=REFLECT_LIMIT,
        ))
    halos = [shift(r, "facet", 1) for r in reflected]

    lift_lhs, next_lhs, interior_lhs, border_lhs, coef_lhs, spectral_lhs, limits = call(
        setup_kernel,
        [
            jax.ShapeDtypeStruct((size, 6 * height), BF16),
            jax.ShapeDtypeStruct((size, 6 * height), BF16),
            jax.ShapeDtypeStruct((2 * height, 2 * size), BF16),
            jax.ShapeDtypeStruct((2 * height, 2 * size), BF16),
            jax.ShapeDtypeStruct((2 * rank, 2 * channels), BF16),
            jax.ShapeDtypeStruct((channels, 3 * rank), BF16),
            flat(rank),
        ],
        [scalars] * 3 + [whole()], (filters, bounds, margin_rows, loading), 100000, 100000,
    )

    def coefficients(parts, spectral):
        operands = (coef_lhs,) + ((spectral,) if spectral is not None else ()) + tuple(parts)
        outs = jax.ShapeDtypeStruct((rank, height * lanes), F32)
        return call(
            functools.partial(coef_kernel, height, spectral is not None), outs,
            [whole()] * len(operands), operands, 6 * rank * rows * lanes, 2 * cubes,
        )

    def synthesis(own, other, image=()):
        outs = [flat(rows)] * (2 if image else 1)
        return call(
            functools.partial(spectral_kernel, height), outs, [whole()] * (4 + len(image)),
            (spectral_lhs, own, other, limits, *image), 6 * rank * rows * lanes, 2 * cubes,
        )

    coefs = coefficients(reflected, None)
    terms = chan_terms(coefs)
    squares = jnp.zeros((size, lanes), F32)
    lifted, below = [], []
    for index in range(chunks):
        out, squares = call(
            functools.partial(lift_kernel, height, "first"), [flat(per * size), flat(size)], [whole()] * 4,
            (halos[index], reflected[index], lift_lhs, squares), work, duals,
        )
        lifted.append(out)
        if index < chunks - 1:
            tied, _, _ = lax.optimization_barrier((reflected[index], squares, coefs))
            below.append(shift(tied, "facet", -1))
            squares, halos[index + 1] = lax.optimization_barrier((squares, halos[index + 1]))
        elif index:
            tied, _, *terms = lax.optimization_barrier((reflected[index], halos[index], *terms))
            below.append(shift(tied, "facet", -1))
        else:
            below.append(shift(reflected[index], "facet", -1))
    own, other = chan_terms(squares)
    *terms, _ = lax.optimization_barrier((*terms, squares))
    (spectral,) = synthesis(*terms)
    other, spectral = lax.optimization_barrier((other, spectral))
    scale = call(scale_kernel, flat(size), [whole()] * 3, (w, own, other), 10 * size * lanes, 16 * size * lanes)
    scale_below = shift(scale, "facet", -1)

    partials = [
        call(
            functools.partial(adjoint_kernel, height, index * block), flat(block), [whole()] * 6,
            (lifted[index], interior_lhs, scale, spectral, x, d), work, duals,
        )
        for index in range(chunks)
    ]
    image, halos, again = [], [], []
    for index in range(chunks):
        updated, r = call(
            functools.partial(border_kernel, height, index * block), [flat(block)] * 2, [whole()] * 8,
            (reflected[index], below[index], next_lhs, border_lhs, scale_below, partials[index], x, d), 2 * work, duals,
        )
        image.append(updated)
        again.append(r)
        halos.append(shift(r, "facet", 1))
    terms = chan_terms(coefficients(again, spectral))

    squares = jnp.zeros((size, lanes), F32)
    final = []
    for index in range(chunks):
        out, squares = call(
            functools.partial(lift_kernel, height, "second"), [flat(per * size), flat(size)], [whole()] * 6,
            (halos[index], again[index], lift_lhs, squares, lifted[index], scale), work, 2 * duals,
        )
        final.append(out)
    own, other = chan_terms(squares)
    image, spectral = synthesis(*terms, image)

    slab = min(per, 16)
    wavelet = call(
        functools.partial(wavelet_kernel, chunks, height),
        jax.ShapeDtypeStruct((bases, channels, height, lanes), F32),
        [whole()] * (chunks + 3), (*final, w, own, other), rows * lanes * bases, 2 * cubes * bases,
        scratch=[pltpu.VMEM((3, bases, slab, height, lanes), F32), pltpu.SemaphoreType.DMA((3,))],
        out_specs=distant,
    )
    return (
        image.reshape(channels, height, lanes),
        wavelet,
        spectral.reshape(channels, height, lanes),
    )


def solution(mesh):
    in_specs = (
        P("chan", "facet", None),
        P("chan", "facet", None),
        P(None, "facet", None),
        P(),
        P("facet", "chan", None),
        P(),
        P(),
    )
    out_specs = (P("chan", "facet", None), P(None, "chan", "facet", None), P("chan", "facet", None))
    return jax.shard_map(body, mesh=mesh, in_specs=in_specs, out_specs=out_specs, check_vma=False)
```

```python
import functools

import jax
import jax.numpy as jnp
from jax import lax
from jax.experimental import pallas as pl
from jax.experimental.pallas import tpu as pltpu
from jax.sharding import PartitionSpec as P

PRIMAL = 0.5
DUAL = 0.5
F32 = jnp.float32
BF16 = jnp.bfloat16
CHUNKS = 2
GROUP = 32
PAD = 8
VMEM_LIMIT = 24 << 20
REFLECT_LIMIT = 56000000


def shift(value, axis, steps):
    count = lax.axis_size(axis)
    initial, last = (max(0, -steps), min(count, count - steps))
    return lax.ppermute(value, axis, [(source, source + steps) for source in range(initial, last)])


def chan_pairs(value, stride):
    count = lax.axis_size("chan")
    return lax.ppermute(value, "chan", [(source, source ^ stride) for source in range(count)])


def chan_terms(value):
    count = lax.axis_size("chan")
    if count & (count - 1):
        return lax.psum(value, "chan"), jnp.zeros_like(value)
    stride = 1
    other = jnp.zeros_like(value)
    while stride < count:
        if stride > 1:
            value = value + other
        other = chan_pairs(value, stride)
        stride *= 2
    return value, other


def split(value):
    high = value.astype(BF16)
    low = (value - high.astype(F32)).astype(BF16)
    return high, low


def three_lhs(matrix):
    high, low = split(matrix)
    return jnp.concatenate([high, high, low], axis=1)


def three_rhs(value):
    high, low = split(value)
    return jnp.concatenate([high, low, high], axis=0)


def two_lhs(matrix):
    high, low = split(matrix)
    top = jnp.concatenate([high, high], axis=1)
    bottom = jnp.concatenate([low, jnp.zeros_like(low)], axis=1)
    return jnp.concatenate([top, bottom], axis=0)


def two_rhs(value):
    high, low = split(value)
    return jnp.concatenate([high, low], axis=0)


def dot(lhs, rhs):
    return jnp.dot(lhs, rhs, preferred_element_type=F32)


def setup_kernel(
    filters_ref, bounds_ref, margin_ref, loading_ref,
    lift_ref, next_ref, interior_ref, border_ref, coef_ref, spectral_ref, limits_ref,
):
    bases, taps = filters_ref.shape
    height = taps
    size = bases * height
    facet = lax.axis_index("facet")
    last = margin_ref.shape[0] - 1
    own_margin = margin_ref[facet]
    next_margin = jnp.where(facet < last, margin_ref[jnp.minimum(facet + 1, last)], 0)

    def toeplitz(columns, column, tap_of):
        basis_of, _ = column(lax.broadcasted_iota(jnp.int32, (1, columns), 1))
        matrix = jnp.zeros((2 * height, columns), F32)
        for tap in range(taps):
            values = jnp.zeros((1, columns), F32)
            for basis in range(tap // 2, bases):
                values = jnp.where(basis_of == basis, filters_ref[basis, tap], values)
            matrix = jnp.where(tap_of == tap, values, matrix)
        return matrix

    def grids(columns, column):
        source = lax.broadcasted_iota(jnp.int32, (2 * height, columns), 0)
        return source, column(lax.broadcasted_iota(jnp.int32, (2 * height, columns), 1))[1]

    def dense(index):
        return lax.div(index, height), lax.rem(index, height)

    def reaching(index):
        basis = jnp.zeros_like(index)
        for number in range(1, bases):
            basis = basis + (index >= number * number).astype(jnp.int32)
        return basis, index - basis * basis

    source, target = grids(size, dense)
    borrowed = jnp.where((source < height - 1) & (height - 1 - source <= own_margin), target - source + height - 1, -1)
    own = toeplitz(size, dense, jnp.where(source >= height, target - source + height, borrowed))
    source, target = grids(bases * bases, reaching)
    tap_of = target - source + height
    below = toeplitz(bases * bases, reaching, jnp.where((source >= height) | (height - source <= next_margin), tap_of, -1))

    lift_ref[...] = three_lhs(DUAL * own.T)
    next_ref[...] = three_lhs(DUAL * below.T)
    interior_ref[...] = two_lhs(own[height:])
    border_ref[...] = two_lhs(below[:height])
    loading = loading_ref[...]
    coef_ref[...] = two_lhs(loading)
    spectral_ref[...] = three_lhs(loading.T)
    row = lax.broadcasted_iota(jnp.int32, limits_ref.shape, 0)
    limits = jnp.zeros(limits_ref.shape, F32)
    for index in range(bounds_ref.shape[0]):
        limits = jnp.where(row == index, bounds_ref[index], limits)
    limits_ref[...] = limits


def pack(source_ref, target_ref, height, first, start=0):
    reach = height - 1
    for channel in range(source_ref.shape[0] // height):
        target_ref[pl.ds(start + channel * reach, reach), :] = source_ref[pl.ds(channel * height + first, reach), :]


def clear_tail(packed_ref):
    packed_ref[pl.ds(packed_ref.shape[0] - PAD, PAD), :] = jnp.zeros((PAD, packed_ref.shape[1]), F32)


def reflect_kernel(height, start, x_ref, d_ref, r_ref, packed_ref, x_buffer, d_buffer, sems):
    rows = pl.ds(start, r_ref.shape[0])
    copies = [
        pltpu.make_async_copy(source.at[rows], target, sems.at[turn])
        for turn, (source, target) in enumerate(((x_ref, x_buffer), (d_ref, d_buffer)))
    ]
    for copy in copies:
        copy.start()
    for copy in copies:
        copy.wait()
    x = x_buffer[...]
    updated = jnp.maximum(x - PRIMAL * (x - d_buffer[...]), 0.0)
    r_ref[...] = 2.0 * updated - x
    pack(r_ref, packed_ref, height, 1)
    clear_tail(packed_ref)


def coef_kernel(height, spectral, lhs_ref, *refs):
    if spectral:
        s_ref, *r_refs, out_ref = refs
    else:
        *r_refs, out_ref, packed_ref = refs
        start = 0
        for r_ref in r_refs:
            pack(r_ref, packed_ref, height, 0, start)
            start += r_ref.shape[0] // height * (height - 1)
        clear_tail(packed_ref)
    rank = out_ref.shape[0]

    def pixels(row):
        parts = [r[pl.ds(row, r.shape[0] // height, stride=height), :] for r in r_refs]
        value = DUAL * jnp.concatenate(parts, axis=0)
        if spectral:
            value = value + s_ref[pl.ds(row, s_ref.shape[0] // height, stride=height), :]
        return value

    lhs = lhs_ref[...]
    lanes = out_ref.shape[1] // height
    for row in range(0, height, 2):
        value = jnp.concatenate([pixels(row), pixels(row + 1)], axis=1)
        both = dot(lhs, two_rhs(value))
        out_ref[:, row * lanes : (row + 2) * lanes] = both[:rank] + both[rank:]


def spectral_kernel(height, lhs_ref, own_ref, other_ref, bounds_ref, *refs):
    image_refs, out_ref = refs[:-1], refs[-1]
    if image_refs:
        image_ref, image_refs = refs[-2], refs[:-2]
        for index, part_ref in enumerate(image_refs):
            image_ref[pl.ds(index * part_ref.shape[0], part_ref.shape[0]), :] = part_ref[...]
    lanes = out_ref.shape[1]
    channels = out_ref.shape[0] // height
    limit = jnp.concatenate([bounds_ref[...]] * 2, axis=1)
    lhs = lhs_ref[...]
    for row in range(0, height, 2):
        span = slice(row * lanes, (row + 2) * lanes)
        total = own_ref[:, span] + other_ref[:, span]
        clipped = jnp.minimum(jnp.maximum(total, -limit), limit)
        both = dot(lhs, three_rhs(clipped))
        out_ref[pl.ds(row, channels, stride=height), :] = both[:, :lanes]
        out_ref[pl.ds(row + 1, channels, stride=height), :] = both[:, lanes:]


def scale_kernel(height, weights_ref, own_ref, other_ref, scale_ref, above_ref):
    weights = weights_ref[...]
    scale_ref[...] = weights / jnp.maximum(jnp.sqrt(own_ref[...] + other_ref[...]), weights)
    for basis in range(weights.shape[0] // height):
        count = 2 * basis + 1
        above_ref[pl.ds(basis * basis, count), :] = scale_ref[pl.ds(basis * height, count), :]


def lift_kernel(height, kind, *refs):
    if kind == "first":
        halo_ref, own_ref, lhs_ref, before_ref, out_ref, squares_ref = refs
    else:
        halo_ref, own_ref, lhs_ref, before_ref, dual_ref, scale_ref, out_ref, squares_ref = refs
        scale = scale_ref[...]
    lhs = lhs_ref[...]
    size = lhs.shape[0]
    lanes = own_ref.shape[1]
    total = before_ref[...]
    for pair in range(0, own_ref.shape[0] // height, 2):
        value = jnp.concatenate(
            [
                jnp.concatenate(
                    [
                        halo_ref[pl.ds(channel * (height - 1), height), :],
                        own_ref[pl.ds(channel * height, height), :],
                    ],
                    axis=0,
                )
                for channel in (pair, pair + 1)
            ],
            axis=1,
        )
        both = dot(lhs, three_rhs(value))
        for half in range(2):
            rows = pl.ds((pair + half) * size, size)
            lifted = both[:, half * lanes : (half + 1) * lanes]
            if kind == "second":
                lifted = lifted + dual_ref[rows, :] * scale
            out_ref[rows, :] = lifted
            total = total + lifted * lifted
    squares_ref[...] = total


def adjoint_kernel(height, start, dual_ref, lhs_ref, scale_ref, s_ref, x_ref, d_ref, partial_ref):
    size, lanes = scale_ref.shape
    channels = partial_ref.shape[0] // height
    scale = scale_ref[...]
    lhs = lhs_ref[...]
    many = min(GROUP, channels)

    def step(group, carry):
        for pair in range(0, many, 2):
            channel = group * many + pair
            duals = [
                dual_ref[pl.ds(pl.multiple_of((channel + half) * size, size), size), :] * scale for half in range(2)
            ]
            both = dot(lhs, two_rhs(jnp.concatenate(duals, axis=1)))
            spread = both[:height] + both[height:]
            for half in range(2):
                rows = pl.ds(pl.multiple_of((channel + half) * height, height), height)
                cube = pl.ds(pl.multiple_of(start + (channel + half) * height, height), height)
                x, d = x_ref[cube, :], d_ref[cube, :]
                before = jnp.maximum(x - PRIMAL * (x - d), 0.0)
                mine = spread[:, half * lanes : (half + 1) * lanes]
                partial_ref[rows, :] = before - PRIMAL * ((before - d) + s_ref[cube, :] + mine)
        return carry

    lax.fori_loop(0, channels // many, step, 0)


def border_kernel(
    height, start, own_ref, below_ref, next_ref, border_ref, scale_ref, partial_ref, x_ref, d_ref,
    updated_ref, reflected_ref, packed_ref,
):
    lanes = scale_ref.shape[1]
    scale = jnp.concatenate([scale_ref[...]] * 2, axis=1)
    lift_lhs = next_ref[...]
    border_lhs = border_ref[...]
    for pair in range(0, partial_ref.shape[0] // height, 2):
        channels = (pair, pair + 1)
        value = jnp.concatenate(
            [
                jnp.concatenate(
                    [
                        own_ref[pl.ds(channel * height, height), :],
                        below_ref[pl.ds((start + channel) * (height - 1), height), :],
                    ],
                    axis=0,
                )
                for channel in channels
            ],
            axis=1,
        )
        duals = dot(lift_lhs, three_rhs(value)) * scale
        both = dot(border_lhs, two_rhs(duals))
        spread = both[:height] + both[height:]
        for half, channel in enumerate(channels):
            rows = pl.ds(channel * height, height)
            cube = pl.ds((start + channel) * height, height)
            x, d = x_ref[cube, :], d_ref[cube, :]
            before = jnp.maximum(x - PRIMAL * (x - d), 0.0)
            mine = spread[:, half * lanes : (half + 1) * lanes]
            updated = jnp.maximum(partial_ref[rows, :] - PRIMAL * mine, 0.0)
            updated_ref[rows, :] = updated
            reflected_ref[rows, :] = 2.0 * updated - before
    pack(reflected_ref, packed_ref, height, 1)
    clear_tail(packed_ref)


def wavelet_kernel(chunks, height, *refs):
    dual_refs = refs[:chunks]
    weights_ref, mine_ref, other_ref, out_ref, buffer, sems = refs[chunks:]
    size = weights_ref.shape[0]
    bases = size // height
    weights = weights_ref[...]
    scale = weights / jnp.maximum(jnp.sqrt(mine_ref[...] + other_ref[...]), weights)
    block = buffer.shape[2]
    slots = buffer.shape[0]
    pending = [None] * slots
    turn = 0
    for index, dual_ref in enumerate(dual_refs):
        channels = dual_ref.shape[0] // size
        for start in range(0, channels, block):
            slot = turn % slots
            if pending[slot] is not None:
                pending[slot].wait()

            def step(channel, carry):
                rows = pl.ds(pl.multiple_of((start + channel) * size, size), size)
                value = dual_ref[rows, :] * scale
                for basis in range(bases):
                    buffer[slot, basis, channel] = value[basis * height : (basis + 1) * height]
                return carry

            lax.fori_loop(0, block, step, 0, unroll=2)
            copy = pltpu.make_async_copy(
                buffer.at[slot], out_ref.at[:, pl.ds(index * channels + start, block)], sems.at[slot]
            )
            copy.start()
            pending[slot] = copy
            turn += 1
    for copy in pending:
        if copy is not None:
            copy.wait()


def whole():
    return pl.BlockSpec(memory_space=pltpu.VMEM)


def call(kernel, outs, ins, operands, flops, nbytes, scratch=(), out_specs=None, limit=VMEM_LIMIT):
    return pl.pallas_call(
        kernel,
        out_shape=outs,
        in_specs=ins,
        out_specs=out_specs if out_specs is not None else jax.tree.map(lambda _: whole(), outs),
        scratch_shapes=scratch,
        compiler_params=pltpu.CompilerParams(vmem_limit_bytes=limit),
        cost_estimate=pl.CostEstimate(flops=flops, bytes_accessed=nbytes, transcendentals=0),
    )(*operands)


def body(x_start, dirty, weights, filters, basis, bounds, margin_rows):
    channels, height, lanes = x_start.shape
    bases, taps = filters.shape
    rank = bounds.shape[0]
    assert taps == height
    size = bases * height
    reaching = bases * bases
    chunks = CHUNKS if channels >= 8 * CHUNKS else 1
    per = channels // chunks
    block = per * height
    rows = channels * height

    def flat(extent):
        return jax.ShapeDtypeStruct((extent, lanes), F32)

    x = x_start.reshape(rows, lanes)
    d = dirty.reshape(rows, lanes)
    w = weights.reshape(size, lanes)
    loading = basis[0].T
    cubes = rows * lanes * 4
    duals = per * size * lanes * 4

    distant = pl.BlockSpec(memory_space=pltpu.HBM)
    scalars = pl.BlockSpec(memory_space=pltpu.SMEM)
    work = 6 * 2 * height * per * size * lanes

    packed = per * (height - 1) + PAD
    reflected, halos = [], []
    for index in range(chunks):
        r, ahead = call(
            functools.partial(reflect_kernel, height, index * block), [flat(block), flat(packed)], [distant] * 2, (x, d),
            4 * block * lanes, 12 * block * lanes,
            scratch=[pltpu.VMEM((block, lanes), F32)] * 2 + [pltpu.SemaphoreType.DMA((2,))], limit=REFLECT_LIMIT,
        )
        reflected.append(r)
        halos.append(shift(ahead, "facet", 1))

    lift_lhs, next_lhs, interior_lhs, border_lhs, coef_lhs, spectral_lhs, limits = call(
        setup_kernel,
        [
            jax.ShapeDtypeStruct((size, 6 * height), BF16),
            jax.ShapeDtypeStruct((reaching, 6 * height), BF16),
            jax.ShapeDtypeStruct((2 * height, 2 * size), BF16),
            jax.ShapeDtypeStruct((2 * height, 2 * reaching), BF16),
            jax.ShapeDtypeStruct((2 * rank, 2 * channels), BF16),
            jax.ShapeDtypeStruct((channels, 3 * rank), BF16),
            flat(rank),
        ],
        [scalars] * 3 + [whole()], (filters, bounds, margin_rows, loading), 100000, 100000,
    )

    def coefficients(parts, spectral):
        operands = (coef_lhs,) + ((spectral,) if spectral is not None else ()) + tuple(parts)
        outs = [jax.ShapeDtypeStruct((rank, height * lanes), F32)] + [flat(channels * (height - 1) + PAD)] * (spectral is None)
        return call(
            functools.partial(coef_kernel, height, spectral is not None), outs,
            [whole()] * len(operands), operands, 6 * rank * rows * lanes, 2 * cubes,
        )

    def synthesis(own, other, image=()):
        outs = [flat(rows)] * (2 if image else 1)
        return call(
            functools.partial(spectral_kernel, height), outs, [whole()] * (4 + len(image)),
            (spectral_lhs, own, other, limits, *image), 6 * rank * rows * lanes, 2 * cubes,
        )

    coefs, everything = coefficients(reflected, None)
    terms = chan_terms(coefs)
    squares = jnp.zeros((size, lanes), F32)
    lifted = []
    for index in range(chunks):
        out, squares = call(
            functools.partial(lift_kernel, height, "first"), [flat(per * size), flat(size)], [whole()] * 4,
            (halos[index], reflected[index], lift_lhs, squares), work, duals,
        )
        lifted.append(out)
        if index == 0:
            tied, _ = lax.optimization_barrier((everything, squares))
            below = shift(tied, "facet", -1)
            squares, *terms = lax.optimization_barrier((squares, *terms))
    own, other = chan_terms(squares)
    (spectral,) = synthesis(*terms)
    other, spectral = lax.optimization_barrier((other, spectral))
    scale, scale_above = call(
        functools.partial(scale_kernel, height), [flat(size), flat(reaching)], [whole()] * 3, (w, own, other),
        10 * size * lanes, 16 * size * lanes,
    )
    scale_below = shift(scale_above, "facet", -1)

    partials = [
        call(
            functools.partial(adjoint_kernel, height, index * block), flat(block), [whole()] * 6,
            (lifted[index], interior_lhs, scale, spectral, x, d), 22 * work, 22 * duals,
        )
        for index in range(chunks)
    ]
    image, halos, again = [], [], []
    for index in range(chunks):
        updated, r, ahead = call(
            functools.partial(border_kernel, height, index * per), [flat(block)] * 2 + [flat(packed)], [whole()] * 8,
            (reflected[index], below, next_lhs, border_lhs, scale_below, partials[index], x, d), 22 * work, 22 * duals,
        )
        image.append(updated)
        again.append(r)
        halos.append(shift(ahead, "facet", 1))
    terms = chan_terms(*coefficients(again, spectral))

    squares = jnp.zeros((size, lanes), F32)
    final = []
    for index in range(chunks):
        out, squares = call(
            functools.partial(lift_kernel, height, "second"), [flat(per * size), flat(size)], [whole()] * 6,
            (halos[index], again[index], lift_lhs, squares, lifted[index], scale), work, 2 * duals,
        )
        final.append(out)
    own, other = chan_terms(squares)
    image, spectral = synthesis(*terms, image)

    slab = min(per, 16)
    wavelet = call(
        functools.partial(wavelet_kernel, chunks, height),
        jax.ShapeDtypeStruct((bases, channels, height, lanes), F32),
        [whole()] * (chunks + 3), (*final, w, own, other), rows * lanes * bases, 2 * cubes * bases,
        scratch=[pltpu.VMEM((3, bases, slab, height, lanes), F32), pltpu.SemaphoreType.DMA((3,))],
        out_specs=distant,
    )
    return (
        image.reshape(channels, height, lanes),
        wavelet,
        spectral.reshape(channels, height, lanes),
    )


def solution(mesh):
    in_specs = (
        P("chan", "facet", None),
        P("chan", "facet", None),
        P(None, "facet", None),
        P(),
        P("facet", "chan", None),
        P(),
        P(),
    )
    out_specs = (P("chan", "facet", None), P(None, "chan", "facet", None), P("chan", "facet", None))
    return jax.shard_map(body, mesh=mesh, in_specs=in_specs, out_specs=out_specs, check_vma=False)
```

```python
import functools

import jax
import jax.numpy as jnp
from jax import lax
from jax.experimental import pallas as pl
from jax.experimental.pallas import tpu as pltpu
from jax.sharding import PartitionSpec as P

PRIMAL = 0.5
DUAL = 0.5
F32 = jnp.float32
BF16 = jnp.bfloat16
CHUNKS = 2
GROUP = 32
PAD = 8
VMEM_LIMIT = 24 << 20
REFLECT_LIMIT = 55000000


def shift(value, axis, steps):
    count = lax.axis_size(axis)
    initial, last = (max(0, -steps), min(count, count - steps))
    return lax.ppermute(value, axis, [(source, source + steps) for source in range(initial, last)])


def chan_pairs(value, stride):
    count = lax.axis_size("chan")
    return lax.ppermute(value, "chan", [(source, source ^ stride) for source in range(count)])


def chan_terms(value):
    count = lax.axis_size("chan")
    if count & (count - 1):
        return lax.psum(value, "chan"), jnp.zeros_like(value)
    stride = 1
    other = jnp.zeros_like(value)
    while stride < count:
        if stride > 1:
            value = value + other
        other = chan_pairs(value, stride)
        stride *= 2
    return value, other


def split(value):
    high = value.astype(BF16)
    low = (value - high.astype(F32)).astype(BF16)
    return high, low


def three_lhs(matrix):
    high, low = split(matrix)
    return jnp.concatenate([high, high, low], axis=1)


def three_rhs(value):
    high, low = split(value)
    return jnp.concatenate([high, low, high], axis=0)


def two_lhs(matrix):
    high, low = split(matrix)
    top = jnp.concatenate([high, high], axis=1)
    bottom = jnp.concatenate([low, jnp.zeros_like(low)], axis=1)
    return jnp.concatenate([top, bottom], axis=0)


def two_rhs(value):
    high, low = split(value)
    return jnp.concatenate([high, low], axis=0)


def dot(lhs, rhs):
    return jnp.dot(lhs, rhs, preferred_element_type=F32)


def setup_kernel(
    filters_ref, bounds_ref, margin_ref, loading_ref,
    lift_ref, next_ref, interior_ref, border_ref, coef_ref, spectral_ref, limits_ref,
):
    bases, taps = filters_ref.shape
    height = taps
    size = bases * height
    facet = lax.axis_index("facet")
    last = margin_ref.shape[0] - 1
    own_margin = margin_ref[facet]
    next_margin = jnp.where(facet < last, margin_ref[jnp.minimum(facet + 1, last)], 0)

    def toeplitz(columns, column, tap_of):
        basis_of, _ = column(lax.broadcasted_iota(jnp.int32, (1, columns), 1))
        matrix = jnp.zeros((2 * height, columns), F32)
        for tap in range(taps):
            values = jnp.zeros((1, columns), F32)
            for basis in range(tap // 2, bases):
                values = jnp.where(basis_of == basis, filters_ref[basis, tap], values)
            matrix = jnp.where(tap_of == tap, values, matrix)
        return matrix

    def grids(columns, column):
        source = lax.broadcasted_iota(jnp.int32, (2 * height, columns), 0)
        return source, column(lax.broadcasted_iota(jnp.int32, (2 * height, columns), 1))[1]

    def dense(index):
        return lax.div(index, height), lax.rem(index, height)

    def reaching(index):
        basis = jnp.zeros_like(index)
        for number in range(1, bases):
            basis = basis + (index >= number * number).astype(jnp.int32)
        return basis, index - basis * basis

    source, target = grids(size, dense)
    borrowed = jnp.where((source < height - 1) & (height - 1 - source <= own_margin), target - source + height - 1, -1)
    own = toeplitz(size, dense, jnp.where(source >= height, target - source + height, borrowed))
    source, target = grids(bases * bases, reaching)
    tap_of = target - source + height
    below = toeplitz(bases * bases, reaching, jnp.where((source >= height) | (height - source <= next_margin), tap_of, -1))

    lift_ref[...] = three_lhs(DUAL * own.T)
    next_ref[...] = three_lhs(DUAL * below.T)
    interior_ref[...] = two_lhs(own[height:])
    border_ref[...] = two_lhs(below[:height])
    loading = loading_ref[...]
    coef_ref[...] = two_lhs(loading)
    spectral_ref[...] = three_lhs(loading.T)
    row = lax.broadcasted_iota(jnp.int32, limits_ref.shape, 0)
    limits = jnp.zeros(limits_ref.shape, F32)
    for index in range(bounds_ref.shape[0]):
        limits = jnp.where(row == index, bounds_ref[index], limits)
    limits_ref[...] = limits


def pack(source_ref, target_ref, height, first, start=0):
    reach = height - 1
    for channel in range(source_ref.shape[0] // height):
        target_ref[pl.ds(start + channel * reach, reach), :] = source_ref[pl.ds(channel * height + first, reach), :]


def clear_tail(packed_ref):
    packed_ref[pl.ds(packed_ref.shape[0] - PAD, PAD), :] = jnp.zeros((PAD, packed_ref.shape[1]), F32)


def reflect_kernel(height, start, x_ref, d_ref, r_ref, packed_ref, x_buffer, d_buffer, sems):
    rows = pl.ds(start, r_ref.shape[0])
    copies = [
        pltpu.make_async_copy(source.at[rows], target, sems.at[turn])
        for turn, (source, target) in enumerate(((x_ref, x_buffer), (d_ref, d_buffer)))
    ]
    for copy in copies:
        copy.start()
    for copy in copies:
        copy.wait()
    x = x_buffer[...]
    updated = jnp.maximum(x - PRIMAL * (x - d_buffer[...]), 0.0)
    r_ref[...] = 2.0 * updated - x
    pack(r_ref, packed_ref, height, 1)
    clear_tail(packed_ref)


def coef_kernel(height, spectral, lhs_ref, *refs):
    if spectral:
        s_ref, *r_refs, out_ref = refs
    else:
        *r_refs, out_ref, packed_ref = refs
        start = 0
        for r_ref in r_refs:
            pack(r_ref, packed_ref, height, 0, start)
            start += r_ref.shape[0] // height * (height - 1)
        clear_tail(packed_ref)
    rank = out_ref.shape[0]

    def pixels(row):
        parts = [r[pl.ds(row, r.shape[0] // height, stride=height), :] for r in r_refs]
        value = DUAL * jnp.concatenate(parts, axis=0)
        if spectral:
            value = value + s_ref[pl.ds(row, s_ref.shape[0] // height, stride=height), :]
        return value

    lhs = lhs_ref[...]
    lanes = out_ref.shape[1] // height
    for row in range(0, height, 2):
        value = jnp.concatenate([pixels(row), pixels(row + 1)], axis=1)
        both = dot(lhs, two_rhs(value))
        out_ref[:, row * lanes : (row + 2) * lanes] = both[:rank] + both[rank:]


def spectral_kernel(height, lhs_ref, own_ref, other_ref, bounds_ref, *refs):
    image_refs, out_ref = refs[:-1], refs[-1]
    if image_refs:
        image_ref, image_refs = refs[-2], refs[:-2]
        for index, part_ref in enumerate(image_refs):
            image_ref[pl.ds(index * part_ref.shape[0], part_ref.shape[0]), :] = part_ref[...]
    lanes = out_ref.shape[1]
    channels = out_ref.shape[0] // height
    limit = jnp.concatenate([bounds_ref[...]] * 2, axis=1)
    lhs = lhs_ref[...]
    for row in range(0, height, 2):
        span = slice(row * lanes, (row + 2) * lanes)
        total = own_ref[:, span] + other_ref[:, span]
        clipped = jnp.minimum(jnp.maximum(total, -limit), limit)
        both = dot(lhs, three_rhs(clipped))
        out_ref[pl.ds(row, channels, stride=height), :] = both[:, :lanes]
        out_ref[pl.ds(row + 1, channels, stride=height), :] = both[:, lanes:]


def scale_kernel(height, weights_ref, own_ref, other_ref, scale_ref, above_ref):
    weights = weights_ref[...]
    scale_ref[...] = weights / jnp.maximum(jnp.sqrt(own_ref[...] + other_ref[...]), weights)
    for basis in range(weights.shape[0] // height):
        count = 2 * basis + 1
        above_ref[pl.ds(basis * basis, count), :] = scale_ref[pl.ds(basis * height, count), :]


def lift_kernel(height, kind, *refs):
    if kind == "first":
        halo_ref, own_ref, lhs_ref, before_ref, out_ref, squares_ref = refs
    else:
        halo_ref, own_ref, lhs_ref, before_ref, dual_ref, scale_ref, out_ref, squares_ref = refs
        scale = scale_ref[...]
    lhs = lhs_ref[...]
    size = lhs.shape[0]
    lanes = own_ref.shape[1]
    total = before_ref[...]
    for pair in range(0, own_ref.shape[0] // height, 2):
        value = jnp.concatenate(
            [
                jnp.concatenate(
                    [
                        halo_ref[pl.ds(channel * (height - 1), height), :],
                        own_ref[pl.ds(channel * height, height), :],
                    ],
                    axis=0,
                )
                for channel in (pair, pair + 1)
            ],
            axis=1,
        )
        both = dot(lhs, three_rhs(value))
        for half in range(2):
            rows = pl.ds((pair + half) * size, size)
            lifted = both[:, half * lanes : (half + 1) * lanes]
            if kind == "second":
                lifted = lifted + dual_ref[rows, :] * scale
            out_ref[rows, :] = lifted
            total = total + lifted * lifted
    squares_ref[...] = total


def adjoint_kernel(height, start, dual_ref, lhs_ref, scale_ref, s_ref, x_ref, d_ref, partial_ref):
    size, lanes = scale_ref.shape
    channels = partial_ref.shape[0] // height
    scale = scale_ref[...]
    lhs = lhs_ref[...]
    many = min(GROUP, channels)

    def step(group, carry):
        for pair in range(0, many, 2):
            channel = group * many + pair
            duals = [
                dual_ref[pl.ds(pl.multiple_of((channel + half) * size, size), size), :] * scale for half in range(2)
            ]
            both = dot(lhs, two_rhs(jnp.concatenate(duals, axis=1)))
            spread = both[:height] + both[height:]
            for half in range(2):
                rows = pl.ds(pl.multiple_of((channel + half) * height, height), height)
                cube = pl.ds(pl.multiple_of(start + (channel + half) * height, height), height)
                x, d = x_ref[cube, :], d_ref[cube, :]
                before = jnp.maximum(x - PRIMAL * (x - d), 0.0)
                mine = spread[:, half * lanes : (half + 1) * lanes]
                partial_ref[rows, :] = before - PRIMAL * ((before - d) + s_ref[cube, :] + mine)
        return carry

    lax.fori_loop(0, channels // many, step, 0)


def border_kernel(
    height, start, own_ref, below_ref, next_ref, border_ref, scale_ref, partial_ref, x_ref, d_ref,
    updated_ref, reflected_ref, packed_ref,
):
    lanes = scale_ref.shape[1]
    scale = jnp.concatenate([scale_ref[...]] * 2, axis=1)
    lift_lhs = next_ref[...]
    border_lhs = border_ref[...]
    for pair in range(0, partial_ref.shape[0] // height, 2):
        channels = (pair, pair + 1)
        value = jnp.concatenate(
            [
                jnp.concatenate(
                    [
                        own_ref[pl.ds(channel * height, height), :],
                        below_ref[pl.ds((start + channel) * (height - 1), height), :],
                    ],
                    axis=0,
                )
                for channel in channels
            ],
            axis=1,
        )
        duals = dot(lift_lhs, three_rhs(value)) * scale
        both = dot(border_lhs, two_rhs(duals))
        spread = both[:height] + both[height:]
        for half, channel in enumerate(channels):
            rows = pl.ds(channel * height, height)
            cube = pl.ds((start + channel) * height, height)
            x, d = x_ref[cube, :], d_ref[cube, :]
            before = jnp.maximum(x - PRIMAL * (x - d), 0.0)
            mine = spread[:, half * lanes : (half + 1) * lanes]
            updated = jnp.maximum(partial_ref[rows, :] - PRIMAL * mine, 0.0)
            updated_ref[rows, :] = updated
            reflected_ref[rows, :] = 2.0 * updated - before
    pack(reflected_ref, packed_ref, height, 1)
    clear_tail(packed_ref)


def wavelet_kernel(chunks, height, *refs):
    dual_refs = refs[:chunks]
    weights_ref, mine_ref, other_ref, out_ref, buffer, sems = refs[chunks:]
    size = weights_ref.shape[0]
    bases = size // height
    weights = weights_ref[...]
    scale = weights / jnp.maximum(jnp.sqrt(mine_ref[...] + other_ref[...]), weights)
    block = buffer.shape[2]
    slots = buffer.shape[0]
    pending = [None] * slots
    turn = 0
    for index, dual_ref in enumerate(dual_refs):
        channels = dual_ref.shape[0] // size
        for start in range(0, channels, block):
            slot = turn % slots
            if pending[slot] is not None:
                pending[slot].wait()

            def step(channel, carry):
                rows = pl.ds(pl.multiple_of((start + channel) * size, size), size)
                value = dual_ref[rows, :] * scale
                for basis in range(bases):
                    buffer[slot, basis, channel] = value[basis * height : (basis + 1) * height]
                return carry

            lax.fori_loop(0, block, step, 0, unroll=2)
            copy = pltpu.make_async_copy(
                buffer.at[slot], out_ref.at[:, pl.ds(index * channels + start, block)], sems.at[slot]
            )
            copy.start()
            pending[slot] = copy
            turn += 1
    for copy in pending:
        if copy is not None:
            copy.wait()


def whole():
    return pl.BlockSpec(memory_space=pltpu.VMEM)


def call(kernel, outs, ins, operands, flops, nbytes, scratch=(), out_specs=None, limit=VMEM_LIMIT):
    return pl.pallas_call(
        kernel,
        out_shape=outs,
        in_specs=ins,
        out_specs=out_specs if out_specs is not None else jax.tree.map(lambda _: whole(), outs),
        scratch_shapes=scratch,
        compiler_params=pltpu.CompilerParams(vmem_limit_bytes=limit),
        cost_estimate=pl.CostEstimate(flops=flops, bytes_accessed=nbytes, transcendentals=0),
    )(*operands)


def body(x_start, dirty, weights, filters, basis, bounds, margin_rows):
    channels, height, lanes = x_start.shape
    bases, taps = filters.shape
    rank = bounds.shape[0]
    assert taps == height
    size = bases * height
    reaching = bases * bases
    chunks = CHUNKS if channels >= 8 * CHUNKS else 1
    per = channels // chunks
    block = per * height
    rows = channels * height

    def flat(extent):
        return jax.ShapeDtypeStruct((extent, lanes), F32)

    x = x_start.reshape(rows, lanes)
    d = dirty.reshape(rows, lanes)
    w = weights.reshape(size, lanes)
    loading = basis[0].T
    cubes = rows * lanes * 4
    duals = per * size * lanes * 4

    distant = pl.BlockSpec(memory_space=pltpu.HBM)
    scalars = pl.BlockSpec(memory_space=pltpu.SMEM)
    work = 6 * 2 * height * per * size * lanes

    packed = per * (height - 1) + PAD
    reflected, halos = [], []
    for index in range(chunks):
        r, ahead = call(
            functools.partial(reflect_kernel, height, index * block), [flat(block), flat(packed)], [distant] * 2, (x, d),
            4 * block * lanes, 12 * block * lanes,
            scratch=[pltpu.VMEM((block, lanes), F32)] * 2 + [pltpu.SemaphoreType.DMA((2,))], limit=REFLECT_LIMIT,
        )
        reflected.append(r)
        halos.append(shift(ahead, "facet", 1))

    lift_lhs, next_lhs, interior_lhs, border_lhs, coef_lhs, spectral_lhs, limits = call(
        setup_kernel,
        [
            jax.ShapeDtypeStruct((size, 6 * height), BF16),
            jax.ShapeDtypeStruct((reaching, 6 * height), BF16),
            jax.ShapeDtypeStruct((2 * height, 2 * size), BF16),
            jax.ShapeDtypeStruct((2 * height, 2 * reaching), BF16),
            jax.ShapeDtypeStruct((2 * rank, 2 * channels), BF16),
            jax.ShapeDtypeStruct((channels, 3 * rank), BF16),
            flat(rank),
        ],
        [scalars] * 3 + [whole()], (filters, bounds, margin_rows, loading), 100000, 100000,
    )

    def coefficients(parts, spectral):
        operands = (coef_lhs,) + ((spectral,) if spectral is not None else ()) + tuple(parts)
        outs = [jax.ShapeDtypeStruct((rank, height * lanes), F32)] + [flat(channels * (height - 1) + PAD)] * (spectral is None)
        return call(
            functools.partial(coef_kernel, height, spectral is not None), outs,
            [whole()] * len(operands), operands, 6 * rank * rows * lanes, 2 * cubes,
        )

    def synthesis(own, other, image=()):
        outs = [flat(rows)] * (2 if image else 1)
        return call(
            functools.partial(spectral_kernel, height), outs, [whole()] * (4 + len(image)),
            (spectral_lhs, own, other, limits, *image), 6 * rank * rows * lanes, 2 * cubes,
        )

    coefs, everything = coefficients(reflected, None)
    terms = chan_terms(coefs)
    squares = jnp.zeros((size, lanes), F32)
    lifted = []
    for index in range(chunks):
        out, squares = call(
            functools.partial(lift_kernel, height, "first"), [flat(per * size), flat(size)], [whole()] * 4,
            (halos[index], reflected[index], lift_lhs, squares), work, duals,
        )
        lifted.append(out)
        if index == 0:
            tied, _ = lax.optimization_barrier((everything, squares))
            below = shift(tied, "facet", -1)
            squares, *terms = lax.optimization_barrier((squares, *terms))
    own, other = chan_terms(squares)
    (spectral,) = synthesis(*terms)
    other, spectral = lax.optimization_barrier((other, spectral))
    scale, scale_above = call(
        functools.partial(scale_kernel, height), [flat(size), flat(reaching)], [whole()] * 3, (w, own, other),
        10 * size * lanes, 16 * size * lanes,
    )
    scale_below = shift(scale_above, "facet", -1)

    partials = [
        call(
            functools.partial(adjoint_kernel, height, index * block), flat(block), [whole()] * 6,
            (lifted[index], interior_lhs, scale, spectral, x, d), 22 * work, 22 * duals,
        )
        for index in range(chunks)
    ]
    image, halos, again = [], [], []
    for index in range(chunks):
        updated, r, ahead = call(
            functools.partial(border_kernel, height, index * per), [flat(block)] * 2 + [flat(packed)], [whole()] * 8,
            (reflected[index], below, next_lhs, border_lhs, scale_below, partials[index], x, d), 22 * work, 22 * duals,
        )
        image.append(updated)
        again.append(r)
        halos.append(shift(ahead, "facet", 1))
    terms = chan_terms(*coefficients(again, spectral))

    squares = jnp.zeros((size, lanes), F32)
    final = []
    for index in range(chunks):
        out, squares = call(
            functools.partial(lift_kernel, height, "second"), [flat(per * size), flat(size)], [whole()] * 6,
            (halos[index], again[index], lift_lhs, squares, lifted[index], scale), work, 2 * duals,
        )
        final.append(out)
    own, other = chan_terms(squares)
    image, spectral = synthesis(*terms, image)

    slab = min(per, 16)
    wavelet = call(
        functools.partial(wavelet_kernel, chunks, height),
        jax.ShapeDtypeStruct((bases, channels, height, lanes), F32),
        [whole()] * (chunks + 3), (*final, w, own, other), rows * lanes * bases, 2 * cubes * bases,
        scratch=[pltpu.VMEM((3, bases, slab, height, lanes), F32), pltpu.SemaphoreType.DMA((3,))],
        out_specs=distant,
    )
    return (
        image.reshape(channels, height, lanes),
        wavelet,
        spectral.reshape(channels, height, lanes),
    )


def solution(mesh):
    in_specs = (
        P("chan", "facet", None),
        P("chan", "facet", None),
        P(None, "facet", None),
        P(),
        P("facet", "chan", None),
        P(),
        P(),
    )
    out_specs = (P("chan", "facet", None), P(None, "chan", "facet", None), P("chan", "facet", None))
    return jax.shard_map(body, mesh=mesh, in_specs=in_specs, out_specs=out_specs, check_vma=False)
```

```python
import functools

import jax
import jax.numpy as jnp
from jax import lax
from jax.experimental import pallas as pl
from jax.experimental.pallas import tpu as pltpu
from jax.sharding import PartitionSpec as P

PRIMAL = 0.5
DUAL = 0.5
F32 = jnp.float32
BF16 = jnp.bfloat16
CHUNKS = 2
GROUP = 32
PAD = 8
VMEM_LIMIT = 24 << 20
REFLECT_LIMIT = 55000000


def shift(value, axis, steps):
    count = lax.axis_size(axis)
    initial, last = (max(0, -steps), min(count, count - steps))
    return lax.ppermute(value, axis, [(source, source + steps) for source in range(initial, last)])


def chan_pairs(value, stride):
    count = lax.axis_size("chan")
    return lax.ppermute(value, "chan", [(source, source ^ stride) for source in range(count)])


def chan_terms(value):
    count = lax.axis_size("chan")
    if count & (count - 1):
        return lax.psum(value, "chan"), jnp.zeros_like(value)
    stride = 1
    other = jnp.zeros_like(value)
    while stride < count:
        if stride > 1:
            value = value + other
        other = chan_pairs(value, stride)
        stride *= 2
    return value, other


def split(value):
    high = value.astype(BF16)
    low = (value - high.astype(F32)).astype(BF16)
    return high, low


def three_lhs(matrix):
    high, low = split(matrix)
    return jnp.concatenate([high, high, low], axis=1)


def three_rhs(value):
    high, low = split(value)
    return jnp.concatenate([high, low, high], axis=0)


def two_lhs(matrix):
    high, low = split(matrix)
    top = jnp.concatenate([high, high], axis=1)
    bottom = jnp.concatenate([low, jnp.zeros_like(low)], axis=1)
    return jnp.concatenate([top, bottom], axis=0)


def two_rhs(value):
    high, low = split(value)
    return jnp.concatenate([high, low], axis=0)


def dot(lhs, rhs):
    return jnp.dot(lhs, rhs, preferred_element_type=F32)


def met_rows(bases, height):
    return [min(height, 8 * (2 * basis // 8 + 1)) for basis in range(bases)]


def setup_kernel(
    filters_ref, bounds_ref, margin_ref, loading_ref,
    lift_ref, inner_ref, outer_ref, next_ref, interior_ref, border_ref, coef_ref, spectral_ref, limits_ref,
):
    bases, taps = filters_ref.shape
    height = taps
    size = bases * height
    facet = lax.axis_index("facet")
    last = margin_ref.shape[0] - 1
    own_margin = margin_ref[facet]
    next_margin = jnp.where(facet < last, margin_ref[jnp.minimum(facet + 1, last)], 0)

    def toeplitz(columns, column, tap_of):
        basis_of, _ = column(lax.broadcasted_iota(jnp.int32, (1, columns), 1))
        matrix = jnp.zeros((2 * height, columns), F32)
        for tap in range(taps):
            values = jnp.zeros((1, columns), F32)
            for basis in range(tap // 2, bases):
                values = jnp.where(basis_of == basis, filters_ref[basis, tap], values)
            matrix = jnp.where(tap_of == tap, values, matrix)
        return matrix

    def grids(columns, column):
        source = lax.broadcasted_iota(jnp.int32, (2 * height, columns), 0)
        return source, column(lax.broadcasted_iota(jnp.int32, (2 * height, columns), 1))[1]

    def dense(index):
        return lax.div(index, height), lax.rem(index, height)

    def reaching(index):
        basis = jnp.zeros_like(index)
        for number in range(1, bases):
            basis = basis + (index >= number * number).astype(jnp.int32)
        return basis, index - basis * basis

    source, target = grids(size, dense)
    borrowed = jnp.where((source < height - 1) & (height - 1 - source <= own_margin), target - source + height - 1, -1)
    own = toeplitz(size, dense, jnp.where(source >= height, target - source + height, borrowed))
    source, target = grids(bases * bases, reaching)
    tap_of = target - source + height
    below = toeplitz(bases * bases, reaching, jnp.where((source >= height) | (height - source <= next_margin), tap_of, -1))

    lift = DUAL * own.T
    lift_ref[...] = three_lhs(lift)
    inner_ref[...] = three_lhs(lift[:, height:])
    met = [
        lift[basis * height : basis * height + count, :height] for basis, count in enumerate(met_rows(bases, height))
    ]
    outer_ref[...] = three_lhs(jnp.concatenate(met, axis=0))
    next_ref[...] = three_lhs(DUAL * below.T)
    interior_ref[...] = two_lhs(own[height:])
    border_ref[...] = two_lhs(below[:height])
    loading = loading_ref[...]
    coef_ref[...] = two_lhs(loading)
    spectral_ref[...] = three_lhs(loading.T)
    row = lax.broadcasted_iota(jnp.int32, limits_ref.shape, 0)
    limits = jnp.zeros(limits_ref.shape, F32)
    for index in range(bounds_ref.shape[0]):
        limits = jnp.where(row == index, bounds_ref[index], limits)
    limits_ref[...] = limits


def pack(source_ref, target_ref, height, first, start=0):
    reach = height - 1
    for channel in range(source_ref.shape[0] // height):
        target_ref[pl.ds(start + channel * reach, reach), :] = source_ref[pl.ds(channel * height + first, reach), :]


def clear_tail(packed_ref):
    packed_ref[pl.ds(packed_ref.shape[0] - PAD, PAD), :] = jnp.zeros((PAD, packed_ref.shape[1]), F32)


def reflect_kernel(height, start, x_ref, d_ref, r_ref, packed_ref, x_buffer, d_buffer, sems):
    rows = pl.ds(start, r_ref.shape[0])
    copies = [
        pltpu.make_async_copy(source.at[rows], target, sems.at[turn])
        for turn, (source, target) in enumerate(((x_ref, x_buffer), (d_ref, d_buffer)))
    ]
    for copy in copies:
        copy.start()
    for copy in copies:
        copy.wait()
    x = x_buffer[...]
    updated = jnp.maximum(x - PRIMAL * (x - d_buffer[...]), 0.0)
    r_ref[...] = 2.0 * updated - x
    pack(r_ref, packed_ref, height, 1)
    clear_tail(packed_ref)


def coef_kernel(height, spectral, lhs_ref, *refs):
    if spectral:
        s_ref, *r_refs, out_ref = refs
    else:
        *r_refs, out_ref, packed_ref = refs
        start = 0
        for r_ref in r_refs:
            pack(r_ref, packed_ref, height, 0, start)
            start += r_ref.shape[0] // height * (height - 1)
        clear_tail(packed_ref)
    rank = out_ref.shape[0]

    def pixels(row):
        parts = [r[pl.ds(row, r.shape[0] // height, stride=height), :] for r in r_refs]
        value = DUAL * jnp.concatenate(parts, axis=0)
        if spectral:
            value = value + s_ref[pl.ds(row, s_ref.shape[0] // height, stride=height), :]
        return value

    lhs = lhs_ref[...]
    lanes = out_ref.shape[1] // height
    for row in range(0, height, 2):
        value = jnp.concatenate([pixels(row), pixels(row + 1)], axis=1)
        both = dot(lhs, two_rhs(value))
        out_ref[:, row * lanes : (row + 2) * lanes] = both[:rank] + both[rank:]


def spectral_kernel(height, lhs_ref, own_ref, other_ref, bounds_ref, *refs):
    image_refs, out_ref = refs[:-1], refs[-1]
    if image_refs:
        image_ref, image_refs = refs[-2], refs[:-2]
        for index, part_ref in enumerate(image_refs):
            image_ref[pl.ds(index * part_ref.shape[0], part_ref.shape[0]), :] = part_ref[...]
    lanes = out_ref.shape[1]
    channels = out_ref.shape[0] // height
    limit = jnp.concatenate([bounds_ref[...]] * 2, axis=1)
    lhs = lhs_ref[...]
    for row in range(0, height, 2):
        span = slice(row * lanes, (row + 2) * lanes)
        total = own_ref[:, span] + other_ref[:, span]
        clipped = jnp.minimum(jnp.maximum(total, -limit), limit)
        both = dot(lhs, three_rhs(clipped))
        out_ref[pl.ds(row, channels, stride=height), :] = both[:, :lanes]
        out_ref[pl.ds(row + 1, channels, stride=height), :] = both[:, lanes:]


def scale_of(weights, own_ref, other_ref):
    return weights / jnp.maximum(jnp.sqrt(own_ref[...] + other_ref[...]), weights)


def scale_kernel(height, weights_ref, own_ref, other_ref, scale_ref, above_ref):
    scale_ref[...] = scale_of(weights_ref[...], own_ref, other_ref)
    for basis in range(weights_ref.shape[0] // height):
        count = 2 * basis + 1
        above_ref[pl.ds(basis * basis, count), :] = scale_ref[pl.ds(basis * height, count), :]


def lift_kernel(height, halo_ref, own_ref, lhs_ref, before_ref, out_ref, squares_ref):
    lhs = lhs_ref[...]
    size = lhs.shape[0]
    lanes = own_ref.shape[1]
    total = before_ref[...]
    for pair in range(0, own_ref.shape[0] // height, 2):
        value = jnp.concatenate(
            [
                jnp.concatenate(
                    [
                        halo_ref[pl.ds(channel * (height - 1), height), :],
                        own_ref[pl.ds(channel * height, height), :],
                    ],
                    axis=0,
                )
                for channel in (pair, pair + 1)
            ],
            axis=1,
        )
        both = dot(lhs, three_rhs(value))
        for half in range(2):
            lifted = both[:, half * lanes : (half + 1) * lanes]
            out_ref[pl.ds((pair + half) * size, size), :] = lifted
            total = total + lifted * lifted
    squares_ref[...] = total


def inner_kernel(height, own_ref, lhs_ref, dual_ref, scale_ref, before_ref, met_ref, free_ref, squares_ref):
    lhs = lhs_ref[...]
    size, lanes = scale_ref.shape
    scale = scale_ref[...]
    counts = met_rows(size // height, height)
    many = sum(counts)
    total = before_ref[...]
    for pair in range(0, own_ref.shape[0] // height, 2):
        value = jnp.concatenate(
            [own_ref[pl.ds(channel * height, height), :] for channel in (pair, pair + 1)], axis=1
        )
        both = dot(lhs, three_rhs(value))
        for half in range(2):
            channel = pair + half
            lifted = both[:, half * lanes : (half + 1) * lanes] + dual_ref[pl.ds(channel * size, size), :] * scale
            met = [lifted[basis * height : basis * height + count] for basis, count in enumerate(counts)]
            free = [
                lifted[basis * height + count : (basis + 1) * height]
                for basis, count in enumerate(counts)
                if count < height
            ]
            met_ref[pl.ds(channel * many, many), :] = jnp.concatenate(met, axis=0)
            free = jnp.concatenate(free, axis=0)
            free_ref[pl.ds(channel * (size - many), size - many), :] = free
            total = total + free * free
    squares_ref[...] = total


def outer_kernel(height, halo_ref, lhs_ref, met_ref, before_ref, free_ref, out_ref, squares_ref):
    lhs = lhs_ref[...]
    many = lhs.shape[0]
    lanes = met_ref.shape[1]
    total = before_ref[:many, :]
    for pair in range(0, met_ref.shape[0] // many, 2):
        value = jnp.concatenate(
            [halo_ref[pl.ds(channel * (height - 1), height), :] for channel in (pair, pair + 1)], axis=1
        )
        both = dot(lhs, three_rhs(value))
        for half in range(2):
            rows = pl.ds((pair + half) * many, many)
            lifted = both[:, half * lanes : (half + 1) * lanes] + met_ref[rows, :]
            out_ref[rows, :] = lifted
            total = total + lifted * lifted
    squares_ref[:many, :] = total
    squares_ref[many:, :] = free_ref[...]


def adjoint_kernel(height, start, dual_ref, lhs_ref, scale_ref, s_ref, x_ref, d_ref, partial_ref):
    size, lanes = scale_ref.shape
    channels = partial_ref.shape[0] // height
    scale = scale_ref[...]
    lhs = lhs_ref[...]
    many = min(GROUP, channels)

    def step(group, carry):
        for pair in range(0, many, 2):
            channel = group * many + pair
            duals = [
                dual_ref[pl.ds(pl.multiple_of((channel + half) * size, size), size), :] * scale for half in range(2)
            ]
            both = dot(lhs, two_rhs(jnp.concatenate(duals, axis=1)))
            spread = both[:height] + both[height:]
            for half in range(2):
                rows = pl.ds(pl.multiple_of((channel + half) * height, height), height)
                cube = pl.ds(pl.multiple_of(start + (channel + half) * height, height), height)
                x, d = x_ref[cube, :], d_ref[cube, :]
                before = jnp.maximum(x - PRIMAL * (x - d), 0.0)
                mine = spread[:, half * lanes : (half + 1) * lanes]
                partial_ref[rows, :] = before - PRIMAL * ((before - d) + s_ref[cube, :] + mine)
        return carry

    lax.fori_loop(0, channels // many, step, 0)


def border_kernel(
    height, start, own_ref, below_ref, next_ref, border_ref, scale_ref, partial_ref, x_ref, d_ref,
    updated_ref, reflected_ref, packed_ref,
):
    lanes = scale_ref.shape[1]
    scale = jnp.concatenate([scale_ref[...]] * 2, axis=1)
    lift_lhs = next_ref[...]
    border_lhs = border_ref[...]
    for pair in range(0, partial_ref.shape[0] // height, 2):
        channels = (pair, pair + 1)
        value = jnp.concatenate(
            [
                jnp.concatenate(
                    [
                        own_ref[pl.ds(channel * height, height), :],
                        below_ref[pl.ds((start + channel) * (height - 1), height), :],
                    ],
                    axis=0,
                )
                for channel in channels
            ],
            axis=1,
        )
        duals = dot(lift_lhs, three_rhs(value)) * scale
        both = dot(border_lhs, two_rhs(duals))
        spread = both[:height] + both[height:]
        for half, channel in enumerate(channels):
            rows = pl.ds(channel * height, height)
            cube = pl.ds((start + channel) * height, height)
            x, d = x_ref[cube, :], d_ref[cube, :]
            before = jnp.maximum(x - PRIMAL * (x - d), 0.0)
            mine = spread[:, half * lanes : (half + 1) * lanes]
            updated = jnp.maximum(partial_ref[rows, :] - PRIMAL * mine, 0.0)
            updated_ref[rows, :] = updated
            reflected_ref[rows, :] = 2.0 * updated - before
    pack(reflected_ref, packed_ref, height, 1)
    clear_tail(packed_ref)


def wavelet_kernel(chunks, height, *refs):
    met_refs, free_refs = refs[:chunks], refs[chunks : 2 * chunks]
    weights_ref, mine_ref, other_ref, out_ref, buffer, sems = refs[2 * chunks :]
    bases = weights_ref.shape[0] // height
    counts = met_rows(bases, height)
    many = sum(counts)
    parts = [weights_ref[pl.ds(basis * height, count), :] for basis, count in enumerate(counts)]
    parts += [
        weights_ref[pl.ds(basis * height + count, height - count), :]
        for basis, count in enumerate(counts)
        if count < height
    ]
    scale = scale_of(jnp.concatenate(parts, axis=0), mine_ref, other_ref)
    rest = scale.shape[0] - many
    slots, block = buffer.shape[0], buffer.shape[2]
    pending = [()] * slots
    turn = 0
    for index, (met_ref, free_ref) in enumerate(zip(met_refs, free_refs)):
        channels = met_ref.shape[0] // many
        for start in range(0, channels, block):
            slot = turn % slots
            for copy in pending[slot]:
                copy.wait()
            for channel in range(block):
                met = met_ref[pl.ds((start + channel) * many, many), :] * scale[:many]
                free = free_ref[pl.ds((start + channel) * rest, rest), :] * scale[many:]
                first = second = 0
                for basis, count in enumerate(counts):
                    buffer[slot, basis, channel, :count] = met[first : first + count]
                    first += count
                    if count < height:
                        buffer[slot, basis, channel, count:] = free[second : second + height - count]
                        second += height - count
            place = pl.ds(index * channels + start, block)
            pending[slot] = [
                pltpu.make_async_copy(buffer.at[slot, basis], out_ref.at[basis, place], sems.at[slot, basis])
                for basis in range(bases)
            ]
            for copy in pending[slot]:
                copy.start()
            turn += 1
    for copies in pending:
        for copy in copies:
            copy.wait()


def whole():
    return pl.BlockSpec(memory_space=pltpu.VMEM)


def call(kernel, outs, ins, operands, flops, nbytes, scratch=(), out_specs=None, limit=VMEM_LIMIT, aliases=None):
    return pl.pallas_call(
        kernel,
        out_shape=outs,
        in_specs=ins,
        out_specs=out_specs if out_specs is not None else jax.tree.map(lambda _: whole(), outs),
        scratch_shapes=scratch,
        input_output_aliases=aliases or {},
        compiler_params=pltpu.CompilerParams(vmem_limit_bytes=limit),
        cost_estimate=pl.CostEstimate(flops=flops, bytes_accessed=nbytes, transcendentals=0),
    )(*operands)


def body(x_start, dirty, weights, filters, basis, bounds, margin_rows):
    channels, height, lanes = x_start.shape
    bases, taps = filters.shape
    rank = bounds.shape[0]
    assert taps == height
    size = bases * height
    reaching = bases * bases
    counts = met_rows(bases, height)
    met = sum(counts)
    free = size - met
    chunks = CHUNKS if channels >= 8 * CHUNKS else 1
    per = channels // chunks
    block = per * height
    rows = channels * height

    def flat(extent):
        return jax.ShapeDtypeStruct((extent, lanes), F32)

    x = x_start.reshape(rows, lanes)
    d = dirty.reshape(rows, lanes)
    w = weights.reshape(size, lanes)
    loading = basis[0].T
    cubes = rows * lanes * 4
    duals = per * size * lanes * 4

    distant = pl.BlockSpec(memory_space=pltpu.HBM)
    scalars = pl.BlockSpec(memory_space=pltpu.SMEM)
    work = 6 * 2 * height * per * size * lanes

    packed = per * (height - 1) + PAD
    reflected, halos = [], []
    for index in range(chunks):
        r, ahead = call(
            functools.partial(reflect_kernel, height, index * block), [flat(block), flat(packed)], [distant] * 2, (x, d),
            4 * block * lanes, 12 * block * lanes,
            scratch=[pltpu.VMEM((block, lanes), F32)] * 2 + [pltpu.SemaphoreType.DMA((2,))], limit=REFLECT_LIMIT,
        )
        reflected.append(r)
        halos.append(shift(ahead, "facet", 1))

    lift_lhs, inner_lhs, outer_lhs, next_lhs, interior_lhs, border_lhs, coef_lhs, spectral_lhs, limits = call(
        setup_kernel,
        [
            jax.ShapeDtypeStruct((size, 6 * height), BF16),
            jax.ShapeDtypeStruct((size, 3 * height), BF16),
            jax.ShapeDtypeStruct((met, 3 * height), BF16),
            jax.ShapeDtypeStruct((reaching, 6 * height), BF16),
            jax.ShapeDtypeStruct((2 * height, 2 * size), BF16),
            jax.ShapeDtypeStruct((2 * height, 2 * reaching), BF16),
            jax.ShapeDtypeStruct((2 * rank, 2 * channels), BF16),
            jax.ShapeDtypeStruct((channels, 3 * rank), BF16),
            flat(rank),
        ],
        [scalars] * 3 + [whole()], (filters, bounds, margin_rows, loading), 100000, 100000,
    )

    def coefficients(parts, spectral):
        operands = (coef_lhs,) + ((spectral,) if spectral is not None else ()) + tuple(parts)
        outs = [jax.ShapeDtypeStruct((rank, height * lanes), F32)] + [flat(channels * (height - 1) + PAD)] * (spectral is None)
        return call(
            functools.partial(coef_kernel, height, spectral is not None), outs,
            [whole()] * len(operands), operands, 6 * rank * rows * lanes, 2 * cubes,
        )

    def synthesis(own, other, image=()):
        outs = [flat(rows)] * (2 if image else 1)
        return call(
            functools.partial(spectral_kernel, height), outs, [whole()] * (4 + len(image)),
            (spectral_lhs, own, other, limits, *image), 6 * rank * rows * lanes, 2 * cubes,
        )

    coefs, everything = coefficients(reflected, None)
    terms = chan_terms(coefs)
    squares = jnp.zeros((size, lanes), F32)
    lifted = []
    for index in range(chunks):
        out, squares = call(
            functools.partial(lift_kernel, height), [flat(per * size), flat(size)], [whole()] * 4,
            (halos[index], reflected[index], lift_lhs, squares), work, duals,
        )
        lifted.append(out)
        if index == 0:
            tied, _ = lax.optimization_barrier((everything, squares))
            below = shift(tied, "facet", -1)
    own, other = chan_terms(squares)
    (spectral,) = synthesis(*terms)
    other, spectral = lax.optimization_barrier((other, spectral))
    scale, scale_above = call(
        functools.partial(scale_kernel, height), [flat(size), flat(reaching)], [whole()] * 3, (w, own, other),
        10 * size * lanes, 16 * size * lanes,
    )
    scale_below = shift(scale_above, "facet", -1)

    partials = [
        call(
            functools.partial(adjoint_kernel, height, index * block), flat(block), [whole()] * 6,
            (lifted[index], interior_lhs, scale, spectral, x, d), 22 * work, 22 * duals,
        )
        for index in range(chunks)
    ]
    image, halos, again = [], [], []
    for index in range(chunks):
        updated, r, ahead = call(
            functools.partial(border_kernel, height, index * per), [flat(block)] * 2 + [flat(packed)], [whole()] * 8,
            (reflected[index], below, next_lhs, border_lhs, scale_below, partials[index], x, d), 22 * work, 22 * duals,
        )
        image.append(updated)
        again.append(r)
        halos.append(shift(ahead, "facet", 1))
    terms = chan_terms(*coefficients(again, spectral))

    squares = jnp.zeros((free, lanes), F32)
    inner, early = [], []
    for index in range(chunks):
        for_halo, done, squares = call(
            functools.partial(inner_kernel, height), [flat(per * met), flat(per * free), flat(free)], [whole()] * 5,
            (again[index], inner_lhs, lifted[index], scale, squares), work, 2 * duals,
        )
        inner.append(for_halo)
        early.append(done)
    apart = squares

    squares = jnp.zeros((size, lanes), F32)
    late = []
    for index in range(chunks):
        out, squares = call(
            functools.partial(outer_kernel, height), [flat(per * met), flat(size)], [whole()] * 5,
            (halos[index], outer_lhs, inner[index], squares, apart), work, 2 * duals,
        )
        late.append(out)
    own, other = chan_terms(squares)
    image, spectral = synthesis(*terms, image)

    slab = min(per, 16)
    wavelet = call(
        functools.partial(wavelet_kernel, chunks, height),
        jax.ShapeDtypeStruct((bases, channels, height, lanes), F32),
        [whole()] * (2 * chunks + 3), (*late, *early, w, own, other), rows * lanes * bases, 2 * cubes * bases,
        scratch=[pltpu.VMEM((3, bases, slab, height, lanes), F32), pltpu.SemaphoreType.DMA((3, bases))],
        out_specs=distant,
    )
    return (
        image.reshape(channels, height, lanes),
        wavelet,
        spectral.reshape(channels, height, lanes),
    )


def solution(mesh):
    in_specs = (
        P("chan", "facet", None),
        P("chan", "facet", None),
        P(None, "facet", None),
        P(),
        P("facet", "chan", None),
        P(),
        P(),
    )
    out_specs = (P("chan", "facet", None), P(None, "chan", "facet", None), P("chan", "facet", None))
    return jax.shard_map(body, mesh=mesh, in_specs=in_specs, out_specs=out_specs, check_vma=False)
```

```python
import functools

import jax
import jax.numpy as jnp
from jax import lax
from jax.experimental import pallas as pl
from jax.experimental.pallas import tpu as pltpu
from jax.sharding import PartitionSpec as P

PRIMAL = 0.5
DUAL = 0.5
F32 = jnp.float32
BF16 = jnp.bfloat16
CHUNKS = 2
GROUP = 32
PAD = 8
STEPS = 2
VMEM_LIMIT = 24 << 20
REFLECT_LIMIT = 55000000


def shift(value, axis, steps):
    count = lax.axis_size(axis)
    initial, last = (max(0, -steps), min(count, count - steps))
    return lax.ppermute(value, axis, [(source, source + steps) for source in range(initial, last)])


def chan_pairs(value, stride):
    count = lax.axis_size("chan")
    return lax.ppermute(value, "chan", [(source, source ^ stride) for source in range(count)])


def chan_terms(value):
    count = lax.axis_size("chan")
    if count & (count - 1):
        return lax.psum(value, "chan"), jnp.zeros_like(value)
    stride = 1
    other = jnp.zeros_like(value)
    while stride < count:
        if stride > 1:
            value = value + other
        other = chan_pairs(value, stride)
        stride *= 2
    return value, other


def split(value):
    high = value.astype(BF16)
    low = (value - high.astype(F32)).astype(BF16)
    return high, low


def three_lhs(matrix):
    high, low = split(matrix)
    return jnp.concatenate([high, high, low], axis=1)


def three_rhs(value):
    high, low = split(value)
    return jnp.concatenate([high, low, high], axis=0)


def two_lhs(matrix):
    high, low = split(matrix)
    top = jnp.concatenate([high, high], axis=1)
    bottom = jnp.concatenate([low, jnp.zeros_like(low)], axis=1)
    return jnp.concatenate([top, bottom], axis=0)


def two_rhs(value):
    high, low = split(value)
    return jnp.concatenate([high, low], axis=0)


def dot(lhs, rhs):
    return jnp.dot(lhs, rhs, preferred_element_type=F32)


def met_rows(bases, height):
    return [min(height, 8 * (2 * basis // 8 + 1)) for basis in range(bases)]


def setup_kernel(
    filters_ref, bounds_ref, margin_ref, loading_ref,
    lift_ref, inner_ref, outer_ref, next_ref, interior_ref, border_ref, coef_ref, spectral_ref, limits_ref,
):
    bases, taps = filters_ref.shape
    height = taps
    size = bases * height
    facet = lax.axis_index("facet")
    last = margin_ref.shape[0] - 1
    own_margin = margin_ref[facet]
    next_margin = jnp.where(facet < last, margin_ref[jnp.minimum(facet + 1, last)], 0)

    def toeplitz(columns, column, tap_of):
        basis_of, _ = column(lax.broadcasted_iota(jnp.int32, (1, columns), 1))
        matrix = jnp.zeros((2 * height, columns), F32)
        for tap in range(taps):
            values = jnp.zeros((1, columns), F32)
            for basis in range(tap // 2, bases):
                values = jnp.where(basis_of == basis, filters_ref[basis, tap], values)
            matrix = jnp.where(tap_of == tap, values, matrix)
        return matrix

    def grids(columns, column):
        source = lax.broadcasted_iota(jnp.int32, (2 * height, columns), 0)
        return source, column(lax.broadcasted_iota(jnp.int32, (2 * height, columns), 1))[1]

    def dense(index):
        return lax.div(index, height), lax.rem(index, height)

    def reaching(index):
        basis = jnp.zeros_like(index)
        for number in range(1, bases):
            basis = basis + (index >= number * number).astype(jnp.int32)
        return basis, index - basis * basis

    source, target = grids(size, dense)
    borrowed = jnp.where((source < height - 1) & (height - 1 - source <= own_margin), target - source + height - 1, -1)
    own = toeplitz(size, dense, jnp.where(source >= height, target - source + height, borrowed))
    source, target = grids(bases * bases, reaching)
    tap_of = target - source + height
    below = toeplitz(bases * bases, reaching, jnp.where((source >= height) | (height - source <= next_margin), tap_of, -1))

    lift = DUAL * own.T
    lift_ref[...] = three_lhs(lift)
    inner_ref[...] = three_lhs(lift[:, height:])
    met = [
        lift[basis * height : basis * height + count, :height] for basis, count in enumerate(met_rows(bases, height))
    ]
    outer_ref[...] = three_lhs(jnp.concatenate(met, axis=0))
    next_ref[...] = three_lhs(DUAL * below.T)
    interior_ref[...] = two_lhs(own[height:])
    border_ref[...] = two_lhs(below[:height])
    loading = loading_ref[...]
    coef_ref[...] = two_lhs(loading)
    spectral_ref[...] = three_lhs(loading.T)
    row = lax.broadcasted_iota(jnp.int32, limits_ref.shape, 0)
    limits = jnp.zeros(limits_ref.shape, F32)
    for index in range(bounds_ref.shape[0]):
        limits = jnp.where(row == index, bounds_ref[index], limits)
    limits_ref[...] = limits


def pack(source_ref, target_ref, height, first, start=0):
    reach = height - 1
    for channel in range(source_ref.shape[0] // height):
        target_ref[pl.ds(start + channel * reach, reach), :] = source_ref[pl.ds(channel * height + first, reach), :]


def clear_tail(packed_ref):
    packed_ref[pl.ds(packed_ref.shape[0] - PAD, PAD), :] = jnp.zeros((PAD, packed_ref.shape[1]), F32)


def reflect_kernel(height, start, x_ref, d_ref, r_ref, packed_ref, x_buffer, d_buffer, sems):
    steps = sems.shape[0]
    block = r_ref.shape[0] // steps
    copies = []
    for step in range(steps):
        here = pl.ds(step * block, block)
        there = pl.ds(start + step * block, block)
        copies.append(
            [
                pltpu.make_async_copy(source.at[there], target.at[here], sems.at[step, turn])
                for turn, (source, target) in enumerate(((x_ref, x_buffer), (d_ref, d_buffer)))
            ]
        )
        for copy in copies[-1]:
            copy.start()
    clear_tail(packed_ref)
    for step in range(steps):
        for copy in copies[step]:
            copy.wait()
        here = pl.ds(step * block, block)
        x = x_buffer[here, :]
        updated = jnp.maximum(x - PRIMAL * (x - d_buffer[here, :]), 0.0)
        r_ref[here, :] = 2.0 * updated - x
        pack(r_ref.at[here], packed_ref, height, 1, step * (block // height) * (height - 1))


def coef_kernel(height, spectral, lhs_ref, *refs):
    if spectral:
        s_ref, *r_refs, out_ref = refs
    else:
        *r_refs, out_ref, packed_ref = refs
        start = 0
        for r_ref in r_refs:
            pack(r_ref, packed_ref, height, 0, start)
            start += r_ref.shape[0] // height * (height - 1)
        clear_tail(packed_ref)
    rank = out_ref.shape[0]

    def pixels(row):
        parts = [r[pl.ds(row, r.shape[0] // height, stride=height), :] for r in r_refs]
        value = DUAL * jnp.concatenate(parts, axis=0)
        if spectral:
            value = value + s_ref[pl.ds(row, s_ref.shape[0] // height, stride=height), :]
        return value

    lhs = lhs_ref[...]
    lanes = out_ref.shape[1] // height
    for row in range(0, height, 2):
        value = jnp.concatenate([pixels(row), pixels(row + 1)], axis=1)
        both = dot(lhs, two_rhs(value))
        out_ref[:, row * lanes : (row + 2) * lanes] = both[:rank] + both[rank:]


def spectral_kernel(height, lhs_ref, own_ref, other_ref, bounds_ref, *refs):
    image_refs, out_ref = refs[:-1], refs[-1]
    if image_refs:
        image_ref, image_refs = refs[-2], refs[:-2]
        for index, part_ref in enumerate(image_refs):
            image_ref[pl.ds(index * part_ref.shape[0], part_ref.shape[0]), :] = part_ref[...]
    lanes = out_ref.shape[1]
    channels = out_ref.shape[0] // height
    limit = jnp.concatenate([bounds_ref[...]] * 2, axis=1)
    lhs = lhs_ref[...]
    for row in range(0, height, 2):
        span = slice(row * lanes, (row + 2) * lanes)
        total = own_ref[:, span] + other_ref[:, span]
        clipped = jnp.minimum(jnp.maximum(total, -limit), limit)
        both = dot(lhs, three_rhs(clipped))
        out_ref[pl.ds(row, channels, stride=height), :] = both[:, :lanes]
        out_ref[pl.ds(row + 1, channels, stride=height), :] = both[:, lanes:]


def scale_of(weights, own_ref, other_ref):
    return weights / jnp.maximum(jnp.sqrt(own_ref[...] + other_ref[...]), weights)


def scale_kernel(height, weights_ref, own_ref, other_ref, scale_ref, above_ref):
    scale_ref[...] = scale_of(weights_ref[...], own_ref, other_ref)
    for basis in range(weights_ref.shape[0] // height):
        count = 2 * basis + 1
        above_ref[pl.ds(basis * basis, count), :] = scale_ref[pl.ds(basis * height, count), :]


def lift_kernel(height, halo_ref, own_ref, lhs_ref, before_ref, out_ref, squares_ref):
    lhs = lhs_ref[...]
    size = lhs.shape[0]
    lanes = own_ref.shape[1]
    total = before_ref[...]
    for pair in range(0, own_ref.shape[0] // height, 2):
        value = jnp.concatenate(
            [
                jnp.concatenate(
                    [
                        halo_ref[pl.ds(channel * (height - 1), height), :],
                        own_ref[pl.ds(channel * height, height), :],
                    ],
                    axis=0,
                )
                for channel in (pair, pair + 1)
            ],
            axis=1,
        )
        both = dot(lhs, three_rhs(value))
        for half in range(2):
            lifted = both[:, half * lanes : (half + 1) * lanes]
            out_ref[pl.ds((pair + half) * size, size), :] = lifted
            total = total + lifted * lifted
    squares_ref[...] = total


def inner_kernel(height, own_ref, lhs_ref, dual_ref, scale_ref, before_ref, met_ref, free_ref, squares_ref):
    lhs = lhs_ref[...]
    size, lanes = scale_ref.shape
    scale = scale_ref[...]
    counts = met_rows(size // height, height)
    many = sum(counts)
    total = before_ref[...]
    for pair in range(0, own_ref.shape[0] // height, 2):
        value = jnp.concatenate(
            [own_ref[pl.ds(channel * height, height), :] for channel in (pair, pair + 1)], axis=1
        )
        both = dot(lhs, three_rhs(value))
        for half in range(2):
            channel = pair + half
            lifted = both[:, half * lanes : (half + 1) * lanes] + dual_ref[pl.ds(channel * size, size), :] * scale
            met = [lifted[basis * height : basis * height + count] for basis, count in enumerate(counts)]
            free = [
                lifted[basis * height + count : (basis + 1) * height]
                for basis, count in enumerate(counts)
                if count < height
            ]
            met_ref[pl.ds(channel * many, many), :] = jnp.concatenate(met, axis=0)
            free = jnp.concatenate(free, axis=0)
            free_ref[pl.ds(channel * (size - many), size - many), :] = free
            total = total + free * free
    squares_ref[...] = total


def outer_kernel(height, halo_ref, lhs_ref, met_ref, before_ref, free_ref, out_ref, squares_ref):
    lhs = lhs_ref[...]
    many = lhs.shape[0]
    lanes = met_ref.shape[1]
    total = before_ref[:many, :]
    for pair in range(0, met_ref.shape[0] // many, 2):
        value = jnp.concatenate(
            [halo_ref[pl.ds(channel * (height - 1), height), :] for channel in (pair, pair + 1)], axis=1
        )
        both = dot(lhs, three_rhs(value))
        for half in range(2):
            rows = pl.ds((pair + half) * many, many)
            lifted = both[:, half * lanes : (half + 1) * lanes] + met_ref[rows, :]
            out_ref[rows, :] = lifted
            total = total + lifted * lifted
    squares_ref[:many, :] = total
    squares_ref[many:, :] = free_ref[...]


def adjoint_kernel(height, start, dual_ref, lhs_ref, scale_ref, s_ref, x_ref, d_ref, partial_ref):
    size, lanes = scale_ref.shape
    channels = partial_ref.shape[0] // height
    scale = scale_ref[...]
    lhs = lhs_ref[...]
    many = min(GROUP, channels)

    def step(group, carry):
        for pair in range(0, many, 2):
            channel = group * many + pair
            duals = [
                dual_ref[pl.ds(pl.multiple_of((channel + half) * size, size), size), :] * scale for half in range(2)
            ]
            both = dot(lhs, two_rhs(jnp.concatenate(duals, axis=1)))
            spread = both[:height] + both[height:]
            for half in range(2):
                rows = pl.ds(pl.multiple_of((channel + half) * height, height), height)
                cube = pl.ds(pl.multiple_of(start + (channel + half) * height, height), height)
                x, d = x_ref[cube, :], d_ref[cube, :]
                before = jnp.maximum(x - PRIMAL * (x - d), 0.0)
                mine = spread[:, half * lanes : (half + 1) * lanes]
                partial_ref[rows, :] = before - PRIMAL * ((before - d) + s_ref[cube, :] + mine)
        return carry

    lax.fori_loop(0, channels // many, step, 0)


def border_kernel(
    height, start, own_ref, below_ref, next_ref, border_ref, scale_ref, partial_ref, x_ref, d_ref,
    updated_ref, reflected_ref, packed_ref,
):
    lanes = scale_ref.shape[1]
    scale = jnp.concatenate([scale_ref[...]] * 2, axis=1)
    lift_lhs = next_ref[...]
    border_lhs = border_ref[...]
    for pair in range(0, partial_ref.shape[0] // height, 2):
        channels = (pair, pair + 1)
        value = jnp.concatenate(
            [
                jnp.concatenate(
                    [
                        own_ref[pl.ds(channel * height, height), :],
                        below_ref[pl.ds((start + channel) * (height - 1), height), :],
                    ],
                    axis=0,
                )
                for channel in channels
            ],
            axis=1,
        )
        duals = dot(lift_lhs, three_rhs(value)) * scale
        both = dot(border_lhs, two_rhs(duals))
        spread = both[:height] + both[height:]
        for half, channel in enumerate(channels):
            rows = pl.ds(channel * height, height)
            cube = pl.ds((start + channel) * height, height)
            x, d = x_ref[cube, :], d_ref[cube, :]
            before = jnp.maximum(x - PRIMAL * (x - d), 0.0)
            mine = spread[:, half * lanes : (half + 1) * lanes]
            updated = jnp.maximum(partial_ref[rows, :] - PRIMAL * mine, 0.0)
            updated_ref[rows, :] = updated
            reflected_ref[rows, :] = 2.0 * updated - before
    pack(reflected_ref, packed_ref, height, 1)
    clear_tail(packed_ref)


def wavelet_kernel(chunks, height, *refs):
    met_refs, free_refs = refs[:chunks], refs[chunks : 2 * chunks]
    weights_ref, mine_ref, other_ref, out_ref, buffer, sems = refs[2 * chunks :]
    bases = weights_ref.shape[0] // height
    counts = met_rows(bases, height)
    many = sum(counts)
    parts = [weights_ref[pl.ds(basis * height, count), :] for basis, count in enumerate(counts)]
    parts += [
        weights_ref[pl.ds(basis * height + count, height - count), :]
        for basis, count in enumerate(counts)
        if count < height
    ]
    scale = scale_of(jnp.concatenate(parts, axis=0), mine_ref, other_ref)
    rest = scale.shape[0] - many
    slots, block = buffer.shape[0], buffer.shape[2]
    pending = [()] * slots
    turn = 0
    for index, (met_ref, free_ref) in enumerate(zip(met_refs, free_refs)):
        channels = met_ref.shape[0] // many
        for start in range(0, channels, block):
            slot = turn % slots
            for copy in pending[slot]:
                copy.wait()
            for channel in range(block):
                met = met_ref[pl.ds((start + channel) * many, many), :] * scale[:many]
                free = free_ref[pl.ds((start + channel) * rest, rest), :] * scale[many:]
                first = second = 0
                for basis, count in enumerate(counts):
                    buffer[slot, basis, channel, :count] = met[first : first + count]
                    first += count
                    if count < height:
                        buffer[slot, basis, channel, count:] = free[second : second + height - count]
                        second += height - count
            place = pl.ds(index * channels + start, block)
            pending[slot] = [
                pltpu.make_async_copy(buffer.at[slot, basis], out_ref.at[basis, place], sems.at[slot, basis])
                for basis in range(bases)
            ]
            for copy in pending[slot]:
                copy.start()
            turn += 1
    for copies in pending:
        for copy in copies:
            copy.wait()


def whole():
    return pl.BlockSpec(memory_space=pltpu.VMEM)


def call(kernel, outs, ins, operands, flops, nbytes, scratch=(), out_specs=None, limit=VMEM_LIMIT, aliases=None):
    return pl.pallas_call(
        kernel,
        out_shape=outs,
        in_specs=ins,
        out_specs=out_specs if out_specs is not None else jax.tree.map(lambda _: whole(), outs),
        scratch_shapes=scratch,
        input_output_aliases=aliases or {},
        compiler_params=pltpu.CompilerParams(vmem_limit_bytes=limit),
        cost_estimate=pl.CostEstimate(flops=flops, bytes_accessed=nbytes, transcendentals=0),
    )(*operands)


def body(x_start, dirty, weights, filters, basis, bounds, margin_rows):
    channels, height, lanes = x_start.shape
    bases, taps = filters.shape
    rank = bounds.shape[0]
    assert taps == height
    size = bases * height
    reaching = bases * bases
    counts = met_rows(bases, height)
    met = sum(counts)
    free = size - met
    chunks = CHUNKS if channels >= 8 * CHUNKS else 1
    per = channels // chunks
    block = per * height
    rows = channels * height

    def flat(extent):
        return jax.ShapeDtypeStruct((extent, lanes), F32)

    x = x_start.reshape(rows, lanes)
    d = dirty.reshape(rows, lanes)
    w = weights.reshape(size, lanes)
    loading = basis[0].T
    cubes = rows * lanes * 4
    duals = per * size * lanes * 4

    distant = pl.BlockSpec(memory_space=pltpu.HBM)
    scalars = pl.BlockSpec(memory_space=pltpu.SMEM)
    work = 6 * 2 * height * per * size * lanes

    packed = per * (height - 1) + PAD
    reflected, halos = [], []
    for index in range(chunks):
        r, ahead = call(
            functools.partial(reflect_kernel, height, index * block), [flat(block), flat(packed)], [distant] * 2, (x, d),
            4 * block * lanes, 12 * block * lanes,
            scratch=[pltpu.VMEM((block, lanes), F32)] * 2 + [pltpu.SemaphoreType.DMA((STEPS, 2))], limit=REFLECT_LIMIT,
        )
        reflected.append(r)
        halos.append(shift(ahead, "facet", 1))

    lift_lhs, inner_lhs, outer_lhs, next_lhs, interior_lhs, border_lhs, coef_lhs, spectral_lhs, limits = call(
        setup_kernel,
        [
            jax.ShapeDtypeStruct((size, 6 * height), BF16),
            jax.ShapeDtypeStruct((size, 3 * height), BF16),
            jax.ShapeDtypeStruct((met, 3 * height), BF16),
            jax.ShapeDtypeStruct((reaching, 6 * height), BF16),
            jax.ShapeDtypeStruct((2 * height, 2 * size), BF16),
            jax.ShapeDtypeStruct((2 * height, 2 * reaching), BF16),
            jax.ShapeDtypeStruct((2 * rank, 2 * channels), BF16),
            jax.ShapeDtypeStruct((channels, 3 * rank), BF16),
            flat(rank),
        ],
        [scalars] * 3 + [whole()], (filters, bounds, margin_rows, loading), 100000, 100000,
    )

    def coefficients(parts, spectral):
        operands = (coef_lhs,) + ((spectral,) if spectral is not None else ()) + tuple(parts)
        outs = [jax.ShapeDtypeStruct((rank, height * lanes), F32)] + [flat(channels * (height - 1) + PAD)] * (spectral is None)
        return call(
            functools.partial(coef_kernel, height, spectral is not None), outs,
            [whole()] * len(operands), operands, 6 * rank * rows * lanes, 2 * cubes,
        )

    def synthesis(own, other, image=()):
        outs = [flat(rows)] * (2 if image else 1)
        return call(
            functools.partial(spectral_kernel, height), outs, [whole()] * (4 + len(image)),
            (spectral_lhs, own, other, limits, *image), 6 * rank * rows * lanes, 2 * cubes,
        )

    coefs, everything = coefficients(reflected, None)
    terms = chan_terms(coefs)
    squares = jnp.zeros((size, lanes), F32)
    lifted = []
    for index in range(chunks):
        out, squares = call(
            functools.partial(lift_kernel, height), [flat(per * size), flat(size)], [whole()] * 4,
            (halos[index], reflected[index], lift_lhs, squares), work, duals,
        )
        lifted.append(out)
        if index == 0:
            tied, _ = lax.optimization_barrier((everything, squares))
            below = shift(tied, "facet", -1)
    own, other = chan_terms(squares)
    (spectral,) = synthesis(*terms)
    other, spectral = lax.optimization_barrier((other, spectral))
    scale, scale_above = call(
        functools.partial(scale_kernel, height), [flat(size), flat(reaching)], [whole()] * 3, (w, own, other),
        10 * size * lanes, 16 * size * lanes,
    )
    scale_below = shift(scale_above, "facet", -1)

    partials = [
        call(
            functools.partial(adjoint_kernel, height, index * block), flat(block), [whole()] * 6,
            (lifted[index], interior_lhs, scale, spectral, x, d), 22 * work, 22 * duals,
        )
        for index in range(chunks)
    ]
    image, halos, again = [], [], []
    for index in range(chunks):
        updated, r, ahead = call(
            functools.partial(border_kernel, height, index * per), [flat(block)] * 2 + [flat(packed)], [whole()] * 8,
            (reflected[index], below, next_lhs, border_lhs, scale_below, partials[index], x, d), 22 * work, 22 * duals,
        )
        image.append(updated)
        again.append(r)
        halos.append(shift(ahead, "facet", 1))
    terms = chan_terms(*coefficients(again, spectral))

    squares = jnp.zeros((free, lanes), F32)
    inner, early = [], []
    for index in range(chunks):
        for_halo, done, squares = call(
            functools.partial(inner_kernel, height), [flat(per * met), flat(per * free), flat(free)], [whole()] * 5,
            (again[index], inner_lhs, lifted[index], scale, squares), work, 2 * duals,
        )
        inner.append(for_halo)
        early.append(done)
    apart = squares

    squares = jnp.zeros((size, lanes), F32)
    late = []
    for index in range(chunks):
        out, squares = call(
            functools.partial(outer_kernel, height), [flat(per * met), flat(size)], [whole()] * 5,
            (halos[index], outer_lhs, inner[index], squares, apart), work, 2 * duals,
        )
        late.append(out)
    own, other = chan_terms(squares)
    image, spectral = synthesis(*terms, image)

    slab = min(per, 16)
    wavelet = call(
        functools.partial(wavelet_kernel, chunks, height),
        jax.ShapeDtypeStruct((bases, channels, height, lanes), F32),
        [whole()] * (2 * chunks + 3), (*late, *early, w, own, other), rows * lanes * bases, 2 * cubes * bases,
        scratch=[pltpu.VMEM((3, bases, slab, height, lanes), F32), pltpu.SemaphoreType.DMA((3, bases))],
        out_specs=distant,
    )
    return (
        image.reshape(channels, height, lanes),
        wavelet,
        spectral.reshape(channels, height, lanes),
    )


def solution(mesh):
    in_specs = (
        P("chan", "facet", None),
        P("chan", "facet", None),
        P(None, "facet", None),
        P(),
        P("facet", "chan", None),
        P(),
        P(),
    )
    out_specs = (P("chan", "facet", None), P(None, "chan", "facet", None), P("chan", "facet", None))
    return jax.shard_map(body, mesh=mesh, in_specs=in_specs, out_specs=out_specs, check_vma=False)
```

```python
import functools

import jax
import jax.numpy as jnp
from jax import lax
from jax.experimental import pallas as pl
from jax.experimental.pallas import tpu as pltpu
from jax.sharding import PartitionSpec as P

PRIMAL = 0.5
DUAL = 0.5
F32 = jnp.float32
BF16 = jnp.bfloat16
CHUNKS = 2
GROUP = 64
PAD = 8
STEPS = 2
VMEM_LIMIT = 24 << 20
REFLECT_LIMIT = 55000000


def shift(value, axis, steps):
    count = lax.axis_size(axis)
    initial, last = (max(0, -steps), min(count, count - steps))
    return lax.ppermute(value, axis, [(source, source + steps) for source in range(initial, last)])


def chan_pairs(value, stride):
    count = lax.axis_size("chan")
    return lax.ppermute(value, "chan", [(source, source ^ stride) for source in range(count)])


def chan_terms(value):
    count = lax.axis_size("chan")
    if count & (count - 1):
        return lax.psum(value, "chan"), jnp.zeros_like(value)
    stride = 1
    other = jnp.zeros_like(value)
    while stride < count:
        if stride > 1:
            value = value + other
        other = chan_pairs(value, stride)
        stride *= 2
    return value, other


def split(value):
    high = value.astype(BF16)
    low = (value - high.astype(F32)).astype(BF16)
    return high, low


def three_lhs(matrix):
    high, low = split(matrix)
    return jnp.concatenate([high, high, low], axis=1)


def three_rhs(value):
    high, low = split(value)
    return jnp.concatenate([high, low, high], axis=0)


def two_lhs(matrix):
    high, low = split(matrix)
    top = jnp.concatenate([high, high], axis=1)
    bottom = jnp.concatenate([low, jnp.zeros_like(low)], axis=1)
    return jnp.concatenate([top, bottom], axis=0)


def two_rhs(value):
    high, low = split(value)
    return jnp.concatenate([high, low], axis=0)


def dot(lhs, rhs):
    return jnp.dot(lhs, rhs, preferred_element_type=F32)


def met_rows(bases, height):
    return [min(height, 8 * (2 * basis // 8 + 1)) for basis in range(bases)]


def setup_kernel(
    filters_ref, bounds_ref, margin_ref, loading_ref,
    lift_ref, inner_ref, outer_ref, next_ref, interior_ref, border_ref, coef_ref, spectral_ref, limits_ref,
):
    bases, taps = filters_ref.shape
    height = taps
    size = bases * height
    facet = lax.axis_index("facet")
    last = margin_ref.shape[0] - 1
    own_margin = margin_ref[facet]
    next_margin = jnp.where(facet < last, margin_ref[jnp.minimum(facet + 1, last)], 0)

    def toeplitz(columns, column, tap_of):
        basis_of, _ = column(lax.broadcasted_iota(jnp.int32, (1, columns), 1))
        matrix = jnp.zeros((2 * height, columns), F32)
        for tap in range(taps):
            values = jnp.zeros((1, columns), F32)
            for basis in range(tap // 2, bases):
                values = jnp.where(basis_of == basis, filters_ref[basis, tap], values)
            matrix = jnp.where(tap_of == tap, values, matrix)
        return matrix

    def grids(columns, column):
        source = lax.broadcasted_iota(jnp.int32, (2 * height, columns), 0)
        return source, column(lax.broadcasted_iota(jnp.int32, (2 * height, columns), 1))[1]

    def dense(index):
        return lax.div(index, height), lax.rem(index, height)

    def reaching(index):
        basis = jnp.zeros_like(index)
        for number in range(1, bases):
            basis = basis + (index >= number * number).astype(jnp.int32)
        return basis, index - basis * basis

    source, target = grids(size, dense)
    borrowed = jnp.where((source < height - 1) & (height - 1 - source <= own_margin), target - source + height - 1, -1)
    own = toeplitz(size, dense, jnp.where(source >= height, target - source + height, borrowed))
    source, target = grids(bases * bases, reaching)
    tap_of = target - source + height
    below = toeplitz(bases * bases, reaching, jnp.where((source >= height) | (height - source <= next_margin), tap_of, -1))

    lift = DUAL * own.T
    lift_ref[...] = three_lhs(lift)
    inner_ref[...] = three_lhs(lift[:, height:])
    met = [
        lift[basis * height : basis * height + count, :height] for basis, count in enumerate(met_rows(bases, height))
    ]
    outer_ref[...] = three_lhs(jnp.concatenate(met, axis=0))
    next_ref[...] = three_lhs(DUAL * below.T)
    interior_ref[...] = two_lhs(own[height:])
    border_ref[...] = two_lhs(below[:height])
    loading = loading_ref[...]
    coef_ref[...] = two_lhs(loading)
    spectral_ref[...] = three_lhs(loading.T)
    row = lax.broadcasted_iota(jnp.int32, limits_ref.shape, 0)
    limits = jnp.zeros(limits_ref.shape, F32)
    for index in range(bounds_ref.shape[0]):
        limits = jnp.where(row == index, bounds_ref[index], limits)
    limits_ref[...] = limits


def pack(source_ref, target_ref, height, first, start=0):
    reach = height - 1
    for channel in range(source_ref.shape[0] // height):
        target_ref[pl.ds(start + channel * reach, reach), :] = source_ref[pl.ds(channel * height + first, reach), :]


def clear_tail(packed_ref):
    packed_ref[pl.ds(packed_ref.shape[0] - PAD, PAD), :] = jnp.zeros((PAD, packed_ref.shape[1]), F32)


def reflect_kernel(height, start, x_ref, d_ref, r_ref, packed_ref, x_buffer, d_buffer, sems):
    steps = sems.shape[0]
    block = r_ref.shape[0] // steps
    copies = []
    for step in range(steps):
        here = pl.ds(step * block, block)
        there = pl.ds(start + step * block, block)
        copies.append(
            [
                pltpu.make_async_copy(source.at[there], target.at[here], sems.at[step, turn])
                for turn, (source, target) in enumerate(((x_ref, x_buffer), (d_ref, d_buffer)))
            ]
        )
        for copy in copies[-1]:
            copy.start()
    clear_tail(packed_ref)
    for step in range(steps):
        for copy in copies[step]:
            copy.wait()
        here = pl.ds(step * block, block)
        x = x_buffer[here, :]
        updated = jnp.maximum(x - PRIMAL * (x - d_buffer[here, :]), 0.0)
        r_ref[here, :] = 2.0 * updated - x
        pack(r_ref.at[here], packed_ref, height, 1, step * (block // height) * (height - 1))


def coef_kernel(height, spectral, lhs_ref, *refs):
    if spectral:
        s_ref, *r_refs, out_ref = refs
    else:
        *r_refs, out_ref, packed_ref = refs
        start = 0
        for r_ref in r_refs:
            pack(r_ref, packed_ref, height, 0, start)
            start += r_ref.shape[0] // height * (height - 1)
        clear_tail(packed_ref)
    rank = out_ref.shape[0]

    def pixels(row):
        parts = [r[pl.ds(row, r.shape[0] // height, stride=height), :] for r in r_refs]
        value = DUAL * jnp.concatenate(parts, axis=0)
        if spectral:
            value = value + s_ref[pl.ds(row, s_ref.shape[0] // height, stride=height), :]
        return value

    lhs = lhs_ref[...]
    lanes = out_ref.shape[1] // height
    for row in range(0, height, 2):
        value = jnp.concatenate([pixels(row), pixels(row + 1)], axis=1)
        both = dot(lhs, two_rhs(value))
        out_ref[:, row * lanes : (row + 2) * lanes] = both[:rank] + both[rank:]


def spectral_kernel(height, lhs_ref, own_ref, other_ref, bounds_ref, *refs):
    image_refs, out_ref = refs[:-1], refs[-1]
    if image_refs:
        image_ref, image_refs = refs[-2], refs[:-2]
        for index, part_ref in enumerate(image_refs):
            image_ref[pl.ds(index * part_ref.shape[0], part_ref.shape[0]), :] = part_ref[...]
    lanes = out_ref.shape[1]
    channels = out_ref.shape[0] // height
    limit = jnp.concatenate([bounds_ref[...]] * 2, axis=1)
    lhs = lhs_ref[...]
    for row in range(0, height, 2):
        span = slice(row * lanes, (row + 2) * lanes)
        total = own_ref[:, span] + other_ref[:, span]
        clipped = jnp.minimum(jnp.maximum(total, -limit), limit)
        both = dot(lhs, three_rhs(clipped))
        out_ref[pl.ds(row, channels, stride=height), :] = both[:, :lanes]
        out_ref[pl.ds(row + 1, channels, stride=height), :] = both[:, lanes:]


def scale_of(weights, own_ref, other_ref):
    return weights / jnp.maximum(jnp.sqrt(own_ref[...] + other_ref[...]), weights)


def scale_kernel(height, weights_ref, own_ref, other_ref, scale_ref, above_ref):
    scale_ref[...] = scale_of(weights_ref[...], own_ref, other_ref)
    for basis in range(weights_ref.shape[0] // height):
        count = 2 * basis + 1
        above_ref[pl.ds(basis * basis, count), :] = scale_ref[pl.ds(basis * height, count), :]


def lift_kernel(height, halo_ref, own_ref, lhs_ref, before_ref, out_ref, squares_ref):
    lhs = lhs_ref[...]
    size = lhs.shape[0]
    lanes = own_ref.shape[1]
    total = before_ref[...]
    for pair in range(0, own_ref.shape[0] // height, 2):
        value = jnp.concatenate(
            [
                jnp.concatenate(
                    [
                        halo_ref[pl.ds(channel * (height - 1), height), :],
                        own_ref[pl.ds(channel * height, height), :],
                    ],
                    axis=0,
                )
                for channel in (pair, pair + 1)
            ],
            axis=1,
        )
        both = dot(lhs, three_rhs(value))
        for half in range(2):
            lifted = both[:, half * lanes : (half + 1) * lanes]
            out_ref[pl.ds((pair + half) * size, size), :] = lifted
            total = total + lifted * lifted
    squares_ref[...] = total


def inner_kernel(height, own_ref, lhs_ref, dual_ref, scale_ref, before_ref, met_ref, free_ref, squares_ref):
    lhs = lhs_ref[...]
    size, lanes = scale_ref.shape
    scale = scale_ref[...]
    counts = met_rows(size // height, height)
    many = sum(counts)
    total = before_ref[...]
    for pair in range(0, own_ref.shape[0] // height, 2):
        value = jnp.concatenate(
            [own_ref[pl.ds(channel * height, height), :] for channel in (pair, pair + 1)], axis=1
        )
        both = dot(lhs, three_rhs(value))
        for half in range(2):
            channel = pair + half
            lifted = both[:, half * lanes : (half + 1) * lanes] + dual_ref[pl.ds(channel * size, size), :] * scale
            met = [lifted[basis * height : basis * height + count] for basis, count in enumerate(counts)]
            free = [
                lifted[basis * height + count : (basis + 1) * height]
                for basis, count in enumerate(counts)
                if count < height
            ]
            met_ref[pl.ds(channel * many, many), :] = jnp.concatenate(met, axis=0)
            free = jnp.concatenate(free, axis=0)
            free_ref[pl.ds(channel * (size - many), size - many), :] = free
            total = total + free * free
    squares_ref[...] = total


def outer_kernel(height, halo_ref, lhs_ref, met_ref, before_ref, free_ref, out_ref, squares_ref):
    lhs = lhs_ref[...]
    many = lhs.shape[0]
    lanes = met_ref.shape[1]
    total = before_ref[:many, :]
    for pair in range(0, met_ref.shape[0] // many, 2):
        value = jnp.concatenate(
            [halo_ref[pl.ds(channel * (height - 1), height), :] for channel in (pair, pair + 1)], axis=1
        )
        both = dot(lhs, three_rhs(value))
        for half in range(2):
            rows = pl.ds((pair + half) * many, many)
            lifted = both[:, half * lanes : (half + 1) * lanes] + met_ref[rows, :]
            out_ref[rows, :] = lifted
            total = total + lifted * lifted
    squares_ref[:many, :] = total
    squares_ref[many:, :] = free_ref[...]


def adjoint_kernel(height, start, dual_ref, lhs_ref, scale_ref, s_ref, x_ref, d_ref, partial_ref):
    size, lanes = scale_ref.shape
    channels = partial_ref.shape[0] // height
    scale = scale_ref[...]
    lhs = lhs_ref[...]
    many = min(GROUP, channels)

    def step(group, carry):
        for pair in range(0, many, 2):
            channel = group * many + pair
            duals = [
                dual_ref[pl.ds(pl.multiple_of((channel + half) * size, size), size), :] * scale for half in range(2)
            ]
            both = dot(lhs, two_rhs(jnp.concatenate(duals, axis=1)))
            spread = both[:height] + both[height:]
            for half in range(2):
                rows = pl.ds(pl.multiple_of((channel + half) * height, height), height)
                cube = pl.ds(pl.multiple_of(start + (channel + half) * height, height), height)
                x, d = x_ref[cube, :], d_ref[cube, :]
                before = jnp.maximum(x - PRIMAL * (x - d), 0.0)
                mine = spread[:, half * lanes : (half + 1) * lanes]
                partial_ref[rows, :] = before - PRIMAL * ((before - d) + s_ref[cube, :] + mine)
        return carry

    lax.fori_loop(0, channels // many, step, 0)


def border_kernel(
    height, start, own_ref, below_ref, next_ref, border_ref, scale_ref, partial_ref, x_ref, d_ref,
    updated_ref, reflected_ref, packed_ref,
):
    lanes = scale_ref.shape[1]
    scale = jnp.concatenate([scale_ref[...]] * 2, axis=1)
    lift_lhs = next_ref[...]
    border_lhs = border_ref[...]
    for pair in range(0, partial_ref.shape[0] // height, 2):
        channels = (pair, pair + 1)
        value = jnp.concatenate(
            [
                jnp.concatenate(
                    [
                        own_ref[pl.ds(channel * height, height), :],
                        below_ref[pl.ds((start + channel) * (height - 1), height), :],
                    ],
                    axis=0,
                )
                for channel in channels
            ],
            axis=1,
        )
        duals = dot(lift_lhs, three_rhs(value)) * scale
        both = dot(border_lhs, two_rhs(duals))
        spread = both[:height] + both[height:]
        for half, channel in enumerate(channels):
            rows = pl.ds(channel * height, height)
            cube = pl.ds((start + channel) * height, height)
            x, d = x_ref[cube, :], d_ref[cube, :]
            before = jnp.maximum(x - PRIMAL * (x - d), 0.0)
            mine = spread[:, half * lanes : (half + 1) * lanes]
            updated = jnp.maximum(partial_ref[rows, :] - PRIMAL * mine, 0.0)
            updated_ref[rows, :] = updated
            reflected_ref[rows, :] = 2.0 * updated - before
    pack(reflected_ref, packed_ref, height, 1)
    clear_tail(packed_ref)


def wavelet_kernel(chunks, height, *refs):
    met_refs, free_refs = refs[:chunks], refs[chunks : 2 * chunks]
    weights_ref, mine_ref, other_ref, out_ref, buffer, sems = refs[2 * chunks :]
    bases = weights_ref.shape[0] // height
    counts = met_rows(bases, height)
    many = sum(counts)
    parts = [weights_ref[pl.ds(basis * height, count), :] for basis, count in enumerate(counts)]
    parts += [
        weights_ref[pl.ds(basis * height + count, height - count), :]
        for basis, count in enumerate(counts)
        if count < height
    ]
    scale = scale_of(jnp.concatenate(parts, axis=0), mine_ref, other_ref)
    rest = scale.shape[0] - many
    slots, block = buffer.shape[0], buffer.shape[2]
    pending = [()] * slots
    turn = 0
    for index, (met_ref, free_ref) in enumerate(zip(met_refs, free_refs)):
        channels = met_ref.shape[0] // many
        for start in range(0, channels, block):
            slot = turn % slots
            for copy in pending[slot]:
                copy.wait()
            for channel in range(block):
                met = met_ref[pl.ds((start + channel) * many, many), :] * scale[:many]
                free = free_ref[pl.ds((start + channel) * rest, rest), :] * scale[many:]
                first = second = 0
                for basis, count in enumerate(counts):
                    buffer[slot, basis, channel, :count] = met[first : first + count]
                    first += count
                    if count < height:
                        buffer[slot, basis, channel, count:] = free[second : second + height - count]
                        second += height - count
            place = pl.ds(index * channels + start, block)
            pending[slot] = [
                pltpu.make_async_copy(buffer.at[slot, basis], out_ref.at[basis, place], sems.at[slot, basis])
                for basis in range(bases)
            ]
            for copy in pending[slot]:
                copy.start()
            turn += 1
    for copies in pending:
        for copy in copies:
            copy.wait()


def whole():
    return pl.BlockSpec(memory_space=pltpu.VMEM)


def call(kernel, outs, ins, operands, flops, nbytes, scratch=(), out_specs=None, limit=VMEM_LIMIT, aliases=None):
    return pl.pallas_call(
        kernel,
        out_shape=outs,
        in_specs=ins,
        out_specs=out_specs if out_specs is not None else jax.tree.map(lambda _: whole(), outs),
        scratch_shapes=scratch,
        input_output_aliases=aliases or {},
        compiler_params=pltpu.CompilerParams(vmem_limit_bytes=limit),
        cost_estimate=pl.CostEstimate(flops=flops, bytes_accessed=nbytes, transcendentals=0),
    )(*operands)


def body(x_start, dirty, weights, filters, basis, bounds, margin_rows):
    channels, height, lanes = x_start.shape
    bases, taps = filters.shape
    rank = bounds.shape[0]
    assert taps == height
    size = bases * height
    reaching = bases * bases
    counts = met_rows(bases, height)
    met = sum(counts)
    free = size - met
    chunks = CHUNKS if channels >= 8 * CHUNKS else 1
    per = channels // chunks
    block = per * height
    rows = channels * height

    def flat(extent):
        return jax.ShapeDtypeStruct((extent, lanes), F32)

    x = x_start.reshape(rows, lanes)
    d = dirty.reshape(rows, lanes)
    w = weights.reshape(size, lanes)
    loading = basis[0].T
    cubes = rows * lanes * 4
    duals = per * size * lanes * 4

    distant = pl.BlockSpec(memory_space=pltpu.HBM)
    scalars = pl.BlockSpec(memory_space=pltpu.SMEM)
    work = 6 * 2 * height * per * size * lanes

    packed = per * (height - 1) + PAD
    reflected, halos = [], []
    for index in range(chunks):
        r, ahead = call(
            functools.partial(reflect_kernel, height, index * block), [flat(block), flat(packed)], [distant] * 2, (x, d),
            4 * block * lanes, 12 * block * lanes,
            scratch=[pltpu.VMEM((block, lanes), F32)] * 2 + [pltpu.SemaphoreType.DMA((STEPS, 2))], limit=REFLECT_LIMIT,
        )
        reflected.append(r)
        halos.append(shift(ahead, "facet", 1))

    lift_lhs, inner_lhs, outer_lhs, next_lhs, interior_lhs, border_lhs, coef_lhs, spectral_lhs, limits = call(
        setup_kernel,
        [
            jax.ShapeDtypeStruct((size, 6 * height), BF16),
            jax.ShapeDtypeStruct((size, 3 * height), BF16),
            jax.ShapeDtypeStruct((met, 3 * height), BF16),
            jax.ShapeDtypeStruct((reaching, 6 * height), BF16),
            jax.ShapeDtypeStruct((2 * height, 2 * size), BF16),
            jax.ShapeDtypeStruct((2 * height, 2 * reaching), BF16),
            jax.ShapeDtypeStruct((2 * rank, 2 * channels), BF16),
            jax.ShapeDtypeStruct((channels, 3 * rank), BF16),
            flat(rank),
        ],
        [scalars] * 3 + [whole()], (filters, bounds, margin_rows, loading), 100000, 100000,
    )

    def coefficients(parts, spectral):
        operands = (coef_lhs,) + ((spectral,) if spectral is not None else ()) + tuple(parts)
        outs = [jax.ShapeDtypeStruct((rank, height * lanes), F32)] + [flat(channels * (height - 1) + PAD)] * (spectral is None)
        return call(
            functools.partial(coef_kernel, height, spectral is not None), outs,
            [whole()] * len(operands), operands, 6 * rank * rows * lanes, 2 * cubes,
        )

    def synthesis(own, other, image=()):
        outs = [flat(rows)] * (2 if image else 1)
        return call(
            functools.partial(spectral_kernel, height), outs, [whole()] * (4 + len(image)),
            (spectral_lhs, own, other, limits, *image), 6 * rank * rows * lanes, 2 * cubes,
        )

    coefs, everything = coefficients(reflected, None)
    terms = chan_terms(coefs)
    squares = jnp.zeros((size, lanes), F32)
    lifted = []
    for index in range(chunks):
        out, squares = call(
            functools.partial(lift_kernel, height), [flat(per * size), flat(size)], [whole()] * 4,
            (halos[index], reflected[index], lift_lhs, squares), work, duals,
        )
        lifted.append(out)
        if index == 0:
            tied, _ = lax.optimization_barrier((everything, squares))
            below = shift(tied, "facet", -1)
    own, other = chan_terms(squares)
    (spectral,) = synthesis(*terms)
    other, spectral = lax.optimization_barrier((other, spectral))
    scale, scale_above = call(
        functools.partial(scale_kernel, height), [flat(size), flat(reaching)], [whole()] * 3, (w, own, other),
        10 * size * lanes, 16 * size * lanes,
    )
    scale_below = shift(scale_above, "facet", -1)

    partials = [
        call(
            functools.partial(adjoint_kernel, height, index * block), flat(block), [whole()] * 6,
            (lifted[index], interior_lhs, scale, spectral, x, d), 22 * work, 22 * duals,
        )
        for index in range(chunks)
    ]
    image, halos, again = [], [], []
    for index in range(chunks):
        updated, r, ahead = call(
            functools.partial(border_kernel, height, index * per), [flat(block)] * 2 + [flat(packed)], [whole()] * 8,
            (reflected[index], below, next_lhs, border_lhs, scale_below, partials[index], x, d), 22 * work, 22 * duals,
        )
        image.append(updated)
        again.append(r)
        halos.append(shift(ahead, "facet", 1))
    terms = chan_terms(*coefficients(again, spectral))

    squares = jnp.zeros((free, lanes), F32)
    inner, early = [], []
    for index in range(chunks):
        for_halo, done, squares = call(
            functools.partial(inner_kernel, height), [flat(per * met), flat(per * free), flat(free)], [whole()] * 5,
            (again[index], inner_lhs, lifted[index], scale, squares), work, 2 * duals,
        )
        inner.append(for_halo)
        early.append(done)
    apart = squares

    squares = jnp.zeros((size, lanes), F32)
    late = []
    for index in range(chunks):
        out, squares = call(
            functools.partial(outer_kernel, height), [flat(per * met), flat(size)], [whole()] * 5,
            (halos[index], outer_lhs, inner[index], squares, apart), work, 2 * duals,
        )
        late.append(out)
    own, other = chan_terms(squares)
    image, spectral = synthesis(*terms, image)

    slab = min(per, 16)
    wavelet = call(
        functools.partial(wavelet_kernel, chunks, height),
        jax.ShapeDtypeStruct((bases, channels, height, lanes), F32),
        [whole()] * (2 * chunks + 3), (*late, *early, w, own, other), rows * lanes * bases, 2 * cubes * bases,
        scratch=[pltpu.VMEM((3, bases, slab, height, lanes), F32), pltpu.SemaphoreType.DMA((3, bases))],
        out_specs=distant,
    )
    return (
        image.reshape(channels, height, lanes),
        wavelet,
        spectral.reshape(channels, height, lanes),
    )


def solution(mesh):
    in_specs = (
        P("chan", "facet", None),
        P("chan", "facet", None),
        P(None, "facet", None),
        P(),
        P("facet", "chan", None),
        P(),
        P(),
    )
    out_specs = (P("chan", "facet", None), P(None, "chan", "facet", None), P("chan", "facet", None))
    return jax.shard_map(body, mesh=mesh, in_specs=in_specs, out_specs=out_specs, check_vma=False)
```

```python
import functools

import jax
import jax.numpy as jnp
from jax import lax
from jax.experimental import pallas as pl
from jax.experimental.pallas import tpu as pltpu
from jax.sharding import PartitionSpec as P

PRIMAL = 0.5
DUAL = 0.5
F32 = jnp.float32
BF16 = jnp.bfloat16
CHUNKS = 2
GROUP = 32
PAD = 8
STEPS = 2
VMEM_LIMIT = 24 << 20
REFLECT_LIMIT = 55000000


def shift(value, axis, steps):
    count = lax.axis_size(axis)
    initial, last = (max(0, -steps), min(count, count - steps))
    return lax.ppermute(value, axis, [(source, source + steps) for source in range(initial, last)])


def chan_pairs(value, stride):
    count = lax.axis_size("chan")
    return lax.ppermute(value, "chan", [(source, source ^ stride) for source in range(count)])


def chan_terms(value):
    count = lax.axis_size("chan")
    if count & (count - 1):
        return lax.psum(value, "chan"), jnp.zeros_like(value)
    stride = 1
    other = jnp.zeros_like(value)
    while stride < count:
        if stride > 1:
            value = value + other
        other = chan_pairs(value, stride)
        stride *= 2
    return value, other


def split(value):
    high = value.astype(BF16)
    low = (value - high.astype(F32)).astype(BF16)
    return high, low


def three_lhs(matrix):
    high, low = split(matrix)
    return jnp.concatenate([high, high, low], axis=1)


def three_rhs(value):
    high, low = split(value)
    return jnp.concatenate([high, low, high], axis=0)


def two_lhs(matrix):
    high, low = split(matrix)
    top = jnp.concatenate([high, high], axis=1)
    bottom = jnp.concatenate([low, jnp.zeros_like(low)], axis=1)
    return jnp.concatenate([top, bottom], axis=0)


def two_rhs(value):
    high, low = split(value)
    return jnp.concatenate([high, low], axis=0)


def dot(lhs, rhs):
    return jnp.dot(lhs, rhs, preferred_element_type=F32)


def met_rows(bases, height):
    return [min(height, 8 * (2 * basis // 8 + 1)) for basis in range(bases)]


def setup_kernel(
    filters_ref, bounds_ref, margin_ref, loading_ref,
    lift_ref, inner_ref, outer_ref, next_ref, interior_ref, border_ref, coef_ref, spectral_ref, limits_ref,
):
    bases, taps = filters_ref.shape
    height = taps
    size = bases * height
    facet = lax.axis_index("facet")
    last = margin_ref.shape[0] - 1
    own_margin = margin_ref[facet]
    next_margin = jnp.where(facet < last, margin_ref[jnp.minimum(facet + 1, last)], 0)

    def toeplitz(columns, column, tap_of):
        basis_of, _ = column(lax.broadcasted_iota(jnp.int32, (1, columns), 1))
        matrix = jnp.zeros((2 * height, columns), F32)
        for tap in range(taps):
            values = jnp.zeros((1, columns), F32)
            for basis in range(tap // 2, bases):
                values = jnp.where(basis_of == basis, filters_ref[basis, tap], values)
            matrix = jnp.where(tap_of == tap, values, matrix)
        return matrix

    def grids(columns, column):
        source = lax.broadcasted_iota(jnp.int32, (2 * height, columns), 0)
        return source, column(lax.broadcasted_iota(jnp.int32, (2 * height, columns), 1))[1]

    def dense(index):
        return lax.div(index, height), lax.rem(index, height)

    def reaching(index):
        basis = jnp.zeros_like(index)
        for number in range(1, bases):
            basis = basis + (index >= number * number).astype(jnp.int32)
        return basis, index - basis * basis

    source, target = grids(size, dense)
    borrowed = jnp.where((source < height - 1) & (height - 1 - source <= own_margin), target - source + height - 1, -1)
    own = toeplitz(size, dense, jnp.where(source >= height, target - source + height, borrowed))
    source, target = grids(bases * bases, reaching)
    tap_of = target - source + height
    below = toeplitz(bases * bases, reaching, jnp.where((source >= height) | (height - source <= next_margin), tap_of, -1))

    lift = DUAL * own.T
    lift_ref[...] = three_lhs(lift)
    inner_ref[...] = three_lhs(lift[:, height:])
    met = [
        lift[basis * height : basis * height + count, :height] for basis, count in enumerate(met_rows(bases, height))
    ]
    outer_ref[...] = three_lhs(jnp.concatenate(met, axis=0))
    next_ref[...] = three_lhs(DUAL * below.T)
    interior_ref[...] = two_lhs(own[height:])
    border_ref[...] = two_lhs(below[:height])
    loading = loading_ref[...]
    coef_ref[...] = two_lhs(loading)
    spectral_ref[...] = three_lhs(loading.T)
    row = lax.broadcasted_iota(jnp.int32, limits_ref.shape, 0)
    limits = jnp.zeros(limits_ref.shape, F32)
    for index in range(bounds_ref.shape[0]):
        limits = jnp.where(row == index, bounds_ref[index], limits)
    limits_ref[...] = limits


def pack(source_ref, target_ref, height, first, start=0):
    reach = height - 1
    for channel in range(source_ref.shape[0] // height):
        target_ref[pl.ds(start + channel * reach, reach), :] = source_ref[pl.ds(channel * height + first, reach), :]


def clear_tail(packed_ref):
    packed_ref[pl.ds(packed_ref.shape[0] - PAD, PAD), :] = jnp.zeros((PAD, packed_ref.shape[1]), F32)


def reflect_kernel(height, start, x_ref, d_ref, r_ref, packed_ref, x_buffer, d_buffer, sems):
    steps = sems.shape[0]
    block = r_ref.shape[0] // steps
    copies = []
    for step in range(steps):
        here = pl.ds(step * block, block)
        there = pl.ds(start + step * block, block)
        copies.append(
            [
                pltpu.make_async_copy(source.at[there], target.at[here], sems.at[step, turn])
                for turn, (source, target) in enumerate(((x_ref, x_buffer), (d_ref, d_buffer)))
            ]
        )
        for copy in copies[-1]:
            copy.start()
    clear_tail(packed_ref)
    for step in range(steps):
        for copy in copies[step]:
            copy.wait()
        here = pl.ds(step * block, block)
        x = x_buffer[here, :]
        updated = jnp.maximum(x - PRIMAL * (x - d_buffer[here, :]), 0.0)
        r_ref[here, :] = 2.0 * updated - x
        pack(r_ref.at[here], packed_ref, height, 1, step * (block // height) * (height - 1))


def coef_kernel(height, spectral, lhs_ref, *refs):
    if spectral:
        s_ref, *r_refs, out_ref = refs
    else:
        *r_refs, out_ref, packed_ref = refs
        start = 0
        for r_ref in r_refs:
            pack(r_ref, packed_ref, height, 0, start)
            start += r_ref.shape[0] // height * (height - 1)
        clear_tail(packed_ref)
    rank = out_ref.shape[0]

    def pixels(row):
        parts = [r[pl.ds(row, r.shape[0] // height, stride=height), :] for r in r_refs]
        value = DUAL * jnp.concatenate(parts, axis=0)
        if spectral:
            value = value + s_ref[pl.ds(row, s_ref.shape[0] // height, stride=height), :]
        return value

    lhs = lhs_ref[...]
    lanes = out_ref.shape[1] // height
    for row in range(0, height, 2):
        value = jnp.concatenate([pixels(row), pixels(row + 1)], axis=1)
        both = dot(lhs, two_rhs(value))
        out_ref[:, row * lanes : (row + 2) * lanes] = both[:rank] + both[rank:]


def spectral_kernel(height, lhs_ref, own_ref, other_ref, bounds_ref, *refs):
    image_refs, out_ref = refs[:-1], refs[-1]
    if image_refs:
        image_ref, image_refs = refs[-2], refs[:-2]
        for index, part_ref in enumerate(image_refs):
            image_ref[pl.ds(index * part_ref.shape[0], part_ref.shape[0]), :] = part_ref[...]
    lanes = out_ref.shape[1]
    channels = out_ref.shape[0] // height
    limit = jnp.concatenate([bounds_ref[...]] * 2, axis=1)
    lhs = lhs_ref[...]
    for row in range(0, height, 2):
        span = slice(row * lanes, (row + 2) * lanes)
        total = own_ref[:, span] + other_ref[:, span]
        clipped = jnp.minimum(jnp.maximum(total, -limit), limit)
        both = dot(lhs, three_rhs(clipped))
        out_ref[pl.ds(row, channels, stride=height), :] = both[:, :lanes]
        out_ref[pl.ds(row + 1, channels, stride=height), :] = both[:, lanes:]


def scale_of(weights, own_ref, other_ref):
    return weights / jnp.maximum(jnp.sqrt(own_ref[...] + other_ref[...]), weights)


def scale_kernel(height, weights_ref, own_ref, other_ref, scale_ref, above_ref):
    scale_ref[...] = scale_of(weights_ref[...], own_ref, other_ref)
    for basis in range(weights_ref.shape[0] // height):
        count = 2 * basis + 1
        above_ref[pl.ds(basis * basis, count), :] = scale_ref[pl.ds(basis * height, count), :]


def lift_kernel(height, halo_ref, own_ref, lhs_ref, before_ref, out_ref, squares_ref):
    lhs = lhs_ref[...]
    size = lhs.shape[0]
    lanes = own_ref.shape[1]
    total = before_ref[...]
    for pair in range(0, own_ref.shape[0] // height, 2):
        value = jnp.concatenate(
            [
                jnp.concatenate(
                    [
                        halo_ref[pl.ds(channel * (height - 1), height), :],
                        own_ref[pl.ds(channel * height, height), :],
                    ],
                    axis=0,
                )
                for channel in (pair, pair + 1)
            ],
            axis=1,
        )
        both = dot(lhs, three_rhs(value))
        for half in range(2):
            lifted = both[:, half * lanes : (half + 1) * lanes]
            out_ref[pl.ds((pair + half) * size, size), :] = lifted
            total = total + lifted * lifted
    squares_ref[...] = total


def inner_kernel(height, own_ref, lhs_ref, dual_ref, scale_ref, before_ref, met_ref, free_ref, squares_ref):
    lhs = lhs_ref[...]
    size, lanes = scale_ref.shape
    scale = scale_ref[...]
    counts = met_rows(size // height, height)
    many = sum(counts)
    total = before_ref[...]
    for pair in range(0, own_ref.shape[0] // height, 2):
        value = jnp.concatenate(
            [own_ref[pl.ds(channel * height, height), :] for channel in (pair, pair + 1)], axis=1
        )
        both = dot(lhs, three_rhs(value))
        for half in range(2):
            channel = pair + half
            lifted = both[:, half * lanes : (half + 1) * lanes] + dual_ref[pl.ds(channel * size, size), :] * scale
            met = [lifted[basis * height : basis * height + count] for basis, count in enumerate(counts)]
            free = [
                lifted[basis * height + count : (basis + 1) * height]
                for basis, count in enumerate(counts)
                if count < height
            ]
            met_ref[pl.ds(channel * many, many), :] = jnp.concatenate(met, axis=0)
            free = jnp.concatenate(free, axis=0)
            free_ref[pl.ds(channel * (size - many), size - many), :] = free
            total = total + free * free
    squares_ref[...] = total


def outer_kernel(height, halo_ref, lhs_ref, met_ref, before_ref, free_ref, out_ref, squares_ref):
    lhs = lhs_ref[...]
    many = lhs.shape[0]
    lanes = met_ref.shape[1]
    total = before_ref[:many, :]
    for pair in range(0, met_ref.shape[0] // many, 2):
        value = jnp.concatenate(
            [halo_ref[pl.ds(channel * (height - 1), height), :] for channel in (pair, pair + 1)], axis=1
        )
        both = dot(lhs, three_rhs(value))
        for half in range(2):
            rows = pl.ds((pair + half) * many, many)
            lifted = both[:, half * lanes : (half + 1) * lanes] + met_ref[rows, :]
            out_ref[rows, :] = lifted
            total = total + lifted * lifted
    squares_ref[:many, :] = total
    squares_ref[many:, :] = free_ref[...]


def adjoint_kernel(height, start, dual_ref, lhs_ref, scale_ref, s_ref, x_ref, d_ref, partial_ref):
    size, lanes = scale_ref.shape
    channels = partial_ref.shape[0] // height
    scale = scale_ref[...]
    lhs = lhs_ref[...]
    many = min(GROUP, channels)

    def step(group, carry):
        for pair in range(0, many, 2):
            channel = group * many + pair
            duals = [
                dual_ref[pl.ds(pl.multiple_of((channel + half) * size, size), size), :] * scale for half in range(2)
            ]
            both = dot(lhs, two_rhs(jnp.concatenate(duals, axis=1)))
            spread = both[:height] + both[height:]
            for half in range(2):
                rows = pl.ds(pl.multiple_of((channel + half) * height, height), height)
                cube = pl.ds(pl.multiple_of(start + (channel + half) * height, height), height)
                x, d = x_ref[cube, :], d_ref[cube, :]
                before = jnp.maximum(x - PRIMAL * (x - d), 0.0)
                mine = spread[:, half * lanes : (half + 1) * lanes]
                partial_ref[rows, :] = before - PRIMAL * ((before - d) + s_ref[cube, :] + mine)
        return carry

    lax.fori_loop(0, channels // many, step, 0)


def border_kernel(
    height, start, own_ref, below_ref, next_ref, border_ref, scale_ref, partial_ref, x_ref, d_ref,
    updated_ref, reflected_ref, packed_ref,
):
    lanes = scale_ref.shape[1]
    scale = jnp.concatenate([scale_ref[...]] * 2, axis=1)
    lift_lhs = next_ref[...]
    border_lhs = border_ref[...]
    for pair in range(0, partial_ref.shape[0] // height, 2):
        channels = (pair, pair + 1)
        value = jnp.concatenate(
            [
                jnp.concatenate(
                    [
                        own_ref[pl.ds(channel * height, height), :],
                        below_ref[pl.ds((start + channel) * (height - 1), height), :],
                    ],
                    axis=0,
                )
                for channel in channels
            ],
            axis=1,
        )
        duals = dot(lift_lhs, three_rhs(value)) * scale
        both = dot(border_lhs, two_rhs(duals))
        spread = both[:height] + both[height:]
        for half, channel in enumerate(channels):
            rows = pl.ds(channel * height, height)
            cube = pl.ds((start + channel) * height, height)
            x, d = x_ref[cube, :], d_ref[cube, :]
            before = jnp.maximum(x - PRIMAL * (x - d), 0.0)
            mine = spread[:, half * lanes : (half + 1) * lanes]
            updated = jnp.maximum(partial_ref[rows, :] - PRIMAL * mine, 0.0)
            updated_ref[rows, :] = updated
            reflected_ref[rows, :] = 2.0 * updated - before
    pack(reflected_ref, packed_ref, height, 1)
    clear_tail(packed_ref)


def wavelet_kernel(chunks, height, *refs):
    met_refs, free_refs = refs[:chunks], refs[chunks : 2 * chunks]
    weights_ref, mine_ref, other_ref, out_ref, buffer, sems = refs[2 * chunks :]
    bases = weights_ref.shape[0] // height
    counts = met_rows(bases, height)
    many = sum(counts)
    parts = [weights_ref[pl.ds(basis * height, count), :] for basis, count in enumerate(counts)]
    parts += [
        weights_ref[pl.ds(basis * height + count, height - count), :]
        for basis, count in enumerate(counts)
        if count < height
    ]
    scale = scale_of(jnp.concatenate(parts, axis=0), mine_ref, other_ref)
    rest = scale.shape[0] - many
    slots, block = buffer.shape[0], buffer.shape[2]
    pending = [()] * slots
    turn = 0
    for index, (met_ref, free_ref) in enumerate(zip(met_refs, free_refs)):
        channels = met_ref.shape[0] // many
        opening = block // 2 if index == 0 else block
        starts = [0, *range(opening, channels, block)]
        for start, stop in zip(starts, [*starts[1:], channels]):
            slot = turn % slots
            for copy in pending[slot]:
                copy.wait()
            for channel in range(stop - start):
                met = met_ref[pl.ds((start + channel) * many, many), :] * scale[:many]
                free = free_ref[pl.ds((start + channel) * rest, rest), :] * scale[many:]
                first = second = 0
                for basis, count in enumerate(counts):
                    buffer[slot, basis, channel, :count] = met[first : first + count]
                    first += count
                    if count < height:
                        buffer[slot, basis, channel, count:] = free[second : second + height - count]
                        second += height - count
            place = pl.ds(index * channels + start, stop - start)
            pending[slot] = [
                pltpu.make_async_copy(buffer.at[slot, basis, pl.ds(0, stop - start)], out_ref.at[basis, place], sems.at[slot, basis])
                for basis in range(bases)
            ]
            for copy in pending[slot]:
                copy.start()
            turn += 1
    for copies in pending:
        for copy in copies:
            copy.wait()


def whole():
    return pl.BlockSpec(memory_space=pltpu.VMEM)


def call(kernel, outs, ins, operands, flops, nbytes, scratch=(), out_specs=None, limit=VMEM_LIMIT, aliases=None):
    return pl.pallas_call(
        kernel,
        out_shape=outs,
        in_specs=ins,
        out_specs=out_specs if out_specs is not None else jax.tree.map(lambda _: whole(), outs),
        scratch_shapes=scratch,
        input_output_aliases=aliases or {},
        compiler_params=pltpu.CompilerParams(vmem_limit_bytes=limit),
        cost_estimate=pl.CostEstimate(flops=flops, bytes_accessed=nbytes, transcendentals=0),
    )(*operands)


def body(x_start, dirty, weights, filters, basis, bounds, margin_rows):
    channels, height, lanes = x_start.shape
    bases, taps = filters.shape
    rank = bounds.shape[0]
    assert taps == height
    size = bases * height
    reaching = bases * bases
    counts = met_rows(bases, height)
    met = sum(counts)
    free = size - met
    chunks = CHUNKS if channels >= 8 * CHUNKS else 1
    per = channels // chunks
    block = per * height
    rows = channels * height

    def flat(extent):
        return jax.ShapeDtypeStruct((extent, lanes), F32)

    x = x_start.reshape(rows, lanes)
    d = dirty.reshape(rows, lanes)
    w = weights.reshape(size, lanes)
    loading = basis[0].T
    cubes = rows * lanes * 4
    duals = per * size * lanes * 4

    distant = pl.BlockSpec(memory_space=pltpu.HBM)
    scalars = pl.BlockSpec(memory_space=pltpu.SMEM)
    work = 6 * 2 * height * per * size * lanes

    packed = per * (height - 1) + PAD
    reflected, halos = [], []
    for index in range(chunks):
        r, ahead = call(
            functools.partial(reflect_kernel, height, index * block), [flat(block), flat(packed)], [distant] * 2, (x, d),
            4 * block * lanes, 12 * block * lanes,
            scratch=[pltpu.VMEM((block, lanes), F32)] * 2 + [pltpu.SemaphoreType.DMA((STEPS, 2))], limit=REFLECT_LIMIT,
        )
        reflected.append(r)
        halos.append(shift(ahead, "facet", 1))

    lift_lhs, inner_lhs, outer_lhs, next_lhs, interior_lhs, border_lhs, coef_lhs, spectral_lhs, limits = call(
        setup_kernel,
        [
            jax.ShapeDtypeStruct((size, 6 * height), BF16),
            jax.ShapeDtypeStruct((size, 3 * height), BF16),
            jax.ShapeDtypeStruct((met, 3 * height), BF16),
            jax.ShapeDtypeStruct((reaching, 6 * height), BF16),
            jax.ShapeDtypeStruct((2 * height, 2 * size), BF16),
            jax.ShapeDtypeStruct((2 * height, 2 * reaching), BF16),
            jax.ShapeDtypeStruct((2 * rank, 2 * channels), BF16),
            jax.ShapeDtypeStruct((channels, 3 * rank), BF16),
            flat(rank),
        ],
        [scalars] * 3 + [whole()], (filters, bounds, margin_rows, loading), 100000, 100000,
    )

    def coefficients(parts, spectral):
        operands = (coef_lhs,) + ((spectral,) if spectral is not None else ()) + tuple(parts)
        outs = [jax.ShapeDtypeStruct((rank, height * lanes), F32)] + [flat(channels * (height - 1) + PAD)] * (spectral is None)
        return call(
            functools.partial(coef_kernel, height, spectral is not None), outs,
            [whole()] * len(operands), operands, 6 * rank * rows * lanes, 2 * cubes,
        )

    def synthesis(own, other, image=()):
        outs = [flat(rows)] * (2 if image else 1)
        return call(
            functools.partial(spectral_kernel, height), outs, [whole()] * (4 + len(image)),
            (spectral_lhs, own, other, limits, *image), 6 * rank * rows * lanes, 2 * cubes,
        )

    coefs, everything = coefficients(reflected, None)
    terms = chan_terms(coefs)
    squares = jnp.zeros((size, lanes), F32)
    lifted = []
    for index in range(chunks):
        out, squares = call(
            functools.partial(lift_kernel, height), [flat(per * size), flat(size)], [whole()] * 4,
            (halos[index], reflected[index], lift_lhs, squares), work, duals,
        )
        lifted.append(out)
        if index == 0:
            tied, _ = lax.optimization_barrier((everything, squares))
            below = shift(tied, "facet", -1)
    own, other = chan_terms(squares)
    (spectral,) = synthesis(*terms)
    other, spectral = lax.optimization_barrier((other, spectral))
    scale, scale_above = call(
        functools.partial(scale_kernel, height), [flat(size), flat(reaching)], [whole()] * 3, (w, own, other),
        10 * size * lanes, 16 * size * lanes,
    )
    scale_below = shift(scale_above, "facet", -1)

    partials = [
        call(
            functools.partial(adjoint_kernel, height, index * block), flat(block), [whole()] * 6,
            (lifted[index], interior_lhs, scale, spectral, x, d), 22 * work, 22 * duals,
        )
        for index in range(chunks)
    ]
    image, halos, again = [], [], []
    for index in range(chunks):
        updated, r, ahead = call(
            functools.partial(border_kernel, height, index * per), [flat(block)] * 2 + [flat(packed)], [whole()] * 8,
            (reflected[index], below, next_lhs, border_lhs, scale_below, partials[index], x, d), 22 * work, 22 * duals,
        )
        image.append(updated)
        again.append(r)
        halos.append(shift(ahead, "facet", 1))
    terms = chan_terms(*coefficients(again, spectral))

    squares = jnp.zeros((free, lanes), F32)
    inner, early = [], []
    for index in range(chunks):
        for_halo, done, squares = call(
            functools.partial(inner_kernel, height), [flat(per * met), flat(per * free), flat(free)], [whole()] * 5,
            (again[index], inner_lhs, lifted[index], scale, squares), work, 2 * duals,
        )
        inner.append(for_halo)
        early.append(done)
    apart = squares

    squares = jnp.zeros((size, lanes), F32)
    late = []
    for index in range(chunks):
        out, squares = call(
            functools.partial(outer_kernel, height), [flat(per * met), flat(size)], [whole()] * 5,
            (halos[index], outer_lhs, inner[index], squares, apart), work, 2 * duals,
        )
        late.append(out)
    own, other = chan_terms(squares)
    image, spectral = synthesis(*terms, image)

    slab = min(per, 16)
    wavelet = call(
        functools.partial(wavelet_kernel, chunks, height),
        jax.ShapeDtypeStruct((bases, channels, height, lanes), F32),
        [whole()] * (2 * chunks + 3), (*late, *early, w, own, other), rows * lanes * bases, 2 * cubes * bases,
        scratch=[pltpu.VMEM((3, bases, slab, height, lanes), F32), pltpu.SemaphoreType.DMA((3, bases))],
        out_specs=distant,
    )
    return (
        image.reshape(channels, height, lanes),
        wavelet,
        spectral.reshape(channels, height, lanes),
    )


def solution(mesh):
    in_specs = (
        P("chan", "facet", None),
        P("chan", "facet", None),
        P(None, "facet", None),
        P(),
        P("facet", "chan", None),
        P(),
        P(),
    )
    out_specs = (P("chan", "facet", None), P(None, "chan", "facet", None), P("chan", "facet", None))
    return jax.shard_map(body, mesh=mesh, in_specs=in_specs, out_specs=out_specs, check_vma=False)
```
